256 devices in a mesh: shot: 4 (over y), gx: 8 (over z_hi, x), gy: 8 (over z_lo, core).
Axes of the slice: x: 4, y: 4, z: 8 (z_hi: 2, z_lo: 4; z = z_hi * 4 + z_lo), core: 2. Of those that a mesh axis runs over, the one named last changes fastest.
Arguments:
- stiffness: float32 [256, 256, 512], P('gx', 'gy'), may hold values from 0.05 to 0.3
- buoyancy: float32 [256, 256, 512], P('gx', 'gy'), may hold values from 0.5 to 1
- older_field: float32 [4, 256, 256, 512], P('shot', 'gx', 'gy'), may hold values from -6 to 6
- current_field: float32 [4, 256, 256, 512], P('shot', 'gx', 'gy'), may hold values from -6 to 6
- stored_tiles: float32 [32, 8, 32, 32, 256], P(('shot', 'gx'), 'gy'), may hold values from -6 to 6
- tile_ids: int32 [32, 8, 32, 32], P(('shot', 'gx'), 'gy'), may hold values from 0 to 511, as said below
- tile_counts: int32 [32, 8, 32], P(('shot', 'gx'), 'gy'), may hold values from 0 to 32, as said below
- receiver_cells: int32 [4, 3, 1024], P('shot'), may hold values from 0 to 255, as said below
- receiver_data: float32 [4, 2, 1024], P('shot'), may hold values from -6 to 6
- source_cell: int32 [4, 3], P('shot'), may hold values from 0 to 255, as said below
Outputs:
- image: float32 [4, 256, 256, 512], P('shot', 'gx', 'gy')
- last_older: float32 [4, 256, 256, 512], P('shot', 'gx', 'gy')
- last_current: float32 [4, 256, 256, 512], P('shot', 'gx', 'gy')
The draws below stay inside these ranges and needn't reach their ends.
Inputs may be any that keep to these rules, and one draw needn't show every extreme that they name: `tile_counts`: for each owner and second-dimension block, the counts over holders sum to 512; holders of the owner's own shot have none; at least one holder has 32. `tile_ids`: for each owner and second-dimension block, the filled slots over all holders name every tile number once; unfilled slots carry arbitrary tile numbers. `receiver_cells`: depth index 1 to 7; first index below 256, second below 256. `source_cell`: depth index 1 to 3; first index below 256, second below 256.
All inputs are finite; a program needn't handle non-finite values.
Results may differ from the reference program's by a relative error of at most 0.0003.
Values sent between devices are 32-bit elements; how exact they have to be, the bound alone decides.
No kernel may reach another device: no remote copies, remote signals or barrier semaphores. Data moves between devices by JAX's collectives and lax.ppermute only.
A program may use at most 128 MiB of HBM per device.

```python
import math
import jax
import jax.numpy as jnp
from jax import lax

CX = 32
CY = 32
NZ = 512
NREC = 1024
STEPS = 2
SHOTS = 4
NX = 256
NY = 256
ZC = 256
TILES = 512
HOLDERS = 32
ELIGIBLE = 24
CAP = 32
YBLOCKS = 8
N_GX = 8


def make_plan(key):
    base_key = jax.random.fold_in(key, 9173)
    group = HOLDERS - ELIGIBLE
    leftover_tiles = TILES - CAP

    def one_owner(owner_row):
        sub_key = jax.random.fold_in(base_key, owner_row)
        key_order, key_weight, key_perm, key_fill = jax.random.split(sub_key, 4)
        owner_index = owner_row // YBLOCKS
        holder = jnp.arange(HOLDERS, dtype=jnp.int32)
        barred = (holder // group == owner_index // group).astype(jnp.int32)
        rank_keys = jax.random.permutation(key_order, HOLDERS).astype(jnp.int32)
        holder_order = jnp.argsort(rank_keys + HOLDERS * barred, stable=True).astype(jnp.int32)
        position = jnp.arange(HOLDERS, dtype=jnp.int32)
        active = (position >= 1) & (position < ELIGIBLE)
        weights = jnp.where(active, jax.random.randint(key_weight, (HOLDERS,), 2, 6), 0)
        base_counts = leftover_tiles * weights // jnp.sum(weights)
        leftover = leftover_tiles - jnp.sum(base_counts)
        extra = ((position >= 1) & (position <= leftover)).astype(jnp.int32)
        trial = jnp.where(active, jnp.minimum(base_counts + extra, CAP), 0).astype(jnp.int32)
        deficit = leftover_tiles - jnp.sum(trial)
        room = jnp.where(active, CAP - trial, 0).astype(jnp.int32)
        room_before = jnp.cumsum(room) - room
        added = jnp.clip(deficit - room_before, 0, room).astype(jnp.int32)
        by_rank = jnp.where(position == 0, CAP, trial + added).astype(jnp.int32)
        first_slot = jnp.cumsum(by_rank) - by_rank
        tile_perm = jax.random.permutation(key_perm, TILES).astype(jnp.int32)
        slot_index = jnp.arange(CAP, dtype=jnp.int32)
        positions = jnp.minimum(first_slot[:, None] + slot_index[None, :], TILES - 1)
        filled = slot_index[None, :] < by_rank[:, None]
        filler = jax.random.randint(key_fill, (HOLDERS, CAP), 0, TILES)
        ids_rank = jnp.where(filled, tile_perm[positions], filler).astype(jnp.int32)
        counts = jnp.zeros((HOLDERS,), jnp.int32).at[holder_order].set(by_rank)
        slot_ids = jnp.zeros((HOLDERS, CAP), jnp.int32).at[holder_order].set(ids_rank)
        return (counts, slot_ids)
    counts, slot_ids = jax.vmap(one_owner)(jnp.arange(HOLDERS * YBLOCKS, dtype=jnp.int32))
    return (counts.reshape(HOLDERS, YBLOCKS, HOLDERS), slot_ids.reshape(HOLDERS, YBLOCKS, HOLDERS, CAP))


def draw_tile_counts(key, part):
    return make_plan(key)[0]


def draw_tile_ids(key, part):
    return make_plan(key)[1]


def draw_receiver_cells(key, part):
    key_x, key_y, key_z = jax.random.split(jax.random.fold_in(key, 311), 3)
    cell_x = jax.random.randint(key_x, (SHOTS, 1, NREC), 0, NX)
    cell_y = jax.random.randint(key_y, (SHOTS, 1, NREC), 0, NY)
    cell_z = jax.random.randint(key_z, (SHOTS, 1, NREC), 1, 8)
    cell_x = cell_x.at[0, 0, 0].set(NX - 1).at[0, 0, 1].set(0)
    cell_y = cell_y.at[0, 0, 0].set(NY - 1).at[0, 0, 1].set(0)
    return jnp.concatenate([cell_x, cell_y, cell_z], axis=1).astype(jnp.int32)


def draw_source_cell(key, part):
    key_x, key_y, key_z = jax.random.split(jax.random.fold_in(key, 523), 3)
    cell_x = jax.random.randint(key_x, (SHOTS, 1), 0, NX)
    cell_y = jax.random.randint(key_y, (SHOTS, 1), 0, NY)
    cell_z = jax.random.randint(key_z, (SHOTS, 1), 1, 4)
    cell_x = cell_x.at[0, 0].set(NX - 1).at[1, 0].set(0)
    cell_y = cell_y.at[0, 0].set(NY - 1).at[1, 0].set(0)
    return jnp.concatenate([cell_x, cell_y, cell_z], axis=1).astype(jnp.int32)


def steps_of(rng, shape, pieces, low, top_value):
    def one(dim, parts):
        draws = jax.random.uniform(jax.random.fold_in(jax.random.fold_in(rng, 6), dim), (parts,), jnp.float32, low / len(pieces), top_value / len(pieces))
        return jnp.repeat(jnp.exp(draws), shape[dim] // parts).reshape((-1,) + (1,) * (len(shape) - dim - 1))

    loudness = one(*pieces[0])
    for cut in pieces[1:]:
        loudness = loudness * one(*cut)
    return loudness


def gaussian(stream_key, shape, spread, reach, pieces=(), kind=jnp.bfloat16):
    values = jax.random.normal(stream_key, shape, jnp.float32) * spread
    if len(pieces) > 0:
        values = steps_of(stream_key, shape, pieces, -0.22, 0.18) * values
    return jnp.clip(values, min=-reach, max=reach).astype(kind)


def setup_inputs(seed: int = 0) -> dict:
    arg_keys = jax.random.split(jax.random.key(seed), 11)
    stiffness = jnp.clip(jnp.exp(math.log(0.3) - 1.7917595 * jax.random.uniform(arg_keys[0], (NX, NY, NZ), jnp.float32) ** steps_of(arg_keys[0], (NX, NY, NZ), ((0, 8), (1, 8)), -0.2, 0.2)), 0.05, 0.3)
    buoyancy = jnp.clip(0.5 + 0.5 * jax.random.uniform(arg_keys[1], (NX, NY, NZ), jnp.float32) ** steps_of(arg_keys[1], (NX, NY, NZ), ((0, 8), (1, 8)), -0.2, 0.2), 0.5, 1.0)
    older_field = gaussian(arg_keys[2], (SHOTS, NX, NY, NZ), 1.0, 6.0, ((0, 4), (1, 8), (2, 8)), jnp.float32)
    current_field = gaussian(arg_keys[3], (SHOTS, NX, NY, NZ), 1.0, 6.0, ((0, 4), (1, 8), (2, 8)), jnp.float32)
    stored_tiles = gaussian(arg_keys[4], (HOLDERS, YBLOCKS, HOLDERS, CAP, ZC), 1.0, 6.0, ((0, 32), (1, 8)), jnp.float32)
    tile_ids = draw_tile_ids(jax.random.fold_in(arg_keys[10], 71), 0)
    tile_counts = draw_tile_counts(jax.random.fold_in(arg_keys[10], 71), 0)
    receiver_cells = draw_receiver_cells(jax.random.fold_in(arg_keys[10], 71), 0)
    receiver_data = gaussian(arg_keys[8], (SHOTS, STEPS, NREC), 1.0, 6.0, ((0, 4),), jnp.float32)
    source_cell = draw_source_cell(jax.random.fold_in(arg_keys[10], 71), 0)
    return {"stiffness": stiffness, "buoyancy": buoyancy, "older_field": older_field, "current_field": current_field, "stored_tiles": stored_tiles, "tile_ids": tile_ids, "tile_counts": tile_counts, "receiver_cells": receiver_cells, "receiver_data": receiver_data, "source_cell": source_cell}


MUTE_RADIUS = 3.0


def operate(padded_f, padded_b):
    centre = padded_f[1:-1, 1:-1, 1:-1]
    coef = padded_b[1:-1, 1:-1, 1:-1]
    upper_x = 0.5 * (coef + padded_b[2:, 1:-1, 1:-1])
    lower_x = 0.5 * (coef + padded_b[:-2, 1:-1, 1:-1])
    result = upper_x * (padded_f[2:, 1:-1, 1:-1] - centre) - lower_x * (centre - padded_f[:-2, 1:-1, 1:-1])
    upper_y = 0.5 * (coef + padded_b[1:-1, 2:, 1:-1])
    lower_y = 0.5 * (coef + padded_b[1:-1, :-2, 1:-1])
    result = result + (upper_y * (padded_f[1:-1, 2:, 1:-1] - centre) - lower_y * (centre - padded_f[1:-1, :-2, 1:-1]))
    upper_z = 0.5 * (coef + padded_b[1:-1, 1:-1, 2:])
    lower_z = 0.5 * (coef + padded_b[1:-1, 1:-1, :-2])
    result = result + (upper_z * (padded_f[1:-1, 1:-1, 2:] - centre) - lower_z * (centre - padded_f[1:-1, 1:-1, :-2]))
    return result


def refine(extended, along):
    count = extended.shape[along] - 1
    lower = lax.slice_in_dim(extended, 0, count, axis=along)
    upper = lax.slice_in_dim(extended, 1, count + 1, axis=along)
    middle = 0.5 * (lower + upper)
    paired = jnp.stack([lower, middle], axis=along + 1)
    new_shape = list(lower.shape)
    new_shape[along] = 2 * count
    return paired.reshape(new_shape)


def upsample(extended):
    coarse_z = extended.shape[-1]
    fine_index = jnp.arange(2 * coarse_z, dtype=jnp.int32)
    coarse_index = jnp.arange(coarse_z, dtype=jnp.int32)
    lower_index = fine_index // 2
    is_odd = (fine_index % 2) == 1
    same_cell = coarse_index[:, None] == lower_index[None, :]
    next_cell = (coarse_index[:, None] == lower_index[None, :] + 1) & is_odd[None, :]
    weights_z = jnp.where(same_cell, jnp.where(is_odd[None, :], 0.5, 1.0), 0.0) + jnp.where(next_cell, 0.5, 0.0)
    weights_z = weights_z.astype(jnp.float32)
    along_z = jnp.einsum("abcz,zf->abcf", extended, weights_z, precision=lax.Precision.HIGHEST)
    return refine(refine(along_z, 1), 2)


def assemble(received, plan_ids, plan_counts, half_x, half_y):
    coarse_z = received.shape[-1]
    capacity = received.shape[1]
    tile_total = STEPS * half_x * half_y
    slot_index = jnp.arange(capacity, dtype=jnp.int32)
    filled = slot_index[None, :] < plan_counts[:, None]
    targets = jnp.where(filled, plan_ids, tile_total).reshape(-1)
    tile_rows = jnp.zeros((tile_total, coarse_z), received.dtype)
    tile_rows = tile_rows.at[targets].set(received.reshape(-1, coarse_z), mode="drop")
    return tile_rows.reshape(STEPS, half_x, half_y, coarse_z)


def reference(stiffness, buoyancy, older_field, current_field, stored_tiles, tile_ids, tile_counts, receiver_cells, receiver_data, source_cell):
    padded_b = jnp.pad(buoyancy, 1)
    half_x = CX // 2
    half_y = CY // 2
    grid_x = jnp.arange(NX, dtype=jnp.int32).astype(jnp.float32)
    grid_y = jnp.arange(NY, dtype=jnp.int32).astype(jnp.float32)
    grid_z = jnp.arange(NZ, dtype=jnp.int32).astype(jnp.float32)

    def build_block(received, plan_ids, plan_counts):
        return assemble(received, plan_ids, plan_counts, half_x, half_y)

    def one_shot(packed):
        shot_index, older, current, cells, traces, source = packed
        start = (shot_index * N_GX).astype(jnp.int32)
        held = lax.dynamic_slice_in_dim(stored_tiles, start, N_GX, 2)
        held = jnp.transpose(held, (2, 1, 0, 3, 4))
        plan_ids = lax.dynamic_slice_in_dim(tile_ids, start, N_GX, 0)
        plan_counts = lax.dynamic_slice_in_dim(tile_counts, start, N_GX, 0)
        blocks = jax.vmap(jax.vmap(build_block))(held, plan_ids, plan_counts)
        coarse = jnp.transpose(blocks, (2, 0, 3, 1, 4, 5)).reshape(STEPS, NX // 2, NY // 2, ZC)
        extended = jnp.pad(coarse, ((0, 0), (0, 1), (0, 1), (0, 0)))
        snapshot = upsample(extended)
        source_f = source.astype(jnp.float32)
        diff_x = grid_x - source_f[0]
        diff_y = grid_y - source_f[1]
        diff_z = grid_z - source_f[2]
        distance = (diff_x * diff_x)[:, None, None] + (diff_y * diff_y)[None, :, None] + (diff_z * diff_z)[None, None, :]
        taper = 1.0 - jnp.exp(-distance / (2.0 * MUTE_RADIUS * MUTE_RADIUS))
        image_sum = jnp.zeros((NX, NY, NZ), jnp.float32)
        for section_index in range(STEPS):
            newer = 2.0 * current - older + stiffness * operate(jnp.pad(current, 1), padded_b)
            newer = newer.at[cells[0], cells[1], cells[2]].add(traces[section_index])
            image_sum = image_sum + snapshot[section_index] * newer
            older, current = current, newer
        return taper * image_sum, older, current

    shot_ids = jnp.arange(SHOTS, dtype=jnp.int32)
    image, last_older, last_current = lax.map(one_shot, (shot_ids, older_field, current_field, receiver_cells, receiver_data, source_cell))
    return (image, last_older, last_current)
```

```python
import jax
import jax.numpy as jnp
from jax import lax
from jax.experimental import pallas as pl
from jax.experimental.pallas import tpu as pltpu
from jax.sharding import PartitionSpec as P

MUTE_RADIUS = 3.0
PLANES = 32
ROWS = 1024
DEPTH = 512
COARSE = 256
CHUNKS = 4
SPAN = ROWS // CHUNKS
VMEM = pl.BlockSpec(memory_space=pltpu.VMEM)
SMEM = pl.BlockSpec(memory_space=pltpu.SMEM)
ANY = pl.BlockSpec(memory_space=pl.ANY)


def rotate(block, axis, step):
    count = lax.axis_size(axis)
    return lax.ppermute(block, axis, [(i, (i + step) % count) for i in range(count)])


def f32(*shape):
    return jax.ShapeDtypeStruct(shape, jnp.float32)


def split_bf16(x):
    high = x.astype(jnp.bfloat16)
    return high, (x - high.astype(jnp.float32)).astype(jnp.bfloat16)


def faces_kernel(fx_lo, fx_hi, fy_lo, fy_hi, bx_lo, bx_hi, by_lo, by_hi, sx_lo, sx_hi, sy_lo, sy_hi):
    for slot, refs in enumerate(((fx_lo, fx_hi, fy_lo, fy_hi), (bx_lo, bx_hi, by_lo, by_hi))):
        sx_lo[slot] = refs[0][0]
        sx_hi[slot] = refs[1][0]
        for x in range(PLANES):
            sy_lo[slot, x : x + 1, :] = refs[2][x, 0:1, :]
            sy_hi[slot, x : x + 1, :] = refs[3][x, 7:8, :]


def faces(field, buoyancy):
    plane_lo = pl.BlockSpec((1, PLANES, DEPTH), lambda i: (0, 0, 0))
    plane_hi = pl.BlockSpec((1, PLANES, DEPTH), lambda i: (PLANES - 1, 0, 0))
    rows_lo = pl.BlockSpec((PLANES, 8, DEPTH), lambda i: (0, 0, 0))
    rows_hi = pl.BlockSpec((PLANES, 8, DEPTH), lambda i: (0, PLANES // 8 - 1, 0))
    out = pl.BlockSpec((2, PLANES, DEPTH), lambda i: (0, 0, 0))
    return pl.pallas_call(
        faces_kernel,
        grid=(1,),
        in_specs=[plane_lo, plane_hi, rows_lo, rows_hi] * 2,
        out_specs=[out] * 4,
        out_shape=[f32(2, PLANES, DEPTH)] * 4,
        cost_estimate=pl.CostEstimate(flops=0, bytes_accessed=3 << 20, transcendentals=0),
        name="faces",
    )(*([field] * 4 + [buoyancy] * 4))


def sources_kernel(cells, data, out):
    base_x = lax.axis_index("gx") * PLANES
    base_y = lax.axis_index("gy") * PLANES
    local_x = cells[0:1, :] - base_x
    local_y = cells[1:2, :] - base_y
    inside = (local_x >= 0) & (local_x < PLANES) & (local_y >= 0) & (local_y < PLANES)
    row = jnp.where(inside, local_x * PLANES + local_y, -1)
    depth_id = lax.broadcasted_iota(jnp.int32, (8, 1024), 0)
    here = depth_id == cells[2:3, :]
    parts = []
    for step in range(2):
        value = jnp.where(here, data[step : step + 1, :], 0.0)
        parts.append(split_bf16(value))
    table = jnp.concatenate([parts[0][0], parts[0][1], parts[1][0], parts[1][1]], axis=0)
    lane = lax.broadcasted_iota(jnp.int32, (128, 128), 1)
    pad = jnp.zeros((96, 1024), jnp.bfloat16)
    table = jnp.concatenate([table, pad], axis=0)
    for start in range(0, ROWS, 128):
        ids = lax.broadcasted_iota(jnp.int32, (128, 1024), 0) + start
        select = jnp.where(ids == row, 1.0, 0.0).astype(jnp.bfloat16)
        product = lax.dot_general(
            select, table, (((1,), (1,)), ((), ())), preferred_element_type=jnp.float32
        )
        for step in range(2):
            high = pltpu.roll(product, (128 - 16 * step) % 128, 1)
            low = pltpu.roll(product, 128 - 16 * step - 8, 1)
            out[step, start : start + 128, :] = jnp.where(lane < 8, high + low, 0.0)


def sources(cells, data):
    return pl.pallas_call(
        sources_kernel,
        in_specs=[VMEM, VMEM],
        out_specs=VMEM,
        out_shape=f32(2, ROWS, 128),
        cost_estimate=pl.CostEstimate(flops=1 << 29, bytes_accessed=2 << 20, transcendentals=0),
        name="sources",
    )(cells, data)


def onehot_kernel(ids, out):
    for start in range(0, 512, 128):
        tile = lax.broadcasted_iota(jnp.int32, (128, 1024), 0) + start
        out[start : start + 128, :] = jnp.where(tile == ids[...], 1.0, 0.0).astype(jnp.bfloat16)


def onehots(ids):
    return pl.pallas_call(
        onehot_kernel,
        in_specs=[VMEM],
        out_specs=VMEM,
        out_shape=jax.ShapeDtypeStruct((512, 1024), jnp.bfloat16),
        cost_estimate=pl.CostEstimate(flops=1 << 20, bytes_accessed=2 << 20, transcendentals=0),
        name="onehots",
    )(ids)


def step_kernel(
    field, older, buoy, stiff, hx_lo, hx_hi, hy_lo, hy_hi, bx_lo, bx_hi, by_lo, by_hi, src,
    out, *rest, step, give_faces,
):
    if give_faces:
        sx_lo, sx_hi, sy_lo, sy_hi = rest[:4]
        rest = rest[4:]
    f_ext, b_ext, s_buf, o_buf, n_buf, in_sem, out_sem = rest
    copies = []
    for chunk in range(CHUNKS):
        part = pl.ds(chunk * SPAN, SPAN)
        shifted = pl.ds(chunk * SPAN + PLANES, SPAN)
        group = [
            pltpu.make_async_copy(field.at[part], f_ext.at[shifted], in_sem.at[chunk, 0]),
            pltpu.make_async_copy(buoy.at[part], b_ext.at[shifted], in_sem.at[chunk, 1]),
            pltpu.make_async_copy(stiff.at[part], s_buf.at[part], in_sem.at[chunk, 2]),
            pltpu.make_async_copy(older.at[part], o_buf.at[part], in_sem.at[chunk, 3]),
        ]
        for copy in group:
            copy.start()
        copies.append(group)
    gx = lax.axis_index("gx")
    gy = lax.axis_index("gy")
    x_lo = jnp.where(gx > 0, 1.0, 0.0)
    x_hi = jnp.where(gx < lax.axis_size("gx") - 1, 1.0, 0.0)
    y_lo = jnp.where(gy > 0, 1.0, 0.0)
    y_hi = jnp.where(gy < lax.axis_size("gy") - 1, 1.0, 0.0)
    f_ext[0:PLANES] = hx_lo[...] * x_lo
    b_ext[0:PLANES] = bx_lo[...] * x_lo
    f_ext[ROWS + PLANES : ROWS + 2 * PLANES] = hx_hi[...] * x_hi
    b_ext[ROWS + PLANES : ROWS + 2 * PLANES] = bx_hi[...] * x_hi
    row_id = lax.broadcasted_iota(jnp.int32, (PLANES, DEPTH), 0)
    lane_id = lax.broadcasted_iota(jnp.int32, (PLANES, DEPTH), 1)
    per = SPAN // PLANES
    out_copies = []
    for group in copies[0][:2]:
        group.wait()
    carry = (b_ext[0:PLANES] + b_ext[PLANES : 2 * PLANES]) * (
        f_ext[PLANES : 2 * PLANES] - f_ext[0:PLANES]
    )
    for chunk in range(CHUNKS):
        for copy in copies[chunk][2:]:
            copy.wait()
        if chunk + 1 < CHUNKS:
            for copy in copies[chunk + 1][:2]:
                copy.wait()
        first = chunk * per

        def plane(k, flux_before, first=first):
            x = first + k
            base = pl.multiple_of((x + 1) * PLANES, PLANES)
            c = f_ext[pl.ds(base, PLANES), :]
            b = b_ext[pl.ds(base, PLANES), :]
            c_next = f_ext[pl.ds(base + PLANES, PLANES), :]
            b_next = b_ext[pl.ds(base + PLANES, PLANES), :]
            flux_x = (b + b_next) * (c_next - c)
            lo_f = hy_lo[pl.ds(x, 1), :] * y_lo
            lo_b = by_lo[pl.ds(x, 1), :] * y_lo
            hi_f = hy_hi[pl.ds(x, 1), :] * y_hi
            hi_b = by_hi[pl.ds(x, 1), :] * y_hi
            c_up = jnp.where(row_id == PLANES - 1, hi_f, pltpu.roll(c, PLANES - 1, 0))
            b_up = jnp.where(row_id == PLANES - 1, hi_b, pltpu.roll(b, PLANES - 1, 0))
            flux_y = (b + b_up) * (c_up - c)
            first_flux = (b[0:1, :] + lo_b) * (c[0:1, :] - lo_f)
            flux_y_before = jnp.where(row_id == 0, first_flux, pltpu.roll(flux_y, 1, 0))
            edge_flux = b * c
            flux_z = (b + pltpu.roll(b, DEPTH - 1, 1)) * (pltpu.roll(c, DEPTH - 1, 1) - c)
            flux_z = jnp.where(lane_id == DEPTH - 1, -edge_flux, flux_z)
            flux_z_before = jnp.where(lane_id == 0, edge_flux, pltpu.roll(flux_z, 1, 1))
            total = (flux_x - flux_before) + (flux_y - flux_y_before) + (flux_z - flux_z_before)
            at = pl.multiple_of(x * PLANES, PLANES)
            new = (2.0 * c - o_buf[pl.ds(at, PLANES), :]) + (
                0.5 * s_buf[pl.ds(at, PLANES), :]
            ) * total
            n_buf[pl.ds(at, PLANES), :] = new
            head = new[:, 0:128] + src[step, pl.ds(at, PLANES), :]
            n_buf[pl.ds(at, PLANES), 0:128] = head
            if give_faces:
                sy_lo[pl.ds(x, 1), :] = n_buf[pl.ds(at, 1), :]
                sy_hi[pl.ds(x, 1), :] = n_buf[pl.ds(at + PLANES - 1, 1), :]
            return flux_x

        carry = lax.fori_loop(0, per, plane, carry)
        part = pl.ds(chunk * SPAN, SPAN)
        copy = pltpu.make_async_copy(n_buf.at[part], out.at[part], out_sem.at[chunk])
        copy.start()
        out_copies.append(copy)
    if give_faces:
        sx_lo[...] = n_buf[0:PLANES]
        sx_hi[...] = n_buf[ROWS - PLANES : ROWS]
    for copy in out_copies:
        copy.wait()


def advance(field, older, buoy, stiff, halos, buoy_halos, src, step, give_faces):
    out_shape = [f32(ROWS, DEPTH)]
    out_specs = [ANY]
    if give_faces:
        out_shape += [f32(PLANES, DEPTH)] * 4
        out_specs += [VMEM] * 4
    return pl.pallas_call(
        lambda *refs: step_kernel(*refs, step=step, give_faces=give_faces),
        in_specs=[ANY] * 4 + [VMEM] * 9,
        out_specs=out_specs,
        out_shape=out_shape,
        scratch_shapes=[
            pltpu.VMEM((ROWS + 2 * PLANES, DEPTH), jnp.float32),
            pltpu.VMEM((ROWS + 2 * PLANES, DEPTH), jnp.float32),
            pltpu.VMEM((ROWS, DEPTH), jnp.float32),
            pltpu.VMEM((ROWS, DEPTH), jnp.float32),
            pltpu.VMEM((ROWS, DEPTH), jnp.float32),
            pltpu.SemaphoreType.DMA((CHUNKS, 4)),
            pltpu.SemaphoreType.DMA((CHUNKS,)),
        ],
        compiler_params=pltpu.CompilerParams(vmem_limit_bytes=32 << 20),
        cost_estimate=pl.CostEstimate(flops=20 << 20, bytes_accessed=10 << 20, transcendentals=0),
        name="advance%d" % step,
    )(field, older, buoy, stiff, *halos, *buoy_halos, src)


def interpolation():
    fine = lax.broadcasted_iota(jnp.int32, (COARSE, DEPTH), 1)
    coarse = lax.broadcasted_iota(jnp.int32, (COARSE, DEPTH), 0)
    gap = jnp.abs(fine - 2 * coarse).astype(jnp.float32)
    return jnp.maximum(1.0 - 0.5 * gap, 0.0).astype(jnp.bfloat16)


def dot(a, b):
    return jnp.dot(a, b, preferred_element_type=jnp.float32)


def coarse_kernel(received, onehot, along, rim_x, rim_y, corner, rows):
    high, low = split_bf16(received[...])
    c_high = dot(onehot[...], high)
    c_low = dot(onehot[...], low)
    coarse = c_high + c_low
    for n in range(2):
        rim_x[n] = coarse[n * 256 : n * 256 + 16, :]
        corner[n] = coarse[n * 256 : n * 256 + 8, :]
    for half in range(2):
        lanes = slice(half * 128, half * 128 + 128)
        rows[half] = coarse[:, lanes]
        for n in range(2):
            rim_y[n, :, lanes] = rows[half, pl.ds(n * 256, 16, stride=16), :]
    weights = interpolation()
    along[...] = dot(c_high.astype(jnp.bfloat16), weights) + dot(c_low.astype(jnp.bfloat16), weights)


def coarse_tiles(received, onehot):
    return pl.pallas_call(
        coarse_kernel,
        in_specs=[VMEM, VMEM],
        out_specs=[VMEM] * 4,
        out_shape=[f32(512, DEPTH), f32(2, 16, COARSE), f32(2, 16, COARSE), f32(2, 8, COARSE)],
        scratch_shapes=[pltpu.VMEM((2, 512, 128), jnp.float32)],
        compiler_params=pltpu.CompilerParams(vmem_limit_bytes=32 << 20),
        cost_estimate=pl.CostEstimate(flops=1 << 30, bytes_accessed=3 << 20, transcendentals=0),
        name="coarse_tiles",
    )(received, onehot)


def image_kernel(source, along, rim_x, rim_y, corner, first, second, out, rims, rim_along, fine):
    gx = lax.axis_index("gx")
    gy = lax.axis_index("gy")
    keep_x = jnp.where(gx < lax.axis_size("gx") - 1, 1.0, 0.0)
    keep_y = jnp.where(gy < lax.axis_size("gy") - 1, 1.0, 0.0)
    for n in range(2):
        rims[n * 40 : n * 40 + 16] = rim_x[n] * keep_x
        rims[n * 40 + 16 : n * 40 + 32] = rim_y[n] * keep_y
        rims[n * 40 + 32 : n * 40 + 40] = corner[n] * (keep_x * keep_y)
    weights = interpolation()
    high, low = split_bf16(rims[...])
    rim_along[...] = dot(high, weights) + dot(low, weights)
    row16 = lax.broadcasted_iota(jnp.int32, (16, DEPTH), 0)
    for n in range(2):
        for k in range(17):
            if k < 16:
                rows = along[n * 256 + k * 16 : n * 256 + k * 16 + 16, :]
                side = rim_along[n * 40 + 16 + k : n * 40 + 17 + k, :]
            else:
                rows = rim_along[n * 40 : n * 40 + 16, :]
                side = rim_along[n * 40 + 32 : n * 40 + 33, :]
            upper = jnp.where(row16 == 15, side, pltpu.roll(rows, 15, 0))
            base = (n * 17 + k) * PLANES
            middle = 0.5 * (rows + upper)
            for part in range(4):
                lanes = slice(part * 128, part * 128 + 128)
                fine[part, pl.ds(base, 16, stride=2), :] = rows[:, lanes]
                fine[part, pl.ds(base + 1, 16, stride=2), :] = middle[:, lanes]
    scale = -1.0 / (2.0 * MUTE_RADIUS * MUTE_RADIUS)
    y = (lax.broadcasted_iota(jnp.int32, (PLANES, DEPTH), 0) + gy * PLANES - source[0, 1]).astype(jnp.float32)
    z = (lax.broadcasted_iota(jnp.int32, (PLANES, DEPTH), 1) - source[0, 2]).astype(jnp.float32)
    decay_yz = jnp.exp((y * y + z * z) * scale)
    x_base = gx * PLANES - source[0, 0]
    for k in range(16):
        for odd in range(2):
            x = 2 * k + odd
            at = slice(x * PLANES, (x + 1) * PLANES)
            dx = jnp.full((1, 128), x_base + x, jnp.int32).astype(jnp.float32)
            decay = jnp.exp((dx * dx) * scale)
            for part in range(4):
                lanes = slice(part * 128, part * 128 + 128)
                taper = 1.0 - decay * decay_yz[:, lanes]
                snaps = []
                for n in range(2):
                    start = (n * 17 + k) * PLANES
                    snap = fine[part, start : start + PLANES, :]
                    if odd:
                        snap = 0.5 * (snap + fine[part, start + PLANES : start + 2 * PLANES, :])
                    snaps.append(snap)
                out[at, lanes] = taper * (
                    snaps[0] * first[at, lanes] + snaps[1] * second[at, lanes]
                )


def imaging(source, along, rims, first, second):
    return pl.pallas_call(
        image_kernel,
        in_specs=[SMEM] + [VMEM] * 6,
        out_specs=VMEM,
        out_shape=f32(ROWS, DEPTH),
        scratch_shapes=[
            pltpu.VMEM((80, COARSE), jnp.float32),
            pltpu.VMEM((80, DEPTH), jnp.float32),
            pltpu.VMEM((4, 2 * 17 * PLANES, 128), jnp.float32),
        ],
        compiler_params=pltpu.CompilerParams(vmem_limit_bytes=32 << 20),
        cost_estimate=pl.CostEstimate(flops=20 << 20, bytes_accessed=8 << 20, transcendentals=0),
        name="imaging",
    )(source, along, *rims, first, second)


def per_device(
    stiffness,
    buoyancy,
    older_field,
    current_field,
    stored_tiles,
    tile_ids,
    tile_counts,
    receiver_cells,
    receiver_data,
    source_cell,
):
    older = older_field[0].reshape(ROWS, DEPTH)
    current = current_field[0].reshape(ROWS, DEPTH)
    stiff = stiffness.reshape(ROWS, DEPTH)
    buoy = buoyancy.reshape(ROWS, DEPTH)

    with jax.named_scope("halo_exchange"):
        sx_lo, sx_hi, sy_lo, sy_hi = faces(current_field[0], buoyancy)
        hx_lo = rotate(sx_hi, "gx", 1)
        hx_hi = rotate(sx_lo, "gx", -1)
        hy_lo = rotate(sy_hi, "gy", 1)
        hy_hi = rotate(sy_lo, "gy", -1)
    both = (hx_lo, hx_hi, hy_lo, hy_hi)
    halos = [h[0] for h in both]
    buoy_halos = [h[1] for h in both]

    received = lax.all_to_all(
        stored_tiles[0, 0], ("shot", "gx"), split_axis=0, concat_axis=0, tiled=True
    ).reshape(1024, COARSE)
    slot = lax.broadcasted_iota(jnp.int32, (32, 32), 1)
    ids = jnp.where(slot < tile_counts[0, 0][:, None], tile_ids[0, 0], -1).reshape(1, 1024)
    onehot = onehots(ids)
    src = sources(receiver_cells[0], receiver_data[0])

    second, sx_lo, sx_hi, sy_lo, sy_hi = advance(
        current, older, buoy, stiff, halos, buoy_halos, src, 0, True
    )
    halos = [
        rotate(sx_hi, "gx", 1),
        rotate(sx_lo, "gx", -1),
        rotate(sy_hi, "gy", 1),
        rotate(sy_lo, "gy", -1),
    ]
    (third,) = advance(second, current, buoy, stiff, halos, buoy_halos, src, 1, False)

    along, rim_x, rim_y, corner = coarse_tiles(received, onehot)
    rims = [
        rotate(rim_x, "gx", -1),
        rotate(rim_y, "gy", -1),
        diagonal(corner),
    ]
    image = imaging(source_cell, along, rims, second, third)
    shape = current_field.shape
    return image.reshape(shape), second.reshape(shape), third.reshape(shape)


def diagonal(block):
    nx, ny = lax.axis_size("gx"), lax.axis_size("gy")
    route = [
        (i * ny + j, ((i - 1) % nx) * ny + (j - 1) % ny) for i in range(nx) for j in range(ny)
    ]
    return lax.ppermute(block, ("gx", "gy"), route)


def solution(mesh):
    in_specs = (
        P("gx", "gy", None),
        P("gx", "gy", None),
        P("shot", "gx", "gy", None),
        P("shot", "gx", "gy", None),
        P(("shot", "gx"), "gy", None, None, None),
        P(("shot", "gx"), "gy", None, None),
        P(("shot", "gx"), "gy", None),
        P("shot", None, None),
        P("shot", None, None),
        P("shot", None),
    )
    out_specs = (
        P("shot", "gx", "gy", None),
        P("shot", "gx", "gy", None),
        P("shot", "gx", "gy", None),
    )
    return jax.shard_map(
        per_device, mesh=mesh, in_specs=in_specs, out_specs=out_specs, check_vma=False
    )
```

```python
import jax
import jax.numpy as jnp
from jax import lax
from jax.experimental import pallas as pl
from jax.experimental.pallas import tpu as pltpu
from jax.sharding import PartitionSpec as P

MUTE_RADIUS = 3.0
PLANES = 32
ROWS = 1024
DEPTH = 512
COARSE = 256
CHUNKS = 4
PER = PLANES // CHUNKS
SPAN = ROWS // CHUNKS
VMEM = pl.BlockSpec(memory_space=pltpu.VMEM)
SMEM = pl.BlockSpec(memory_space=pltpu.SMEM)
ANY = pl.BlockSpec(memory_space=pl.ANY)
ROOM = pltpu.CompilerParams(vmem_limit_bytes=16 << 20)


def rotate(block, axis, step):
    count = lax.axis_size(axis)
    return lax.ppermute(block, axis, [(i, (i + step) % count) for i in range(count)])


def f32(*shape):
    return jax.ShapeDtypeStruct(shape, jnp.float32)


def split_bf16(x):
    high = x.astype(jnp.bfloat16)
    return high, (x - high.astype(jnp.float32)).astype(jnp.bfloat16)


def faces_kernel(fx_lo, fx_hi, fy_lo, fy_hi, bx_lo, bx_hi, by_lo, by_hi, sx_lo, sx_hi, sy_lo, sy_hi):
    for slot, refs in enumerate(((fx_lo, fx_hi, fy_lo, fy_hi), (bx_lo, bx_hi, by_lo, by_hi))):
        sx_lo[slot] = refs[0][0]
        sx_hi[slot] = refs[1][0]
        for x in range(PLANES):
            sy_lo[slot, x : x + 1, :] = refs[2][x, 0:1, :]
            sy_hi[slot, x : x + 1, :] = refs[3][x, 7:8, :]


def faces(field, buoyancy):
    plane_lo = pl.BlockSpec((1, PLANES, DEPTH), lambda i: (0, 0, 0))
    plane_hi = pl.BlockSpec((1, PLANES, DEPTH), lambda i: (PLANES - 1, 0, 0))
    rows_lo = pl.BlockSpec((PLANES, 8, DEPTH), lambda i: (0, 0, 0))
    rows_hi = pl.BlockSpec((PLANES, 8, DEPTH), lambda i: (0, PLANES // 8 - 1, 0))
    out = pl.BlockSpec((2, PLANES, DEPTH), lambda i: (0, 0, 0))
    return pl.pallas_call(
        faces_kernel,
        grid=(1,),
        in_specs=[plane_lo, plane_hi, rows_lo, rows_hi] * 2,
        out_specs=[out] * 4,
        out_shape=[f32(2, PLANES, DEPTH)] * 4,
        compiler_params=ROOM,
        cost_estimate=pl.CostEstimate(flops=0, bytes_accessed=3 << 20, transcendentals=0),
        name="faces",
    )(*([in_hbm(field)] * 4 + [in_hbm(buoyancy)] * 4))


def sources_kernel(cells, data, out):
    base_x = lax.axis_index("gx") * PLANES
    base_y = lax.axis_index("gy") * PLANES
    local_x = cells[0:1, :] - base_x
    local_y = cells[1:2, :] - base_y
    inside = (local_x >= 0) & (local_x < PLANES) & (local_y >= 0) & (local_y < PLANES)
    row = jnp.where(inside, local_x * PLANES + local_y, -1)
    depth_id = lax.broadcasted_iota(jnp.int32, (8, 1024), 0)
    here = depth_id == cells[2:3, :]
    parts = []
    for step in range(2):
        value = jnp.where(here, data[step : step + 1, :], 0.0)
        parts.append(split_bf16(value))
    table = jnp.concatenate([parts[0][0], parts[0][1], parts[1][0], parts[1][1]], axis=0)
    lane = lax.broadcasted_iota(jnp.int32, (128, 128), 1)
    pad = jnp.zeros((96, 1024), jnp.bfloat16)
    table = jnp.concatenate([table, pad], axis=0)
    for start in range(0, ROWS, 128):
        ids = lax.broadcasted_iota(jnp.int32, (128, 1024), 0) + start
        select = jnp.where(ids == row, 1.0, 0.0).astype(jnp.bfloat16)
        product = lax.dot_general(
            select, table, (((1,), (1,)), ((), ())), preferred_element_type=jnp.float32
        )
        for step in range(2):
            high = pltpu.roll(product, (128 - 16 * step) % 128, 1)
            low = pltpu.roll(product, 128 - 16 * step - 8, 1)
            out[step, start : start + 128, :] = jnp.where(lane < 8, high + low, 0.0)


def sources(cells, data):
    return pl.pallas_call(
        sources_kernel,
        in_specs=[VMEM, VMEM],
        out_specs=VMEM,
        out_shape=f32(2, ROWS, 128),
        cost_estimate=pl.CostEstimate(flops=1 << 29, bytes_accessed=2 << 20, transcendentals=0),
        compiler_params=ROOM,
        name="sources",
    )(cells, data)


def onehot_kernel(ids, out):
    for start in range(0, 512, 128):
        tile = lax.broadcasted_iota(jnp.int32, (128, 1024), 0) + start
        out[start : start + 128, :] = jnp.where(tile == ids[...], 1.0, 0.0).astype(jnp.bfloat16)


def onehots(ids):
    return pl.pallas_call(
        onehot_kernel,
        in_specs=[VMEM],
        out_specs=VMEM,
        out_shape=jax.ShapeDtypeStruct((512, 1024), jnp.bfloat16),
        cost_estimate=pl.CostEstimate(flops=1 << 20, bytes_accessed=2 << 20, transcendentals=0),
        compiler_params=ROOM,
        name="onehots",
    )(ids)


def in_hbm(x):
    return pltpu.with_memory_space_constraint(x, pltpu.HBM)


def inner_kernel(field, older, buoy, stiff, src, *rest, step):
    if step == 1:
        fixed, rest = rest[:4], rest[4:]
        out, saved, f_buf, b_buf, s_buf, o_buf, in_sem, out_sem = rest
        n_buf = out
    else:
        out, faces_out, stiff_out = rest[0], rest[1:5], rest[5:9]
        f_buf, b_buf, s_buf, o_buf, n_buf, in_sem, out_sem = rest[9:]
    copies = []
    for chunk in range(CHUNKS):
        part = pl.ds(chunk * SPAN, SPAN)
        pairs = ((field, f_buf), (buoy, b_buf), (stiff, s_buf), (older, o_buf))
        group = [
            pltpu.make_async_copy(hbm.at[part], buf.at[part], in_sem.at[chunk, k])
            for k, (hbm, buf) in enumerate(pairs)
        ]
        for copy in group:
            copy.start()
        copies.append(group)
    row8 = lax.broadcasted_iota(jnp.int32, (8, DEPTH), 0)
    lane128 = lax.broadcasted_iota(jnp.int32, (PLANES, 128), 1)
    out_copies = []

    def arrive(chunk):
        for copy in copies[chunk][:2]:
            copy.wait()
        if step == 1:
            if chunk == 0:
                f_buf[0:PLANES, :] = fixed[0][0]
            if chunk == CHUNKS - 1:
                f_buf[ROWS - PLANES : ROWS, :] = fixed[1][0]
            for x in range(chunk * PER, chunk * PER + PER):
                f_buf[x * PLANES : x * PLANES + 1, :] = fixed[2][0, x : x + 1, :]
                f_buf[x * PLANES + 31 : x * PLANES + 32, :] = fixed[3][0, x : x + 1, :]
            part = pl.ds(chunk * SPAN, SPAN)
            copy = pltpu.make_async_copy(f_buf.at[part], saved.at[part], out_sem.at[chunk])
            copy.start()
            out_copies.append(copy)

    def plane(x, flux_before, last=False):
        base = pl.multiple_of(x * PLANES, PLANES)
        at = pl.ds(base, PLANES)
        c = f_buf[at, :]
        b = b_buf[at, :]
        if last:
            flux_x = jnp.zeros_like(c)
        else:
            nearby = pl.ds(base + PLANES, PLANES)
            flux_x = (b + b_buf[nearby, :]) * (f_buf[nearby, :] - c)
        flux_y = (b + pltpu.roll(b, PLANES - 1, 0)) * (pltpu.roll(c, PLANES - 1, 0) - c)
        flux_y = jnp.concatenate(
            [flux_y[0:24], jnp.where(row8 == 7, 0.0, flux_y[24:32])], axis=0
        )
        flux_z = (b + pltpu.roll(b, DEPTH - 1, 1)) * (pltpu.roll(c, DEPTH - 1, 1) - c)
        flux_z = jnp.concatenate(
            [flux_z[:, : DEPTH - 128], jnp.where(lane128 == 127, 0.0, flux_z[:, DEPTH - 128 :])],
            axis=1,
        )
        total = (flux_x - flux_before) + (flux_y - pltpu.roll(flux_y, 1, 0))
        total = total + (flux_z - pltpu.roll(flux_z, 1, 1))
        head = slice(0, 128)
        tail = slice(DEPTH - 128, DEPTH)
        total = jnp.concatenate(
            [
                total[:, head] - jnp.where(lane128 == 0, b[:, head] * c[:, head], 0.0),
                total[:, 128 : DEPTH - 128],
                total[:, tail] - jnp.where(lane128 == 127, b[:, tail] * c[:, tail], 0.0),
            ],
            axis=1,
        )
        value = (2.0 * c - o_buf[at, :]) + (0.5 * s_buf[at, :]) * total
        n_buf[at, 128:DEPTH] = value[:, 128:]
        n_buf[at, head] = value[:, head] + src[step, at, :]
        if step == 0:
            faces_out[2][pl.ds(x, 1), :] = n_buf[pl.ds(base, 1), :]
            faces_out[3][pl.ds(x, 1), :] = n_buf[pl.ds(base + PLANES - 1, 1), :]
            stiff_out[2][pl.ds(x, 1), :] = s_buf[pl.ds(base, 1), :]
            stiff_out[3][pl.ds(x, 1), :] = s_buf[pl.ds(base + PLANES - 1, 1), :]
        return flux_x

    arrive(0)
    flux = jnp.zeros((PLANES, DEPTH), jnp.float32)
    for chunk in range(CHUNKS):
        for copy in copies[chunk][2:]:
            copy.wait()
        if chunk + 1 < CHUNKS:
            arrive(chunk + 1)
            flux = lax.fori_loop(chunk * PER, chunk * PER + PER, plane, flux, unroll=4)
        else:
            flux = lax.fori_loop(chunk * PER, chunk * PER + PER - 4, plane, flux, unroll=4)
            for x in range(PLANES - 4, PLANES):
                flux = plane(x, flux, x == PLANES - 1)
        if step == 0:
            part = pl.ds(chunk * SPAN, SPAN)
            copy = pltpu.make_async_copy(n_buf.at[part], out.at[part], out_sem.at[chunk])
            copy.start()
            out_copies.append(copy)
    if step == 0:
        faces_out[0][...] = n_buf[0:PLANES, :]
        faces_out[1][...] = n_buf[ROWS - PLANES : ROWS, :]
        stiff_out[0][...] = s_buf[0:PLANES, :]
        stiff_out[1][...] = s_buf[ROWS - PLANES : ROWS, :]
    for copy in out_copies:
        copy.wait()


def inner(field, older, buoy, stiff, src, fixed, step):
    big = pltpu.VMEM((ROWS, DEPTH), jnp.float32)
    if step == 0:
        out_shape = [pltpu.HBM((ROWS, DEPTH), jnp.float32)] + [f32(PLANES, DEPTH)] * 8
        out_specs = [ANY] + [VMEM] * 8
    else:
        out_shape = [big, f32(ROWS, DEPTH)]
        out_specs = [VMEM, ANY]
    return pl.pallas_call(
        lambda *refs: inner_kernel(*refs, step=step),
        in_specs=[ANY] * 4 + [VMEM] * (1 + len(fixed)),
        out_specs=out_specs,
        out_shape=out_shape,
        scratch_shapes=[big] * (5 - step)
        + [pltpu.SemaphoreType.DMA((CHUNKS, 4)), pltpu.SemaphoreType.DMA((CHUNKS,))],
        compiler_params=ROOM,
        cost_estimate=pl.CostEstimate(flops=20 << 20, bytes_accessed=10 << 20, transcendentals=0),
        name="inner%d" % step,
    )(in_hbm(field), in_hbm(older), in_hbm(buoy), in_hbm(stiff), src, *fixed)


def edge_terms(own_b, far_b, own_f, far_f, stiff):
    gx = lax.axis_index("gx")
    gy = lax.axis_index("gy")
    keep = [
        jnp.where(gx > 0, 1.0, 0.0),
        jnp.where(gx < lax.axis_size("gx") - 1, 1.0, 0.0),
        jnp.where(gy > 0, 1.0, 0.0),
        jnp.where(gy < lax.axis_size("gy") - 1, 1.0, 0.0),
    ]
    terms = []
    for side in range(4):
        coef = 0.5 * (own_b[side][1] + keep[side] * far_b[side][1])
        flux = coef * (keep[side] * far_f[side][0] - own_f[side][0])
        terms.append(stiff[side][...] * flux)
    return terms


def fix_kernel(*refs):
    own, far, value, stiff, out = (refs[4 * k : 4 * k + 4] for k in range(5))
    terms = refs[20]
    for side, term in enumerate(edge_terms(own, far, own, far, stiff)):
        terms[side] = term
        out[side][0] = value[side][...] + term
    for side in range(4):
        for end in range(2):
            row = slice(31 * end, 31 * end + 1)
            other = (2 if side < 2 else 0) + end
            at = slice(31 * (side % 2), 31 * (side % 2) + 1)
            out[side][0, row, :] += terms[other, at, :]


def fix_faces(own, far, values, stiff):
    return pl.pallas_call(
        fix_kernel,
        in_specs=[VMEM] * 16,
        out_specs=[VMEM] * 4,
        out_shape=[f32(1, PLANES, DEPTH)] * 4,
        scratch_shapes=[pltpu.VMEM((4, PLANES, DEPTH), jnp.float32)],
        compiler_params=ROOM,
        cost_estimate=pl.CostEstimate(flops=1 << 20, bytes_accessed=2 << 20, transcendentals=0),
        name="fix_faces",
    )(*own, *far, *values, *stiff)


def interpolation():
    fine = lax.broadcasted_iota(jnp.int32, (COARSE, DEPTH), 1)
    coarse = lax.broadcasted_iota(jnp.int32, (COARSE, DEPTH), 0)
    gap = jnp.abs(fine - 2 * coarse).astype(jnp.float32)
    return jnp.maximum(1.0 - 0.5 * gap, 0.0).astype(jnp.bfloat16)


def dot(a, b):
    return jnp.dot(a, b, preferred_element_type=jnp.float32)


def coarse_kernel(received, onehot, along, rim_x, rim_y, corner, rows):
    high, low = split_bf16(received[...])
    c_high = dot(onehot[...], high)
    c_low = dot(onehot[...], low)
    coarse = c_high + c_low
    for n in range(2):
        rim_x[n] = coarse[n * 256 : n * 256 + 16, :]
        corner[n] = coarse[n * 256 : n * 256 + 8, :]
    for half in range(2):
        lanes = slice(half * 128, half * 128 + 128)
        rows[half] = coarse[:, lanes]
        for n in range(2):
            rim_y[n, :, lanes] = rows[half, pl.ds(n * 256, 16, stride=16), :]
    weights = interpolation()
    along[...] = dot(c_high.astype(jnp.bfloat16), weights) + dot(c_low.astype(jnp.bfloat16), weights)


def coarse_tiles(received, onehot):
    return pl.pallas_call(
        coarse_kernel,
        in_specs=[VMEM, VMEM],
        out_specs=[VMEM] * 4,
        out_shape=[f32(512, DEPTH), f32(2, 16, COARSE), f32(2, 16, COARSE), f32(2, 8, COARSE)],
        scratch_shapes=[pltpu.VMEM((2, 512, 128), jnp.float32)],
        compiler_params=ROOM,
        cost_estimate=pl.CostEstimate(flops=1 << 30, bytes_accessed=3 << 20, transcendentals=0),
        name="coarse_tiles",
    )(received, onehot)


def image_kernel(source, along, rim_x, rim_y, corner, first_hbm, second, *rest):
    own, far, own2, far2, stiff = (rest[4 * k : 4 * k + 4] for k in range(5))
    image, saved, rims, rim_along, fine, out, first, terms, third, sem = rest[20:]
    load = pltpu.make_async_copy(first_hbm, first, sem.at[0])
    load.start()
    for side, term in enumerate(edge_terms(own, far, own2, far2, stiff)):
        terms[side] = term
    gx = lax.axis_index("gx")
    gy = lax.axis_index("gy")
    keep_x = jnp.where(gx < lax.axis_size("gx") - 1, 1.0, 0.0)
    keep_y = jnp.where(gy < lax.axis_size("gy") - 1, 1.0, 0.0)
    for n in range(2):
        rims[n * 40 : n * 40 + 16] = rim_x[n] * keep_x
        rims[n * 40 + 16 : n * 40 + 32] = rim_y[n] * keep_y
        rims[n * 40 + 32 : n * 40 + 40] = corner[n] * (keep_x * keep_y)
    weights = interpolation()
    high, low = split_bf16(rims[...])
    rim_along[...] = dot(high, weights) + dot(low, weights)
    row16 = lax.broadcasted_iota(jnp.int32, (16, DEPTH), 0)
    for n in range(2):
        for k in range(17):
            if k < 16:
                rows = along[n * 256 + k * 16 : n * 256 + k * 16 + 16, :]
                side = rim_along[n * 40 + 16 + k : n * 40 + 17 + k, :]
            else:
                rows = rim_along[n * 40 : n * 40 + 16, :]
                side = rim_along[n * 40 + 32 : n * 40 + 33, :]
            upper = jnp.where(row16 == 15, side, pltpu.roll(rows, 15, 0))
            base = (n * 17 + k) * PLANES
            middle = 0.5 * (rows + upper)
            for part in range(4):
                lanes = slice(part * 128, part * 128 + 128)
                fine[part, pl.ds(base, 16, stride=2), :] = rows[:, lanes]
                fine[part, pl.ds(base + 1, 16, stride=2), :] = middle[:, lanes]
    scale = -1.0 / (2.0 * MUTE_RADIUS * MUTE_RADIUS)
    y = (lax.broadcasted_iota(jnp.int32, (PLANES, DEPTH), 0) + gy * PLANES - source[0, 1]).astype(jnp.float32)
    z = (lax.broadcasted_iota(jnp.int32, (PLANES, DEPTH), 1) - source[0, 2]).astype(jnp.float32)
    decay_yz = jnp.exp((y * y + z * z) * scale)
    x_base = gx * PLANES - source[0, 0]
    load.wait()
    copies = []
    for k in range(16):
        for odd in range(2):
            x = 2 * k + odd
            at = slice(x * PLANES, (x + 1) * PLANES)
            value = second[at, :]
            if x == 0:
                value = value + terms[0]
            if x == PLANES - 1:
                value = value + terms[1]
            third[at, :] = value
            third[x * PLANES : x * PLANES + 1, :] += terms[2, x : x + 1, :]
            third[x * PLANES + 31 : x * PLANES + 32, :] += terms[3, x : x + 1, :]
            dx = jnp.full((1, 128), x_base + x, jnp.int32).astype(jnp.float32)
            decay = jnp.exp((dx * dx) * scale)
            for part in range(4):
                lanes = slice(part * 128, part * 128 + 128)
                taper = 1.0 - decay * decay_yz[:, lanes]
                snaps = []
                for n in range(2):
                    start = (n * 17 + k) * PLANES
                    snap = fine[part, start : start + PLANES, :]
                    if odd:
                        snap = 0.5 * (snap + fine[part, start + PLANES : start + 2 * PLANES, :])
                    snaps.append(snap)
                out[at, lanes] = taper * (
                    snaps[0] * first[at, lanes] + snaps[1] * third[at, lanes]
                )
        if k % 4 == 3:
            rows = pl.ds((k - 3) * 2 * PLANES, 8 * PLANES)
            for pos, (here, there) in enumerate(((out, image), (third, saved))):
                slot = 1 + 2 * (k // 4) + pos
                copies.append(pltpu.make_async_copy(here.at[rows], there.at[rows], sem.at[slot]))
                copies[-1].start()
    for copy in copies:
        copy.wait()


def imaging(source, along, rims, first, second, edges):
    big = pltpu.VMEM((ROWS, DEPTH), jnp.float32)
    return pl.pallas_call(
        image_kernel,
        in_specs=[SMEM] + [VMEM] * 4 + [ANY] + [VMEM] * 21,
        out_specs=[ANY, ANY],
        out_shape=[f32(ROWS, DEPTH)] * 2,
        scratch_shapes=[
            pltpu.VMEM((80, COARSE), jnp.float32),
            pltpu.VMEM((80, DEPTH), jnp.float32),
            pltpu.VMEM((4, 2 * 17 * PLANES, 128), jnp.float32),
            big,
            big,
            pltpu.VMEM((4, PLANES, DEPTH), jnp.float32),
            big,
            pltpu.SemaphoreType.DMA((9,)),
        ],
        compiler_params=ROOM,
        cost_estimate=pl.CostEstimate(flops=20 << 20, bytes_accessed=8 << 20, transcendentals=0),
        name="imaging",
    )(source, along, *rims, in_hbm(first), second, *edges)


def per_device(
    stiffness,
    buoyancy,
    older_field,
    current_field,
    stored_tiles,
    tile_ids,
    tile_counts,
    receiver_cells,
    receiver_data,
    source_cell,
):
    older = older_field[0].reshape(ROWS, DEPTH)
    current = current_field[0].reshape(ROWS, DEPTH)
    stiff = stiffness.reshape(ROWS, DEPTH)
    buoy = buoyancy.reshape(ROWS, DEPTH)

    own = faces(current_field[0], buoyancy)
    far = exchange(own)
    tiles, own = lax.optimization_barrier((stored_tiles, own))
    received = lax.all_to_all(
        tiles[0, 0], ("shot", "gx"), split_axis=0, concat_axis=0, tiled=True
    ).reshape(1024, COARSE)
    slot = lax.broadcasted_iota(jnp.int32, (32, 32), 1)
    ids = jnp.where(slot < tile_counts[0, 0][:, None], tile_ids[0, 0], -1).reshape(1, 1024)
    onehot = onehots(ids)
    src = sources(receiver_cells[0], receiver_data[0])
    partial, *rest = inner(current, older, buoy, stiff, src, [], 0)
    values, stiff_faces = rest[:4], rest[4:]
    own2 = fix_faces(own, far, values, stiff_faces)
    far2 = exchange(own2)

    along, rim_x, rim_y, corner = coarse_tiles(received, onehot)
    rims = [rotate(rim_x, "gx", -1), rotate(rim_y, "gy", -1), diagonal(corner)]
    third, last_older = inner(partial, current, buoy, stiff, src, own2, 1)
    edges = [*own, *far, *own2, *far2, *stiff_faces]
    image, last_current = imaging(source_cell, along, rims, last_older, third, edges)
    shape = current_field.shape
    return image.reshape(shape), last_older.reshape(shape), last_current.reshape(shape)


def exchange(own):
    x_lo, x_hi, y_lo, y_hi = own
    return [rotate(x_hi, "gx", 1), rotate(x_lo, "gx", -1), rotate(y_hi, "gy", 1), rotate(y_lo, "gy", -1)]


def diagonal(block):
    nx, ny = lax.axis_size("gx"), lax.axis_size("gy")
    route = [
        (i * ny + j, ((i - 1) % nx) * ny + (j - 1) % ny) for i in range(nx) for j in range(ny)
    ]
    return lax.ppermute(block, ("gx", "gy"), route)


def solution(mesh):
    in_specs = (
        P("gx", "gy", None),
        P("gx", "gy", None),
        P("shot", "gx", "gy", None),
        P("shot", "gx", "gy", None),
        P(("shot", "gx"), "gy", None, None, None),
        P(("shot", "gx"), "gy", None, None),
        P(("shot", "gx"), "gy", None),
        P("shot", None, None),
        P("shot", None, None),
        P("shot", None),
    )
    out_specs = (
        P("shot", "gx", "gy", None),
        P("shot", "gx", "gy", None),
        P("shot", "gx", "gy", None),
    )
    return jax.shard_map(
        per_device, mesh=mesh, in_specs=in_specs, out_specs=out_specs, check_vma=False
    )
```

```python
import jax
import jax.numpy as jnp
from jax import lax
from jax.experimental import pallas as pl
from jax.experimental.pallas import tpu as pltpu
from jax.sharding import PartitionSpec as P

MUTE_RADIUS = 3.0
PLANES = 32
ROWS = 1024
DEPTH = 512
COARSE = 256
CHUNKS = 4
PER = PLANES // CHUNKS
SPAN = ROWS // CHUNKS
VMEM = pl.BlockSpec(memory_space=pltpu.VMEM)
SMEM = pl.BlockSpec(memory_space=pltpu.SMEM)
ANY = pl.BlockSpec(memory_space=pl.ANY)
ROOM = pltpu.CompilerParams(vmem_limit_bytes=16 << 20)


def rotate(block, axis, step):
    count = lax.axis_size(axis)
    return lax.ppermute(block, axis, [(i, (i + step) % count) for i in range(count)])


def f32(*shape):
    return jax.ShapeDtypeStruct(shape, jnp.float32)


def split_bf16(x):
    high = x.astype(jnp.bfloat16)
    return high, (x - high.astype(jnp.float32)).astype(jnp.bfloat16)


def faces_kernel(fx_lo, fx_hi, fy_lo, fy_hi, bx_lo, bx_hi, by_lo, by_hi, sx_lo, sx_hi, sy_lo, sy_hi):
    for slot, refs in enumerate(((fx_lo, fx_hi, fy_lo, fy_hi), (bx_lo, bx_hi, by_lo, by_hi))):
        sx_lo[slot] = refs[0][0]
        sx_hi[slot] = refs[1][0]
        for x in range(PLANES):
            sy_lo[slot, x : x + 1, :] = refs[2][x, 0:1, :]
            sy_hi[slot, x : x + 1, :] = refs[3][x, 7:8, :]


def faces(field, buoyancy):
    plane_lo = pl.BlockSpec((1, PLANES, DEPTH), lambda i: (0, 0, 0))
    plane_hi = pl.BlockSpec((1, PLANES, DEPTH), lambda i: (PLANES - 1, 0, 0))
    rows_lo = pl.BlockSpec((PLANES, 8, DEPTH), lambda i: (0, 0, 0))
    rows_hi = pl.BlockSpec((PLANES, 8, DEPTH), lambda i: (0, PLANES // 8 - 1, 0))
    out = pl.BlockSpec((2, PLANES, DEPTH), lambda i: (0, 0, 0))
    return pl.pallas_call(
        faces_kernel,
        grid=(1,),
        in_specs=[plane_lo, plane_hi, rows_lo, rows_hi] * 2,
        out_specs=[out] * 4,
        out_shape=[f32(2, PLANES, DEPTH)] * 4,
        compiler_params=ROOM,
        cost_estimate=pl.CostEstimate(flops=0, bytes_accessed=3 << 20, transcendentals=0),
        name="faces",
    )(*([in_hbm(field)] * 4 + [in_hbm(buoyancy)] * 4))


def sources_kernel(cells, data, out):
    base_x = lax.axis_index("gx") * PLANES
    base_y = lax.axis_index("gy") * PLANES
    local_x = cells[0:1, :] - base_x
    local_y = cells[1:2, :] - base_y
    inside = (local_x >= 0) & (local_x < PLANES) & (local_y >= 0) & (local_y < PLANES)
    row = jnp.where(inside, local_x * PLANES + local_y, -1)
    depth_id = lax.broadcasted_iota(jnp.int32, (8, 1024), 0)
    here = depth_id == cells[2:3, :]
    parts = []
    for step in range(2):
        value = jnp.where(here, data[step : step + 1, :], 0.0)
        parts.append(split_bf16(value))
    table = jnp.concatenate([parts[0][0], parts[0][1], parts[1][0], parts[1][1]], axis=0)
    lane = lax.broadcasted_iota(jnp.int32, (128, 128), 1)
    pad = jnp.zeros((96, 1024), jnp.bfloat16)
    table = jnp.concatenate([table, pad], axis=0)
    for start in range(0, ROWS, 128):
        ids = lax.broadcasted_iota(jnp.int32, (128, 1024), 0) + start
        select = jnp.where(ids == row, 1.0, 0.0).astype(jnp.bfloat16)
        product = lax.dot_general(
            select, table, (((1,), (1,)), ((), ())), preferred_element_type=jnp.float32
        )
        for step in range(2):
            high = pltpu.roll(product, (128 - 16 * step) % 128, 1)
            low = pltpu.roll(product, 128 - 16 * step - 8, 1)
            out[step, start : start + 128, :] = jnp.where(lane < 8, high + low, 0.0)


def sources(cells, data):
    return pl.pallas_call(
        sources_kernel,
        in_specs=[VMEM, VMEM],
        out_specs=VMEM,
        out_shape=f32(2, ROWS, 128),
        cost_estimate=pl.CostEstimate(flops=1 << 29, bytes_accessed=2 << 20, transcendentals=0),
        compiler_params=ROOM,
        name="sources",
    )(cells, data)


def onehot_kernel(ids, out):
    for start in range(0, 512, 128):
        tile = lax.broadcasted_iota(jnp.int32, (128, 1024), 0) + start
        out[start : start + 128, :] = jnp.where(tile == ids[...], 1.0, 0.0).astype(jnp.bfloat16)


def onehots(ids):
    return pl.pallas_call(
        onehot_kernel,
        in_specs=[VMEM],
        out_specs=VMEM,
        out_shape=jax.ShapeDtypeStruct((512, 1024), jnp.bfloat16),
        cost_estimate=pl.CostEstimate(flops=1 << 20, bytes_accessed=2 << 20, transcendentals=0),
        compiler_params=ROOM,
        name="onehots",
    )(ids)


def in_hbm(x):
    return pltpu.with_memory_space_constraint(x, pltpu.HBM)


def edge_fluxes(own_b, far_b, own_f, far_f):
    gx = lax.axis_index("gx")
    gy = lax.axis_index("gy")
    keep = [
        jnp.where(gx > 0, 1.0, 0.0),
        jnp.where(gx < lax.axis_size("gx") - 1, 1.0, 0.0),
        jnp.where(gy > 0, 1.0, 0.0),
        jnp.where(gy < lax.axis_size("gy") - 1, 1.0, 0.0),
    ]
    return [
        (own_b[side][1] + keep[side] * far_b[side][1])
        * (keep[side] * far_f[side][0] - own_f[side][0])
        for side in range(4)
    ]


def inner_kernel(field, older, buoy, stiff, src, *rest, step):
    if step == 0:
        own, far, rest = rest[:4], rest[4:8], rest[8:]
        out, faces_out, stiff_out = rest[0], rest[1:5], rest[5:9]
        f_buf, b_buf, s_buf, o_buf, n_buf, edges, in_sem, out_sem = rest[9:]
    else:
        n_buf, f_buf, b_buf, s_buf, o_buf, in_sem = rest
    copies = []
    for chunk in range(CHUNKS):
        part = pl.ds(chunk * SPAN, SPAN)
        pairs = ((field, f_buf), (buoy, b_buf), (stiff, s_buf), (older, o_buf))
        group = [
            pltpu.make_async_copy(hbm.at[part], buf.at[part], in_sem.at[chunk, k])
            for k, (hbm, buf) in enumerate(pairs)
        ]
        for copy in group:
            copy.start()
        copies.append(group)
    row8 = lax.broadcasted_iota(jnp.int32, (8, DEPTH), 0)
    lane128 = lax.broadcasted_iota(jnp.int32, (PLANES, 128), 1)
    out_copies = []

    if step == 0:
        for side, flux in enumerate(edge_fluxes(own, far, own, far)):
            edges[side] = flux

    def arrive(chunk):
        for copy in copies[chunk][:2]:
            copy.wait()

    def plane(x, flux_before, last=False):
        base = pl.multiple_of(x * PLANES, PLANES)
        at = pl.ds(base, PLANES)
        c = f_buf[at, :]
        b = b_buf[at, :]
        if last:
            flux_x = edges[1] if step == 0 else jnp.zeros_like(c)
        else:
            nearby = pl.ds(base + PLANES, PLANES)
            flux_x = (b + b_buf[nearby, :]) * (f_buf[nearby, :] - c)
        flux_y = (b + pltpu.roll(b, PLANES - 1, 0)) * (pltpu.roll(c, PLANES - 1, 0) - c)
        flux_y = jnp.concatenate(
            [flux_y[0:24], jnp.where(row8 == 7, 0.0, flux_y[24:32])], axis=0
        )
        flux_z = (b + pltpu.roll(b, DEPTH - 1, 1)) * (pltpu.roll(c, DEPTH - 1, 1) - c)
        flux_z = jnp.concatenate(
            [flux_z[:, : DEPTH - 128], jnp.where(lane128 == 127, 0.0, flux_z[:, DEPTH - 128 :])],
            axis=1,
        )
        total = (flux_x - flux_before) + (flux_y - pltpu.roll(flux_y, 1, 0))
        total = total + (flux_z - pltpu.roll(flux_z, 1, 1))
        if step == 0:
            total = jnp.concatenate(
                [
                    total[0:8] + jnp.where(row8 == 0, edges[2, pl.ds(x, 1), :], 0.0),
                    total[8:24],
                    total[24:32] + jnp.where(row8 == 7, edges[3, pl.ds(x, 1), :], 0.0),
                ],
                axis=0,
            )
        head = slice(0, 128)
        tail = slice(DEPTH - 128, DEPTH)
        total = jnp.concatenate(
            [
                total[:, head] - jnp.where(lane128 == 0, b[:, head] * c[:, head], 0.0),
                total[:, 128 : DEPTH - 128],
                total[:, tail] - jnp.where(lane128 == 127, b[:, tail] * c[:, tail], 0.0),
            ],
            axis=1,
        )
        value = (2.0 * c - o_buf[at, :]) + (0.5 * s_buf[at, :]) * total
        n_buf[at, 128:DEPTH] = value[:, 128:]
        n_buf[at, head] = value[:, head] + src[step, at, :]
        if step == 0:
            faces_out[2][0, pl.ds(x, 1), :] = n_buf[pl.ds(base, 1), :]
            faces_out[3][0, pl.ds(x, 1), :] = n_buf[pl.ds(base + PLANES - 1, 1), :]
            stiff_out[2][pl.ds(x, 1), :] = s_buf[pl.ds(base, 1), :]
            stiff_out[3][pl.ds(x, 1), :] = s_buf[pl.ds(base + PLANES - 1, 1), :]
        return flux_x

    arrive(0)
    flux = -edges[0] if step == 0 else jnp.zeros((PLANES, DEPTH), jnp.float32)
    for chunk in range(CHUNKS):
        for copy in copies[chunk][2:]:
            copy.wait()
        if chunk + 1 < CHUNKS:
            arrive(chunk + 1)
            flux = lax.fori_loop(chunk * PER, chunk * PER + PER, plane, flux, unroll=4)
        else:
            flux = lax.fori_loop(chunk * PER, chunk * PER + PER - 4, plane, flux, unroll=4)
            for x in range(PLANES - 4, PLANES):
                flux = plane(x, flux, x == PLANES - 1)
        if step == 0:
            part = pl.ds(chunk * SPAN, SPAN)
            copy = pltpu.make_async_copy(n_buf.at[part], out.at[part], out_sem.at[chunk])
            copy.start()
            out_copies.append(copy)
    if step == 0:
        faces_out[0][0] = n_buf[0:PLANES, :]
        faces_out[1][0] = n_buf[ROWS - PLANES : ROWS, :]
        stiff_out[0][...] = s_buf[0:PLANES, :]
        stiff_out[1][...] = s_buf[ROWS - PLANES : ROWS, :]
    for copy in out_copies:
        copy.wait()


def inner(field, older, buoy, stiff, src, halos, step):
    big = pltpu.VMEM((ROWS, DEPTH), jnp.float32)
    scratch = [big] * 4
    sems = [pltpu.SemaphoreType.DMA((CHUNKS, 4))]
    if step == 0:
        out_shape = [pltpu.HBM((ROWS, DEPTH), jnp.float32)]
        out_shape += [f32(1, PLANES, DEPTH)] * 4 + [f32(PLANES, DEPTH)] * 4
        out_specs = [ANY] + [VMEM] * 8
        scratch = scratch + [big, pltpu.VMEM((4, PLANES, DEPTH), jnp.float32)]
        sems = sems + [pltpu.SemaphoreType.DMA((CHUNKS,))]
    else:
        out_shape, out_specs = big, VMEM
    return pl.pallas_call(
        lambda *refs: inner_kernel(*refs, step=step),
        in_specs=[ANY] * 4 + [VMEM] * (1 + len(halos)),
        out_specs=out_specs,
        out_shape=out_shape,
        scratch_shapes=scratch + sems,
        compiler_params=ROOM,
        cost_estimate=pl.CostEstimate(bytes_accessed=10 << 20, flops=1<<40, transcendentals=0),
        name="inner%d" % step,
    )(in_hbm(field), in_hbm(older), in_hbm(buoy), in_hbm(stiff), src, *halos)


def interpolation():
    fine = lax.broadcasted_iota(jnp.int32, (COARSE, DEPTH), 1)
    coarse = lax.broadcasted_iota(jnp.int32, (COARSE, DEPTH), 0)
    gap = jnp.abs(fine - 2 * coarse).astype(jnp.float32)
    return jnp.maximum(1.0 - 0.5 * gap, 0.0).astype(jnp.bfloat16)


def dot(a, b):
    return jnp.dot(a, b, preferred_element_type=jnp.float32)


def coarse_kernel(received, onehot, along, rim_x, rim_y, corner, rows):
    high, low = split_bf16(received[...])
    c_high = dot(onehot[...], high)
    c_low = dot(onehot[...], low)
    coarse = c_high + c_low
    for n in range(2):
        rim_x[n] = coarse[n * 256 : n * 256 + 16, :]
        corner[n] = coarse[n * 256 : n * 256 + 8, :]
    for half in range(2):
        lanes = slice(half * 128, half * 128 + 128)
        rows[half] = coarse[:, lanes]
        for n in range(2):
            rim_y[n, :, lanes] = rows[half, pl.ds(n * 256, 16, stride=16), :]
    weights = interpolation()
    along[...] = dot(c_high.astype(jnp.bfloat16), weights) + dot(c_low.astype(jnp.bfloat16), weights)


def coarse_tiles(received, onehot):
    return pl.pallas_call(
        coarse_kernel,
        in_specs=[VMEM, VMEM],
        out_specs=[VMEM] * 4,
        out_shape=[f32(512, DEPTH), f32(2, 16, COARSE), f32(2, 16, COARSE), f32(2, 8, COARSE)],
        scratch_shapes=[pltpu.VMEM((2, 512, 128), jnp.float32)],
        compiler_params=ROOM,
        cost_estimate=pl.CostEstimate(flops=1 << 30, bytes_accessed=3 << 20, transcendentals=0),
        name="coarse_tiles",
    )(received, onehot)


def image_kernel(source, along, rim_x, rim_y, corner, first_hbm, second, *rest):
    own, far, own2, far2, stiff = (rest[4 * k : 4 * k + 4] for k in range(5))
    image, saved, rims, rim_along, fine, out, first, terms, third, sem = rest[20:]
    load = pltpu.make_async_copy(first_hbm, first, sem.at[0])
    load.start()
    for side, flux in enumerate(edge_fluxes(own, far, own2, far2)):
        terms[side] = (0.5 * stiff[side][...]) * flux
    gx = lax.axis_index("gx")
    gy = lax.axis_index("gy")
    keep_x = jnp.where(gx < lax.axis_size("gx") - 1, 1.0, 0.0)
    keep_y = jnp.where(gy < lax.axis_size("gy") - 1, 1.0, 0.0)
    for n in range(2):
        rims[n * 40 : n * 40 + 16] = rim_x[n] * keep_x
        rims[n * 40 + 16 : n * 40 + 32] = rim_y[n] * keep_y
        rims[n * 40 + 32 : n * 40 + 40] = corner[n] * (keep_x * keep_y)
    weights = interpolation()
    high, low = split_bf16(rims[...])
    rim_along[...] = dot(high, weights) + dot(low, weights)
    row16 = lax.broadcasted_iota(jnp.int32, (16, DEPTH), 0)
    for n in range(2):
        for k in range(17):
            if k < 16:
                rows = along[n * 256 + k * 16 : n * 256 + k * 16 + 16, :]
                side = rim_along[n * 40 + 16 + k : n * 40 + 17 + k, :]
            else:
                rows = rim_along[n * 40 : n * 40 + 16, :]
                side = rim_along[n * 40 + 32 : n * 40 + 33, :]
            upper = jnp.where(row16 == 15, side, pltpu.roll(rows, 15, 0))
            base = (n * 17 + k) * PLANES
            middle = 0.5 * (rows + upper)
            for part in range(4):
                lanes = slice(part * 128, part * 128 + 128)
                fine[part, pl.ds(base, 16, stride=2), :] = rows[:, lanes]
                fine[part, pl.ds(base + 1, 16, stride=2), :] = middle[:, lanes]
    scale = -1.0 / (2.0 * MUTE_RADIUS * MUTE_RADIUS)
    y = (lax.broadcasted_iota(jnp.int32, (PLANES, DEPTH), 0) + gy * PLANES - source[0, 1]).astype(jnp.float32)
    z = (lax.broadcasted_iota(jnp.int32, (PLANES, DEPTH), 1) - source[0, 2]).astype(jnp.float32)
    decay_yz = jnp.exp((y * y + z * z) * scale)
    x_base = gx * PLANES - source[0, 0]
    load.wait()
    copies = []
    for k in range(16):
        for odd in range(2):
            x = 2 * k + odd
            at = slice(x * PLANES, (x + 1) * PLANES)
            value = second[at, :]
            if x == 0:
                value = value + terms[0]
            if x == PLANES - 1:
                value = value + terms[1]
            third[at, :] = value
            third[x * PLANES : x * PLANES + 1, :] += terms[2, x : x + 1, :]
            third[x * PLANES + 31 : x * PLANES + 32, :] += terms[3, x : x + 1, :]
            dx = jnp.full((1, 128), x_base + x, jnp.int32).astype(jnp.float32)
            decay = jnp.exp((dx * dx) * scale)
            for part in range(4):
                lanes = slice(part * 128, part * 128 + 128)
                taper = 1.0 - decay * decay_yz[:, lanes]
                snaps = []
                for n in range(2):
                    start = (n * 17 + k) * PLANES
                    snap = fine[part, start : start + PLANES, :]
                    if odd:
                        snap = 0.5 * (snap + fine[part, start + PLANES : start + 2 * PLANES, :])
                    snaps.append(snap)
                out[at, lanes] = taper * (
                    snaps[0] * first[at, lanes] + snaps[1] * third[at, lanes]
                )
        if k % 4 == 3:
            rows = pl.ds((k - 3) * 2 * PLANES, 8 * PLANES)
            for pos, (here, there) in enumerate(((out, image), (third, saved))):
                slot = 1 + 2 * (k // 4) + pos
                copies.append(pltpu.make_async_copy(here.at[rows], there.at[rows], sem.at[slot]))
                copies[-1].start()
    for copy in copies:
        copy.wait()


def imaging(source, along, rims, first, second, edges):
    big = pltpu.VMEM((ROWS, DEPTH), jnp.float32)
    return pl.pallas_call(
        image_kernel,
        in_specs=[SMEM] + [VMEM] * 4 + [ANY] + [VMEM] * 21,
        out_specs=[ANY, ANY],
        out_shape=[f32(ROWS, DEPTH)] * 2,
        scratch_shapes=[
            pltpu.VMEM((80, COARSE), jnp.float32),
            pltpu.VMEM((80, DEPTH), jnp.float32),
            pltpu.VMEM((4, 2 * 17 * PLANES, 128), jnp.float32),
            big,
            big,
            pltpu.VMEM((4, PLANES, DEPTH), jnp.float32),
            big,
            pltpu.SemaphoreType.DMA((9,)),
        ],
        compiler_params=ROOM,
        cost_estimate=pl.CostEstimate(flops=20 << 20, bytes_accessed=8 << 20, transcendentals=0),
        name="imaging",
    )(source, along, *rims, in_hbm(first), second, *edges)


def per_device(
    stiffness,
    buoyancy,
    older_field,
    current_field,
    stored_tiles,
    tile_ids,
    tile_counts,
    receiver_cells,
    receiver_data,
    source_cell,
):
    older = older_field[0].reshape(ROWS, DEPTH)
    current = current_field[0].reshape(ROWS, DEPTH)
    stiff = stiffness.reshape(ROWS, DEPTH)
    buoy = buoyancy.reshape(ROWS, DEPTH)

    own = faces(current_field[0], buoyancy)
    far = exchange(own)
    slot = lax.broadcasted_iota(jnp.int32, (32, 32), 1)
    ids = jnp.where(slot < tile_counts[0, 0][:, None], tile_ids[0, 0], -1).reshape(1, 1024)
    onehot = onehots(ids)
    src = sources(receiver_cells[0], receiver_data[0])
    tiles, far[2], far[3], onehot, src = lax.optimization_barrier(
        (stored_tiles, far[2], far[3], onehot, src)
    )
    received = lax.all_to_all(
        tiles[0, 0], ("shot", "gx"), split_axis=0, concat_axis=0, tiled=True
    ).reshape(1024, COARSE)
    second, *rest = inner(current, older, buoy, stiff, src, [*own, *far], 0)
    own2, stiff_faces = rest[:4], rest[4:]
    far2 = exchange(own2)

    along, rim_x, rim_y, corner = coarse_tiles(received, onehot)
    rims = [rotate(rim_x, "gx", -1), rotate(rim_y, "gy", -1), diagonal(corner)]
    third = inner(second, current, buoy, stiff, src, [], 1)
    edges = [*own, *far, *own2, *far2, *stiff_faces]
    image, last_current = imaging(source_cell, along, rims, second, third, edges)
    shape = current_field.shape
    return image.reshape(shape), second.reshape(shape), last_current.reshape(shape)


def exchange(own):
    x_lo, x_hi, y_lo, y_hi = own
    return [rotate(x_hi, "gx", 1), rotate(x_lo, "gx", -1), rotate(y_hi, "gy", 1), rotate(y_lo, "gy", -1)]


def diagonal(block):
    nx, ny = lax.axis_size("gx"), lax.axis_size("gy")
    route = [
        (i * ny + j, ((i - 1) % nx) * ny + (j - 1) % ny) for i in range(nx) for j in range(ny)
    ]
    return lax.ppermute(block, ("gx", "gy"), route)


def solution(mesh):
    in_specs = (
        P("gx", "gy", None),
        P("gx", "gy", None),
        P("shot", "gx", "gy", None),
        P("shot", "gx", "gy", None),
        P(("shot", "gx"), "gy", None, None, None),
        P(("shot", "gx"), "gy", None, None),
        P(("shot", "gx"), "gy", None),
        P("shot", None, None),
        P("shot", None, None),
        P("shot", None),
    )
    out_specs = (
        P("shot", "gx", "gy", None),
        P("shot", "gx", "gy", None),
        P("shot", "gx", "gy", None),
    )
    return jax.shard_map(
        per_device, mesh=mesh, in_specs=in_specs, out_specs=out_specs, check_vma=False
    )
```

```python
import jax
import jax.numpy as jnp
from jax import lax
from jax.experimental import pallas as pl
from jax.experimental.pallas import tpu as pltpu
from jax.sharding import PartitionSpec as P

MUTE_RADIUS = 3.0
PLANES = 32
ROWS = 1024
DEPTH = 512
COARSE = 256
CHUNKS = 4
PER = PLANES // CHUNKS
SPAN = ROWS // CHUNKS
VMEM = pl.BlockSpec(memory_space=pltpu.VMEM)
SMEM = pl.BlockSpec(memory_space=pltpu.SMEM)
ANY = pl.BlockSpec(memory_space=pl.ANY)
ROOM = pltpu.CompilerParams(vmem_limit_bytes=16 << 20)


def rotate(block, axis, step):
    count = lax.axis_size(axis)
    return lax.ppermute(block, axis, [(i, (i + step) % count) for i in range(count)])


def f32(*shape):
    return jax.ShapeDtypeStruct(shape, jnp.float32)


def split_bf16(x):
    high = x.astype(jnp.bfloat16)
    return high, (x - high.astype(jnp.float32)).astype(jnp.bfloat16)


def faces_kernel(fx_lo, fx_hi, fy_lo, fy_hi, bx_lo, bx_hi, by_lo, by_hi, sx_lo, sx_hi, sy_lo, sy_hi):
    for slot, refs in enumerate(((fx_lo, fx_hi, fy_lo, fy_hi), (bx_lo, bx_hi, by_lo, by_hi))):
        sx_lo[slot] = refs[0][0]
        sx_hi[slot] = refs[1][0]
        for x in range(PLANES):
            sy_lo[slot, x : x + 1, :] = refs[2][x, 0:1, :]
            sy_hi[slot, x : x + 1, :] = refs[3][x, 7:8, :]


def faces(field, buoyancy):
    plane_lo = pl.BlockSpec((1, PLANES, DEPTH), lambda i: (0, 0, 0))
    plane_hi = pl.BlockSpec((1, PLANES, DEPTH), lambda i: (PLANES - 1, 0, 0))
    rows_lo = pl.BlockSpec((PLANES, 8, DEPTH), lambda i: (0, 0, 0))
    rows_hi = pl.BlockSpec((PLANES, 8, DEPTH), lambda i: (0, PLANES // 8 - 1, 0))
    out = pl.BlockSpec((2, PLANES, DEPTH), lambda i: (0, 0, 0))
    return pl.pallas_call(
        faces_kernel,
        grid=(1,),
        in_specs=[plane_lo, plane_hi, rows_lo, rows_hi] * 2,
        out_specs=[out] * 4,
        out_shape=[f32(2, PLANES, DEPTH)] * 4,
        compiler_params=ROOM,
        cost_estimate=pl.CostEstimate(flops=0, bytes_accessed=3 << 20, transcendentals=0),
        name="faces",
    )(*([in_hbm(field)] * 4 + [in_hbm(buoyancy)] * 4))


def sources_kernel(cells, data, out):
    base_x = lax.axis_index("gx") * PLANES
    base_y = lax.axis_index("gy") * PLANES
    local_x = cells[0:1, :] - base_x
    local_y = cells[1:2, :] - base_y
    inside = (local_x >= 0) & (local_x < PLANES) & (local_y >= 0) & (local_y < PLANES)
    row = jnp.where(inside, local_x * PLANES + local_y, -1)
    depth_id = lax.broadcasted_iota(jnp.int32, (8, 1024), 0)
    here = depth_id == cells[2:3, :]
    parts = []
    for step in range(2):
        value = jnp.where(here, data[step : step + 1, :], 0.0)
        parts.append(split_bf16(value))
    table = jnp.concatenate([parts[0][0], parts[0][1], parts[1][0], parts[1][1]], axis=0)
    lane = lax.broadcasted_iota(jnp.int32, (128, 128), 1)
    pad = jnp.zeros((96, 1024), jnp.bfloat16)
    table = jnp.concatenate([table, pad], axis=0)
    for start in range(0, ROWS, 128):
        ids = lax.broadcasted_iota(jnp.int32, (128, 1024), 0) + start
        select = jnp.where(ids == row, 1.0, 0.0).astype(jnp.bfloat16)
        product = lax.dot_general(
            select, table, (((1,), (1,)), ((), ())), preferred_element_type=jnp.float32
        )
        for step in range(2):
            high = pltpu.roll(product, (128 - 16 * step) % 128, 1)
            low = pltpu.roll(product, 128 - 16 * step - 8, 1)
            out[step, start : start + 128, :] = jnp.where(lane < 8, high + low, 0.0)


def sources(cells, data):
    return pl.pallas_call(
        sources_kernel,
        in_specs=[VMEM, VMEM],
        out_specs=VMEM,
        out_shape=f32(2, ROWS, 128),
        cost_estimate=pl.CostEstimate(flops=1, bytes_accessed=1, transcendentals=0),
        compiler_params=ROOM,
        name="sources",
    )(cells, data)


def onehot_kernel(ids, out):
    for start in range(0, 512, 128):
        tile = lax.broadcasted_iota(jnp.int32, (128, 1024), 0) + start
        out[start : start + 128, :] = jnp.where(tile == ids[...], 1.0, 0.0).astype(jnp.bfloat16)


def onehots(ids):
    return pl.pallas_call(
        onehot_kernel,
        in_specs=[VMEM],
        out_specs=VMEM,
        out_shape=jax.ShapeDtypeStruct((512, 1024), jnp.bfloat16),
        cost_estimate=pl.CostEstimate(flops=1, bytes_accessed=1, transcendentals=0),
        compiler_params=ROOM,
        name="onehots",
    )(ids)


def in_hbm(x):
    return pltpu.with_memory_space_constraint(x, pltpu.HBM)


def edge_fluxes(own_b, far_b, own_f, far_f):
    gx = lax.axis_index("gx")
    gy = lax.axis_index("gy")
    keep = [
        jnp.where(gx > 0, 1.0, 0.0),
        jnp.where(gx < lax.axis_size("gx") - 1, 1.0, 0.0),
        jnp.where(gy > 0, 1.0, 0.0),
        jnp.where(gy < lax.axis_size("gy") - 1, 1.0, 0.0),
    ]
    return [
        (own_b[side][1] + keep[side] * far_b[side][1])
        * (keep[side] * far_f[side][0] - own_f[side][0])
        for side in range(4)
    ]


def inner_kernel(field, older, buoy, stiff, src, *rest, step):
    if step == 0:
        own, far, rest = rest[:4], rest[4:8], rest[8:]
        out, faces_out, stiff_out = rest[0], rest[1:5], rest[5:9]
        f_buf, b_buf, s_buf, o_buf, n_buf, edges, in_sem, out_sem = rest[9:]
    else:
        out, f_buf, b_buf, s_buf, o_buf, n_buf, in_sem, out_sem = rest
    copies = []
    for chunk in range(CHUNKS):
        part = pl.ds(chunk * SPAN, SPAN)
        pairs = ((field, f_buf), (buoy, b_buf), (stiff, s_buf), (older, o_buf))
        group = [
            pltpu.make_async_copy(hbm.at[part], buf.at[part], in_sem.at[chunk, k])
            for k, (hbm, buf) in enumerate(pairs)
        ]
        for copy in group:
            copy.start()
        copies.append(group)
    row8 = lax.broadcasted_iota(jnp.int32, (8, DEPTH), 0)
    lane128 = lax.broadcasted_iota(jnp.int32, (PLANES, 128), 1)
    out_copies = []

    if step == 0:
        for side, flux in enumerate(edge_fluxes(own, far, own, far)):
            edges[side] = flux

    def arrive(chunk):
        for copy in copies[chunk][:2]:
            copy.wait()

    def plane(x, flux_before, last=False):
        base = pl.multiple_of(x * PLANES, PLANES)
        at = pl.ds(base, PLANES)
        c = f_buf[at, :]
        b = b_buf[at, :]
        if last:
            flux_x = edges[1] if step == 0 else jnp.zeros_like(c)
        else:
            nearby = pl.ds(base + PLANES, PLANES)
            flux_x = (b + b_buf[nearby, :]) * (f_buf[nearby, :] - c)
        flux_y = (b + pltpu.roll(b, PLANES - 1, 0)) * (pltpu.roll(c, PLANES - 1, 0) - c)
        flux_y = jnp.concatenate(
            [flux_y[0:24], jnp.where(row8 == 7, 0.0, flux_y[24:32])], axis=0
        )
        flux_z = (b + pltpu.roll(b, DEPTH - 1, 1)) * (pltpu.roll(c, DEPTH - 1, 1) - c)
        flux_z = jnp.concatenate(
            [flux_z[:, : DEPTH - 128], jnp.where(lane128 == 127, 0.0, flux_z[:, DEPTH - 128 :])],
            axis=1,
        )
        total = (flux_x - flux_before) + (flux_y - pltpu.roll(flux_y, 1, 0))
        total = total + (flux_z - pltpu.roll(flux_z, 1, 1))
        if step == 0:
            total = jnp.concatenate(
                [
                    total[0:8] + jnp.where(row8 == 0, edges[2, pl.ds(x, 1), :], 0.0),
                    total[8:24],
                    total[24:32] + jnp.where(row8 == 7, edges[3, pl.ds(x, 1), :], 0.0),
                ],
                axis=0,
            )
        head = slice(0, 128)
        tail = slice(DEPTH - 128, DEPTH)
        total = jnp.concatenate(
            [
                total[:, head] - jnp.where(lane128 == 0, b[:, head] * c[:, head], 0.0),
                total[:, 128 : DEPTH - 128],
                total[:, tail] - jnp.where(lane128 == 127, b[:, tail] * c[:, tail], 0.0),
            ],
            axis=1,
        )
        value = (2.0 * c - o_buf[at, :]) + (0.5 * s_buf[at, :]) * total
        n_buf[at, 128:DEPTH] = value[:, 128:]
        n_buf[at, head] = value[:, head] + src[step, at, :]
        if step == 0:
            faces_out[2][0, pl.ds(x, 1), :] = n_buf[pl.ds(base, 1), :]
            faces_out[3][0, pl.ds(x, 1), :] = n_buf[pl.ds(base + PLANES - 1, 1), :]
            stiff_out[2][pl.ds(x, 1), :] = s_buf[pl.ds(base, 1), :]
            stiff_out[3][pl.ds(x, 1), :] = s_buf[pl.ds(base + PLANES - 1, 1), :]
        return flux_x

    arrive(0)
    flux = -edges[0] if step == 0 else jnp.zeros((PLANES, DEPTH), jnp.float32)
    for chunk in range(CHUNKS):
        for copy in copies[chunk][2:]:
            copy.wait()
        if chunk + 1 < CHUNKS:
            arrive(chunk + 1)
            flux = lax.fori_loop(chunk * PER, chunk * PER + PER, plane, flux, unroll=4)
        else:
            flux = lax.fori_loop(chunk * PER, chunk * PER + PER - 4, plane, flux, unroll=4)
            for x in range(PLANES - 4, PLANES):
                flux = plane(x, flux, x == PLANES - 1)
        part = pl.ds(chunk * SPAN, SPAN)
        copy = pltpu.make_async_copy(n_buf.at[part], out.at[part], out_sem.at[chunk])
        copy.start()
        out_copies.append(copy)
    if step == 0:
        faces_out[0][0] = n_buf[0:PLANES, :]
        faces_out[1][0] = n_buf[ROWS - PLANES : ROWS, :]
        stiff_out[0][...] = s_buf[0:PLANES, :]
        stiff_out[1][...] = s_buf[ROWS - PLANES : ROWS, :]
    for copy in out_copies:
        copy.wait()


def inner(field, older, buoy, stiff, src, halos, step):
    big = pltpu.VMEM((ROWS, DEPTH), jnp.float32)
    scratch = [big] * 5
    sems = [pltpu.SemaphoreType.DMA((CHUNKS, 4)), pltpu.SemaphoreType.DMA((CHUNKS,))]
    out_shape = [pltpu.HBM((ROWS, DEPTH), jnp.float32)]
    out_specs = [ANY]
    if step == 0:
        out_shape += [f32(1, PLANES, DEPTH)] * 4 + [f32(PLANES, DEPTH)] * 4
        out_specs += [VMEM] * 8
        scratch = scratch + [pltpu.VMEM((4, PLANES, DEPTH), jnp.float32)]
    return pl.pallas_call(
        lambda *refs: inner_kernel(*refs, step=step),
        in_specs=[ANY] * 4 + [VMEM] * (1 + len(halos)),
        out_specs=out_specs,
        out_shape=out_shape,
        scratch_shapes=scratch + sems,
        compiler_params=ROOM,
        cost_estimate=pl.CostEstimate(bytes_accessed=10 << 20, flops=1<<40, transcendentals=0),
        name="inner%d" % step,
    )(in_hbm(field), in_hbm(older), in_hbm(buoy), in_hbm(stiff), src, *halos)


def interpolation():
    fine = lax.broadcasted_iota(jnp.int32, (COARSE, DEPTH), 1)
    coarse = lax.broadcasted_iota(jnp.int32, (COARSE, DEPTH), 0)
    gap = jnp.abs(fine - 2 * coarse).astype(jnp.float32)
    return jnp.maximum(1.0 - 0.5 * gap, 0.0).astype(jnp.bfloat16)


def dot(a, b):
    return jnp.dot(a, b, preferred_element_type=jnp.float32)


def coarse_kernel(received, onehot, along, rim_x, rim_y, corner, rows):
    high, low = split_bf16(received[...])
    c_high = dot(onehot[...], high)
    c_low = dot(onehot[...], low)
    coarse = c_high + c_low
    for n in range(2):
        rim_x[n] = coarse[n * 256 : n * 256 + 16, :]
        corner[n] = coarse[n * 256 : n * 256 + 8, :]
    for half in range(2):
        lanes = slice(half * 128, half * 128 + 128)
        rows[half] = coarse[:, lanes]
        for n in range(2):
            rim_y[n, :, lanes] = rows[half, pl.ds(n * 256, 16, stride=16), :]
    weights = interpolation()
    along[...] = dot(c_high.astype(jnp.bfloat16), weights) + dot(c_low.astype(jnp.bfloat16), weights)


def coarse_tiles(received, onehot):
    return pl.pallas_call(
        coarse_kernel,
        in_specs=[VMEM, VMEM],
        out_specs=[VMEM] * 4,
        out_shape=[f32(512, DEPTH), f32(2, 16, COARSE), f32(2, 16, COARSE), f32(2, 8, COARSE)],
        scratch_shapes=[pltpu.VMEM((2, 512, 128), jnp.float32)],
        compiler_params=ROOM,
        cost_estimate=pl.CostEstimate(flops=1 << 30, bytes_accessed=3 << 20, transcendentals=0),
        name="coarse_tiles",
    )(received, onehot)


def upsample_kernel(along, first_hbm, second_hbm, fine, first, second, sem):
    loads = [
        pltpu.make_async_copy(first_hbm, first, sem.at[0]),
        pltpu.make_async_copy(second_hbm, second, sem.at[1]),
    ]
    for copy in loads:
        copy.start()
    for n in range(2):
        for k in range(16):
            rows = along[n * 256 + k * 16 : n * 256 + k * 16 + 16, :]
            middle = 0.5 * (rows + pltpu.roll(rows, 15, 0))
            base = (n * 17 + k) * PLANES
            for part in range(4):
                lanes = slice(part * 128, part * 128 + 128)
                fine[part, pl.ds(base, 16, stride=2), :] = rows[:, lanes]
                fine[part, pl.ds(base + 1, 16, stride=2), :] = middle[:, lanes]
    for copy in loads:
        copy.wait()


def upsampling(along, first, second):
    big = pltpu.VMEM((ROWS, DEPTH), jnp.float32)
    return pl.pallas_call(
        upsample_kernel,
        in_specs=[VMEM, ANY, ANY],
        out_specs=[VMEM] * 3,
        out_shape=[pltpu.VMEM((4, 2 * 17 * PLANES, 128), jnp.float32), big, big],
        scratch_shapes=[pltpu.SemaphoreType.DMA((2,))],
        compiler_params=ROOM,
        cost_estimate=pl.CostEstimate(flops=1 << 40, bytes_accessed=8 << 20, transcendentals=0),
        name="upsampling",
    )(along, in_hbm(first), in_hbm(second))


def image_kernel(source, along, fine_in, rim_x, rim_y, corner, first, second, *rest):
    own, far, own2, far2, stiff = (rest[4 * k : 4 * k + 4] for k in range(5))
    image, saved, fine, rims, rim_along, out, terms, third, sem = rest[20:]
    for side, flux in enumerate(edge_fluxes(own, far, own2, far2)):
        terms[side] = (0.5 * stiff[side][...]) * flux
    gx = lax.axis_index("gx")
    gy = lax.axis_index("gy")
    keep_x = jnp.where(gx < lax.axis_size("gx") - 1, 1.0, 0.0)
    keep_y = jnp.where(gy < lax.axis_size("gy") - 1, 1.0, 0.0)
    for n in range(2):
        rims[n * 40 : n * 40 + 16] = rim_x[n] * keep_x
        rims[n * 40 + 16 : n * 40 + 32] = rim_y[n] * keep_y
        rims[n * 40 + 32 : n * 40 + 40] = corner[n] * (keep_x * keep_y)
    weights = interpolation()
    high, low = split_bf16(rims[...])
    rim_along[...] = dot(high, weights) + dot(low, weights)
    row16 = lax.broadcasted_iota(jnp.int32, (16, DEPTH), 0)
    for n in range(2):
        rows = rim_along[n * 40 : n * 40 + 16, :]
        side = rim_along[n * 40 + 32 : n * 40 + 33, :]
        middle = 0.5 * (rows + jnp.where(row16 == 15, side, pltpu.roll(rows, 15, 0)))
        base = (n * 17 + 16) * PLANES
        for part in range(4):
            lanes = slice(part * 128, part * 128 + 128)
            fine[part, pl.ds(base, 16, stride=2), :] = rows[:, lanes]
            fine[part, pl.ds(base + 1, 16, stride=2), :] = middle[:, lanes]
        for k in range(16):
            last = n * 256 + k * 16 + 15
            pair = n * 40 + 16 + k
            middle = 0.5 * (along[last : last + 1, :] + rim_along[pair : pair + 1, :])
            row = (n * 17 + k) * PLANES + 31
            for part in range(4):
                fine[part, row : row + 1, :] = middle[:, part * 128 : part * 128 + 128]
    scale = -1.0 / (2.0 * MUTE_RADIUS * MUTE_RADIUS)
    y = (lax.broadcasted_iota(jnp.int32, (PLANES, DEPTH), 0) + gy * PLANES - source[0, 1]).astype(jnp.float32)
    z = (lax.broadcasted_iota(jnp.int32, (PLANES, DEPTH), 1) - source[0, 2]).astype(jnp.float32)
    decay_yz = jnp.exp((y * y + z * z) * scale)
    x_base = gx * PLANES - source[0, 0]
    copies = []
    for k in range(16):
        for odd in range(2):
            x = 2 * k + odd
            at = slice(x * PLANES, (x + 1) * PLANES)
            value = second[at, :]
            if x == 0:
                value = value + terms[0]
            if x == PLANES - 1:
                value = value + terms[1]
            third[at, :] = value
            third[x * PLANES : x * PLANES + 1, :] += terms[2, x : x + 1, :]
            third[x * PLANES + 31 : x * PLANES + 32, :] += terms[3, x : x + 1, :]
            dx = jnp.full((1, 128), x_base + x, jnp.int32).astype(jnp.float32)
            decay = jnp.exp((dx * dx) * scale)
            for part in range(4):
                lanes = slice(part * 128, part * 128 + 128)
                taper = 1.0 - decay * decay_yz[:, lanes]
                snaps = []
                for n in range(2):
                    start = (n * 17 + k) * PLANES
                    snap = fine[part, start : start + PLANES, :]
                    if odd:
                        snap = 0.5 * (snap + fine[part, start + PLANES : start + 2 * PLANES, :])
                    snaps.append(snap)
                out[at, lanes] = taper * (
                    snaps[0] * first[at, lanes] + snaps[1] * third[at, lanes]
                )
        if k % 2 == 1:
            rows = pl.ds((k - 1) * 2 * PLANES, 4 * PLANES)
            for pos, (here, there) in enumerate(((out, image), (third, saved))):
                slot = 2 * (k // 2) + pos
                copies.append(pltpu.make_async_copy(here.at[rows], there.at[rows], sem.at[slot]))
                copies[-1].start()
    for copy in copies:
        copy.wait()


def imaging(source, along, fine, rims, first, second, edges):
    big = pltpu.VMEM((ROWS, DEPTH), jnp.float32)
    return pl.pallas_call(
        image_kernel,
        in_specs=[SMEM] + [VMEM] * 27,
        out_specs=[ANY, ANY, VMEM],
        out_shape=[pltpu.HBM((ROWS, DEPTH), jnp.float32)] * 2
        + [pltpu.VMEM((4, 2 * 17 * PLANES, 128), jnp.float32)],
        input_output_aliases={2: 2},
        scratch_shapes=[
            pltpu.VMEM((80, COARSE), jnp.float32),
            pltpu.VMEM((80, DEPTH), jnp.float32),
            big,
            pltpu.VMEM((4, PLANES, DEPTH), jnp.float32),
            big,
            pltpu.SemaphoreType.DMA((16,)),
        ],
        compiler_params=ROOM,
        cost_estimate=pl.CostEstimate(flops=20 << 20, bytes_accessed=8 << 20, transcendentals=0),
        name="imaging",
    )(source, along, fine, *rims, first, second, *edges)


def per_device(
    stiffness,
    buoyancy,
    older_field,
    current_field,
    stored_tiles,
    tile_ids,
    tile_counts,
    receiver_cells,
    receiver_data,
    source_cell,
):
    older = older_field[0].reshape(ROWS, DEPTH)
    current = current_field[0].reshape(ROWS, DEPTH)
    stiff = stiffness.reshape(ROWS, DEPTH)
    buoy = buoyancy.reshape(ROWS, DEPTH)

    own = list(faces(current_field[0], buoyancy))
    far = exchange(own)
    tiles, own[0] = lax.optimization_barrier((stored_tiles, own[0]))
    received = lax.all_to_all(
        tiles[0, 0], ("shot", "gx"), split_axis=0, concat_axis=0, tiled=True
    ).reshape(1024, COARSE)
    numbers, counts, far = lax.optimization_barrier((tile_ids, tile_counts, far))
    slot = lax.broadcasted_iota(jnp.int32, (32, 32), 1)
    ids = jnp.where(slot < counts[0, 0][:, None], numbers[0, 0], -1).reshape(1, 1024)
    onehot = onehots(ids)
    src = sources(receiver_cells[0], receiver_data[0])
    second, *rest = inner(current, older, buoy, stiff, src, [*own, *far], 0)
    own2, stiff_faces = rest[:4], rest[4:]
    far2 = exchange(own2)
    (third,) = inner(second, current, buoy, stiff, src, [], 1)

    received, third = lax.optimization_barrier((received, third))
    along, rim_x, rim_y, corner = coarse_tiles(received, onehot)
    rims = [rotate(rim_x, "gx", -1), rotate(rim_y, "gy", -1), diagonal(corner)]
    fine, second_near, third_near = upsampling(along, second, third)
    edges = [*own, *far, *own2, *far2, *stiff_faces]
    image, last_current, _ = imaging(
        source_cell, along, fine, rims, second_near, third_near, edges
    )
    shape = current_field.shape
    return image.reshape(shape), second.reshape(shape), last_current.reshape(shape)


def exchange(own):
    x_lo, x_hi, y_lo, y_hi = own
    return [rotate(x_hi, "gx", 1), rotate(x_lo, "gx", -1), rotate(y_hi, "gy", 1), rotate(y_lo, "gy", -1)]


def diagonal(block):
    nx, ny = lax.axis_size("gx"), lax.axis_size("gy")
    route = [
        (i * ny + j, ((i - 1) % nx) * ny + (j - 1) % ny) for i in range(nx) for j in range(ny)
    ]
    return lax.ppermute(block, ("gx", "gy"), route)


def solution(mesh):
    in_specs = (
        P("gx", "gy", None),
        P("gx", "gy", None),
        P("shot", "gx", "gy", None),
        P("shot", "gx", "gy", None),
        P(("shot", "gx"), "gy", None, None, None),
        P(("shot", "gx"), "gy", None, None),
        P(("shot", "gx"), "gy", None),
        P("shot", None, None),
        P("shot", None, None),
        P("shot", None),
    )
    out_specs = (
        P("shot", "gx", "gy", None),
        P("shot", "gx", "gy", None),
        P("shot", "gx", "gy", None),
    )
    return jax.shard_map(
        per_device, mesh=mesh, in_specs=in_specs, out_specs=out_specs, check_vma=False
    )
```

```python
import jax
import jax.numpy as jnp
from jax import lax
from jax.experimental import pallas as pl
from jax.experimental.pallas import tpu as pltpu
from jax.sharding import PartitionSpec as P

MUTE_RADIUS = 3.0
PLANES = 32
ROWS = 1024
DEPTH = 512
COARSE = 256
CHUNKS = 4
PER = PLANES // CHUNKS
SPAN = ROWS // CHUNKS
VMEM = pl.BlockSpec(memory_space=pltpu.VMEM)
SMEM = pl.BlockSpec(memory_space=pltpu.SMEM)
ANY = pl.BlockSpec(memory_space=pl.ANY)
ROOM = pltpu.CompilerParams(vmem_limit_bytes=16 << 20)


def rotate(block, axis, step):
    count = lax.axis_size(axis)
    return lax.ppermute(block, axis, [(i, (i + step) % count) for i in range(count)])


def f32(*shape):
    return jax.ShapeDtypeStruct(shape, jnp.float32)


def split_bf16(x):
    high = x.astype(jnp.bfloat16)
    return high, (x - high.astype(jnp.float32)).astype(jnp.bfloat16)


def faces_kernel(fx_lo, fx_hi, fy_lo, fy_hi, bx_lo, bx_hi, by_lo, by_hi, sx_lo, sx_hi, sy_lo, sy_hi):
    for slot, refs in enumerate(((fx_lo, fx_hi, fy_lo, fy_hi), (bx_lo, bx_hi, by_lo, by_hi))):
        sx_lo[slot] = refs[0][0]
        sx_hi[slot] = refs[1][0]
        for x in range(PLANES):
            sy_lo[slot, x : x + 1, :] = refs[2][x, 0:1, :]
            sy_hi[slot, x : x + 1, :] = refs[3][x, 7:8, :]


def faces(field, buoyancy):
    plane_lo = pl.BlockSpec((1, PLANES, DEPTH), lambda i: (0, 0, 0))
    plane_hi = pl.BlockSpec((1, PLANES, DEPTH), lambda i: (PLANES - 1, 0, 0))
    rows_lo = pl.BlockSpec((PLANES, 8, DEPTH), lambda i: (0, 0, 0))
    rows_hi = pl.BlockSpec((PLANES, 8, DEPTH), lambda i: (0, PLANES // 8 - 1, 0))
    out = pl.BlockSpec((2, PLANES, DEPTH), lambda i: (0, 0, 0))
    return pl.pallas_call(
        faces_kernel,
        grid=(1,),
        in_specs=[plane_lo, plane_hi, rows_lo, rows_hi] * 2,
        out_specs=[out] * 4,
        out_shape=[f32(2, PLANES, DEPTH)] * 4,
        compiler_params=ROOM,
        cost_estimate=pl.CostEstimate(flops=0, bytes_accessed=3 << 20, transcendentals=0),
        name="faces",
    )(*([in_hbm(field)] * 4 + [in_hbm(buoyancy)] * 4))


def sources_kernel(cells, data, out):
    base_x = lax.axis_index("gx") * PLANES
    base_y = lax.axis_index("gy") * PLANES
    local_x = cells[0:1, :] - base_x
    local_y = cells[1:2, :] - base_y
    inside = (local_x >= 0) & (local_x < PLANES) & (local_y >= 0) & (local_y < PLANES)
    row = jnp.where(inside, local_x * PLANES + local_y, -1)
    depth_id = lax.broadcasted_iota(jnp.int32, (8, 1024), 0)
    here = depth_id == cells[2:3, :]
    parts = []
    for step in range(2):
        value = jnp.where(here, data[step : step + 1, :], 0.0)
        parts.append(split_bf16(value))
    table = jnp.concatenate([parts[0][0], parts[0][1], parts[1][0], parts[1][1]], axis=0)
    lane = lax.broadcasted_iota(jnp.int32, (128, 128), 1)
    pad = jnp.zeros((96, 1024), jnp.bfloat16)
    table = jnp.concatenate([table, pad], axis=0)
    for start in range(0, ROWS, 128):
        ids = lax.broadcasted_iota(jnp.int32, (128, 1024), 0) + start
        select = jnp.where(ids == row, 1.0, 0.0).astype(jnp.bfloat16)
        product = lax.dot_general(
            select, table, (((1,), (1,)), ((), ())), preferred_element_type=jnp.float32
        )
        for step in range(2):
            high = pltpu.roll(product, (128 - 16 * step) % 128, 1)
            low = pltpu.roll(product, 128 - 16 * step - 8, 1)
            out[step, start : start + 128, :] = jnp.where(lane < 8, high + low, 0.0)


def sources(cells, data):
    return pl.pallas_call(
        sources_kernel,
        in_specs=[VMEM, VMEM],
        out_specs=VMEM,
        out_shape=f32(2, ROWS, 128),
        cost_estimate=pl.CostEstimate(flops=1, bytes_accessed=1, transcendentals=0),
        compiler_params=ROOM,
        name="sources",
    )(cells, data)


def onehot_kernel(ids, out):
    for start in range(0, 512, 128):
        tile = lax.broadcasted_iota(jnp.int32, (128, 1024), 0) + start
        out[start : start + 128, :] = jnp.where(tile == ids[...], 1.0, 0.0).astype(jnp.bfloat16)


def onehots(ids):
    return pl.pallas_call(
        onehot_kernel,
        in_specs=[VMEM],
        out_specs=VMEM,
        out_shape=jax.ShapeDtypeStruct((512, 1024), jnp.bfloat16),
        cost_estimate=pl.CostEstimate(flops=1, bytes_accessed=1, transcendentals=0),
        compiler_params=ROOM,
        name="onehots",
    )(ids)


def in_hbm(x):
    return pltpu.with_memory_space_constraint(x, pltpu.HBM)


def sides():
    gx = lax.axis_index("gx")
    gy = lax.axis_index("gy")
    return [
        jnp.where(gx > 0, 1.0, 0.0),
        jnp.where(gx < lax.axis_size("gx") - 1, 1.0, 0.0),
        jnp.where(gy > 0, 1.0, 0.0),
        jnp.where(gy < lax.axis_size("gy") - 1, 1.0, 0.0),
    ]


def edge_terms(own_b, far_b, own_f, far_f, stiff):
    terms = []
    for side, keep in enumerate(sides()):
        coef = 0.5 * (own_b[side][1] + keep * far_b[side][1])
        flux = coef * (keep * far_f[side] - own_f[side])
        terms.append(stiff[side][...] * flux)
    return terms


def inner_kernel(field, older, buoy, stiff, src, *rest, step):
    if step == 1:
        fixed, rest = rest[:4], rest[4:]
        out, saved, f_buf, b_buf, s_buf, o_buf, in_sem, out_sem = rest
        n_buf = out
    else:
        out, faces_out, stiff_out = rest[0], rest[1:5], rest[5:9]
        f_buf, b_buf, s_buf, o_buf, n_buf, in_sem, out_sem = rest[9:]
    copies = []
    for chunk in range(CHUNKS):
        part = pl.ds(chunk * SPAN, SPAN)
        pairs = ((field, f_buf), (buoy, b_buf), (stiff, s_buf), (older, o_buf))
        group = [
            pltpu.make_async_copy(hbm.at[part], buf.at[part], in_sem.at[chunk, k])
            for k, (hbm, buf) in enumerate(pairs)
        ]
        for copy in group:
            copy.start()
        copies.append(group)
    row8 = lax.broadcasted_iota(jnp.int32, (8, DEPTH), 0)
    lane128 = lax.broadcasted_iota(jnp.int32, (PLANES, 128), 1)
    out_copies = []

    def arrive(chunk):
        for copy in copies[chunk][:2]:
            copy.wait()
        if step == 1:
            if chunk == 0:
                f_buf[0:PLANES, :] = fixed[0][0:PLANES]
            if chunk == CHUNKS - 1:
                f_buf[ROWS - PLANES : ROWS, :] = fixed[1][0:PLANES]
            for x in range(chunk * PER, chunk * PER + PER):
                f_buf[x * PLANES : x * PLANES + 1, :] = fixed[2][x : x + 1, :]
                f_buf[x * PLANES + 31 : x * PLANES + 32, :] = fixed[3][x : x + 1, :]
            part = pl.ds(chunk * SPAN, SPAN)
            copy = pltpu.make_async_copy(f_buf.at[part], saved.at[part], out_sem.at[chunk])
            copy.start()
            out_copies.append(copy)

    def plane(x, flux_before, last=False):
        base = pl.multiple_of(x * PLANES, PLANES)
        at = pl.ds(base, PLANES)
        c = f_buf[at, :]
        b = b_buf[at, :]
        if last:
            flux_x = jnp.zeros_like(c)
        else:
            nearby = pl.ds(base + PLANES, PLANES)
            flux_x = (b + b_buf[nearby, :]) * (f_buf[nearby, :] - c)
        flux_y = (b + pltpu.roll(b, PLANES - 1, 0)) * (pltpu.roll(c, PLANES - 1, 0) - c)
        flux_y = jnp.concatenate(
            [flux_y[0:24], jnp.where(row8 == 7, 0.0, flux_y[24:32])], axis=0
        )
        flux_z = (b + pltpu.roll(b, DEPTH - 1, 1)) * (pltpu.roll(c, DEPTH - 1, 1) - c)
        flux_z = jnp.concatenate(
            [flux_z[:, : DEPTH - 128], jnp.where(lane128 == 127, 0.0, flux_z[:, DEPTH - 128 :])],
            axis=1,
        )
        total = (flux_x - flux_before) + (flux_y - pltpu.roll(flux_y, 1, 0))
        total = total + (flux_z - pltpu.roll(flux_z, 1, 1))
        head = slice(0, 128)
        tail = slice(DEPTH - 128, DEPTH)
        total = jnp.concatenate(
            [
                total[:, head] - jnp.where(lane128 == 0, b[:, head] * c[:, head], 0.0),
                total[:, 128 : DEPTH - 128],
                total[:, tail] - jnp.where(lane128 == 127, b[:, tail] * c[:, tail], 0.0),
            ],
            axis=1,
        )
        value = (2.0 * c - o_buf[at, :]) + (0.5 * s_buf[at, :]) * total
        n_buf[at, 128:DEPTH] = value[:, 128:]
        n_buf[at, head] = value[:, head] + src[step, at, :]
        if step == 0:
            faces_out[2][pl.ds(x, 1), :] = n_buf[pl.ds(base, 1), :]
            faces_out[3][pl.ds(x, 1), :] = n_buf[pl.ds(base + PLANES - 1, 1), :]
            stiff_out[2][pl.ds(x, 1), :] = s_buf[pl.ds(base, 1), :]
            stiff_out[3][pl.ds(x, 1), :] = s_buf[pl.ds(base + PLANES - 1, 1), :]
        return flux_x

    arrive(0)
    flux = jnp.zeros((PLANES, DEPTH), jnp.float32)
    for chunk in range(CHUNKS):
        for copy in copies[chunk][2:]:
            copy.wait()
        if chunk + 1 < CHUNKS:
            arrive(chunk + 1)
            flux = lax.fori_loop(chunk * PER, chunk * PER + PER, plane, flux, unroll=4)
        else:
            flux = lax.fori_loop(chunk * PER, chunk * PER + PER - 4, plane, flux, unroll=4)
            for x in range(PLANES - 4, PLANES):
                flux = plane(x, flux, x == PLANES - 1)
        if step == 0:
            part = pl.ds(chunk * SPAN, SPAN)
            copy = pltpu.make_async_copy(n_buf.at[part], out.at[part], out_sem.at[chunk])
            copy.start()
            out_copies.append(copy)
    if step == 0:
        faces_out[0][...] = n_buf[0:PLANES, :]
        faces_out[1][...] = n_buf[ROWS - PLANES : ROWS, :]
        stiff_out[0][...] = s_buf[0:PLANES, :]
        stiff_out[1][...] = s_buf[ROWS - PLANES : ROWS, :]
    for copy in out_copies:
        copy.wait()


def inner(field, older, buoy, stiff, src, fixed, step):
    big = pltpu.VMEM((ROWS, DEPTH), jnp.float32)
    if step == 0:
        out_shape = [pltpu.HBM((ROWS, DEPTH), jnp.float32)] + [f32(PLANES, DEPTH)] * 8
        out_specs = [ANY] + [VMEM] * 8
    else:
        out_shape = [big, pltpu.HBM((ROWS, DEPTH), jnp.float32)]
        out_specs = [VMEM, ANY]
    return pl.pallas_call(
        lambda *refs: inner_kernel(*refs, step=step),
        in_specs=[ANY] * 4 + [VMEM] * (1 + len(fixed)),
        out_specs=out_specs,
        out_shape=out_shape,
        scratch_shapes=[big] * (5 - step)
        + [pltpu.SemaphoreType.DMA((CHUNKS, 4)), pltpu.SemaphoreType.DMA((CHUNKS,))],
        compiler_params=ROOM,
        cost_estimate=pl.CostEstimate(flops=1 << 40, bytes_accessed=10 << 20, transcendentals=0),
        name="inner%d" % step,
    )(in_hbm(field), in_hbm(older), in_hbm(buoy), in_hbm(stiff), src, *fixed)


def fix_kernel(*refs):
    own, far, value, stiff = (refs[4 * k : 4 * k + 4] for k in range(4))
    rim_x, rim_y = refs[16:18]
    out, terms = refs[18:22], refs[22]
    first = [ref[0] for ref in own]
    second = [ref[0] for ref in far]
    for side, term in enumerate(edge_terms(own, far, first, second, stiff)):
        terms[side] = term
        out[side][0:PLANES] = value[side][...] + term
    for side in range(4):
        at = slice(31 * (side % 2), 31 * (side % 2) + 1)
        for end in range(2):
            row = slice(31 * end, 31 * end + 1)
            other = (2 if side < 2 else 0) + end
            out[side][row, :] += terms[other, at, :]
    out[0][PLANES : PLANES + 16] = rim_x[...]
    out[2][PLANES : PLANES + 16] = rim_y[...]


def fix_faces(own, far, values, stiff, rim_x, rim_y):
    return pl.pallas_call(
        fix_kernel,
        in_specs=[VMEM] * 18,
        out_specs=[VMEM] * 4,
        out_shape=[f32(PLANES + 16, DEPTH), f32(PLANES, DEPTH)] * 2,
        scratch_shapes=[pltpu.VMEM((4, PLANES, DEPTH), jnp.float32)],
        compiler_params=ROOM,
        cost_estimate=pl.CostEstimate(flops=1 << 20, bytes_accessed=2 << 20, transcendentals=0),
        name="fix_faces",
    )(*own, *far, *values, *stiff, rim_x, rim_y)


def interpolation():
    fine = lax.broadcasted_iota(jnp.int32, (COARSE, DEPTH), 1)
    coarse = lax.broadcasted_iota(jnp.int32, (COARSE, DEPTH), 0)
    gap = jnp.abs(fine - 2 * coarse).astype(jnp.float32)
    return jnp.maximum(1.0 - 0.5 * gap, 0.0).astype(jnp.bfloat16)


def dot(a, b):
    return jnp.dot(a, b, preferred_element_type=jnp.float32)


def coarse_kernel(received, onehot, along, rim_x, rim_y, rows):
    high, low = split_bf16(received[...])
    c_high = dot(onehot[...], high)
    c_low = dot(onehot[...], low)
    coarse = c_high + c_low
    for n in range(2):
        for half in range(2):
            lanes = slice(half * 128, half * 128 + 128)
            spot = slice(n * 256 + half * 128, n * 256 + half * 128 + 128)
            rim_x[:, spot] = coarse[n * 256 : n * 256 + 16, lanes]
            if n == 0:
                rows[half] = coarse[:, lanes]
            rim_y[:, spot] = rows[half, pl.ds(n * 256, 16, stride=16), :]
    weights = interpolation()
    along[...] = dot(c_high.astype(jnp.bfloat16), weights) + dot(c_low.astype(jnp.bfloat16), weights)


def coarse_tiles(received, onehot):
    return pl.pallas_call(
        coarse_kernel,
        in_specs=[VMEM, VMEM],
        out_specs=[VMEM] * 3,
        out_shape=[f32(512, DEPTH), f32(16, DEPTH), f32(16, DEPTH)],
        scratch_shapes=[pltpu.VMEM((2, 512, 128), jnp.float32)],
        compiler_params=ROOM,
        cost_estimate=pl.CostEstimate(flops=1 << 30, bytes_accessed=3 << 20, transcendentals=0),
        name="coarse_tiles",
    )(received, onehot)


def corner_kernel(message, out):
    out[...] = message[PLANES : PLANES + 8, :]


def corner_block(message):
    return pl.pallas_call(
        corner_kernel,
        in_specs=[VMEM],
        out_specs=VMEM,
        out_shape=f32(8, DEPTH),
        compiler_params=ROOM,
        name="corner_block",
    )(message)


def upsample_kernel(along, first_hbm, fine, first, sem):
    load = pltpu.make_async_copy(first_hbm, first, sem)
    load.start()
    for n in range(2):
        for k in range(16):
            rows = along[n * 256 + k * 16 : n * 256 + k * 16 + 16, :]
            middle = 0.5 * (rows + pltpu.roll(rows, 15, 0))
            base = (n * 17 + k) * PLANES
            for part in range(4):
                lanes = slice(part * 128, part * 128 + 128)
                fine[part, pl.ds(base, 16, stride=2), :] = rows[:, lanes]
                fine[part, pl.ds(base + 1, 16, stride=2), :] = middle[:, lanes]
    load.wait()


def upsampling(along, first):
    return pl.pallas_call(
        upsample_kernel,
        in_specs=[VMEM, ANY],
        out_specs=[VMEM] * 2,
        out_shape=[
            pltpu.VMEM((4, 2 * 17 * PLANES, 128), jnp.float32),
            pltpu.VMEM((ROWS, DEPTH), jnp.float32),
        ],
        scratch_shapes=[pltpu.SemaphoreType.DMA],
        compiler_params=ROOM,
        cost_estimate=pl.CostEstimate(flops=1 << 40, bytes_accessed=8 << 20, transcendentals=0),
        name="upsampling",
    )(along, in_hbm(first))


def image_kernel(source, along, fine_in, corner, first, second, *rest):
    own, far, own2, far2, stiff = (rest[4 * k : 4 * k + 4] for k in range(5))
    image, saved, fine, rims, rim_along, out, terms, third, sem = rest[20:]
    near = [ref[0:PLANES] for ref in own2]
    distant = [ref[0:PLANES] for ref in far2]
    for side, term in enumerate(edge_terms(own, far, near, distant, stiff)):
        terms[side] = term
    gx = lax.axis_index("gx")
    gy = lax.axis_index("gy")
    keep_x = jnp.where(gx < lax.axis_size("gx") - 1, 1.0, 0.0)
    keep_y = jnp.where(gy < lax.axis_size("gy") - 1, 1.0, 0.0)
    for n in range(2):
        lanes = slice(n * 256, n * 256 + 256)
        rims[n * 40 : n * 40 + 16] = far2[1][PLANES : PLANES + 16, lanes] * keep_x
        rims[n * 40 + 16 : n * 40 + 32] = far2[3][PLANES : PLANES + 16, lanes] * keep_y
        rims[n * 40 + 32 : n * 40 + 40] = corner[:, lanes] * (keep_x * keep_y)
    weights = interpolation()
    high, low = split_bf16(rims[...])
    rim_along[...] = dot(high, weights) + dot(low, weights)
    row16 = lax.broadcasted_iota(jnp.int32, (16, DEPTH), 0)
    for n in range(2):
        rows = rim_along[n * 40 : n * 40 + 16, :]
        side = rim_along[n * 40 + 32 : n * 40 + 33, :]
        middle = 0.5 * (rows + jnp.where(row16 == 15, side, pltpu.roll(rows, 15, 0)))
        base = (n * 17 + 16) * PLANES
        for part in range(4):
            lanes = slice(part * 128, part * 128 + 128)
            fine[part, pl.ds(base, 16, stride=2), :] = rows[:, lanes]
            fine[part, pl.ds(base + 1, 16, stride=2), :] = middle[:, lanes]
        for k in range(16):
            last = n * 256 + k * 16 + 15
            pair = n * 40 + 16 + k
            middle = 0.5 * (along[last : last + 1, :] + rim_along[pair : pair + 1, :])
            row = (n * 17 + k) * PLANES + 31
            for part in range(4):
                fine[part, row : row + 1, :] = middle[:, part * 128 : part * 128 + 128]
    scale = -1.0 / (2.0 * MUTE_RADIUS * MUTE_RADIUS)
    y = (lax.broadcasted_iota(jnp.int32, (PLANES, DEPTH), 0) + gy * PLANES - source[0, 1]).astype(jnp.float32)
    z = (lax.broadcasted_iota(jnp.int32, (PLANES, DEPTH), 1) - source[0, 2]).astype(jnp.float32)
    decay_yz = jnp.exp((y * y + z * z) * scale)
    x_base = gx * PLANES - source[0, 0]
    copies = []
    for k in range(16):
        for odd in range(2):
            x = 2 * k + odd
            at = slice(x * PLANES, (x + 1) * PLANES)
            value = second[at, :]
            if x == 0:
                value = value + terms[0]
            if x == PLANES - 1:
                value = value + terms[1]
            third[at, :] = value
            third[x * PLANES : x * PLANES + 1, :] += terms[2, x : x + 1, :]
            third[x * PLANES + 31 : x * PLANES + 32, :] += terms[3, x : x + 1, :]
            dx = jnp.full((1, 128), x_base + x, jnp.int32).astype(jnp.float32)
            decay = jnp.exp((dx * dx) * scale)
            for part in range(4):
                lanes = slice(part * 128, part * 128 + 128)
                taper = 1.0 - decay * decay_yz[:, lanes]
                snaps = []
                for n in range(2):
                    start = (n * 17 + k) * PLANES
                    snap = fine[part, start : start + PLANES, :]
                    if odd:
                        snap = 0.5 * (snap + fine[part, start + PLANES : start + 2 * PLANES, :])
                    snaps.append(snap)
                out[at, lanes] = taper * (
                    snaps[0] * first[at, lanes] + snaps[1] * third[at, lanes]
                )
        if k % 2 == 1:
            rows = pl.ds((k - 1) * 2 * PLANES, 4 * PLANES)
            for pos, (here, there) in enumerate(((out, image), (third, saved))):
                slot = 2 * (k // 2) + pos
                copies.append(pltpu.make_async_copy(here.at[rows], there.at[rows], sem.at[slot]))
                copies[-1].start()
    for copy in copies:
        copy.wait()


def imaging(source, along, fine, corner, first, second, edges):
    big = pltpu.VMEM((ROWS, DEPTH), jnp.float32)
    return pl.pallas_call(
        image_kernel,
        in_specs=[SMEM] + [VMEM] * 25,
        out_specs=[ANY, ANY, VMEM],
        out_shape=[pltpu.HBM((ROWS, DEPTH), jnp.float32)] * 2
        + [pltpu.VMEM((4, 2 * 17 * PLANES, 128), jnp.float32)],
        input_output_aliases={2: 2},
        scratch_shapes=[
            pltpu.VMEM((80, COARSE), jnp.float32),
            pltpu.VMEM((80, DEPTH), jnp.float32),
            big,
            pltpu.VMEM((4, PLANES, DEPTH), jnp.float32),
            big,
            pltpu.SemaphoreType.DMA((16,)),
        ],
        compiler_params=ROOM,
        cost_estimate=pl.CostEstimate(flops=20 << 20, bytes_accessed=8 << 20, transcendentals=0),
        name="imaging",
    )(source, along, fine, corner, first, second, *edges)


def per_device(
    stiffness,
    buoyancy,
    older_field,
    current_field,
    stored_tiles,
    tile_ids,
    tile_counts,
    receiver_cells,
    receiver_data,
    source_cell,
):
    older = older_field[0].reshape(ROWS, DEPTH)
    current = current_field[0].reshape(ROWS, DEPTH)
    stiff = stiffness.reshape(ROWS, DEPTH)
    buoy = buoyancy.reshape(ROWS, DEPTH)

    received = lax.all_to_all(
        stored_tiles[0, 0], ("shot", "gx"), split_axis=0, concat_axis=0, tiled=True
    ).reshape(1024, COARSE)
    own = faces(current_field[0], buoyancy)
    far = exchange(own)
    slot = lax.broadcasted_iota(jnp.int32, (32, 32), 1)
    ids = jnp.where(slot < tile_counts[0, 0][:, None], tile_ids[0, 0], -1).reshape(1, 1024)
    onehot = onehots(ids)
    src = sources(receiver_cells[0], receiver_data[0])
    partial, *rest = inner(current, older, buoy, stiff, src, [], 0)
    values, stiff_faces = rest[:4], rest[4:]
    along, rim_x, rim_y = coarse_tiles(received, onehot)
    own2 = fix_faces(own, far, values, stiff_faces, rim_x, rim_y)
    far2 = exchange(own2)
    third, second = inner(partial, current, buoy, stiff, src, own2, 1)
    corner = rotate(corner_block(far2[1]), "gy", -1)
    fine, second_near = upsampling(along, second)
    edges = [*own, *far, *own2, *far2, *stiff_faces]
    image, last_current, _ = imaging(
        source_cell, along, fine, corner, second_near, third, edges
    )
    shape = current_field.shape
    return image.reshape(shape), second.reshape(shape), last_current.reshape(shape)


def exchange(own):
    x_lo, x_hi, y_lo, y_hi = own
    return [rotate(x_hi, "gx", 1), rotate(x_lo, "gx", -1), rotate(y_hi, "gy", 1), rotate(y_lo, "gy", -1)]


def solution(mesh):
    in_specs = (
        P("gx", "gy", None),
        P("gx", "gy", None),
        P("shot", "gx", "gy", None),
        P("shot", "gx", "gy", None),
        P(("shot", "gx"), "gy", None, None, None),
        P(("shot", "gx"), "gy", None, None),
        P(("shot", "gx"), "gy", None),
        P("shot", None, None),
        P("shot", None, None),
        P("shot", None),
    )
    out_specs = (
        P("shot", "gx", "gy", None),
        P("shot", "gx", "gy", None),
        P("shot", "gx", "gy", None),
    )
    return jax.shard_map(
        per_device, mesh=mesh, in_specs=in_specs, out_specs=out_specs, check_vma=False
    )
```

```python
import jax
import jax.numpy as jnp
from jax import lax
from jax.experimental import pallas as pl
from jax.experimental.pallas import tpu as pltpu
from jax.sharding import PartitionSpec as P

MUTE_RADIUS = 3.0
PLANES = 32
ROWS = 1024
DEPTH = 512
COARSE = 256
CHUNKS = 4
PER = PLANES // CHUNKS
SPAN = ROWS // CHUNKS
VMEM = pl.BlockSpec(memory_space=pltpu.VMEM)
SMEM = pl.BlockSpec(memory_space=pltpu.SMEM)
ANY = pl.BlockSpec(memory_space=pl.ANY)
ROOM = pltpu.CompilerParams(vmem_limit_bytes=16 << 20)


def rotate(block, axis, step):
    count = lax.axis_size(axis)
    return lax.ppermute(block, axis, [(i, (i + step) % count) for i in range(count)])


def swap(block, axis, start):
    count = lax.axis_size(axis)
    route = []
    for low in range(start, count - 1, 2):
        route += [(low, low + 1), (low + 1, low)]
    return lax.ppermute(block, axis, route)


def parity():
    return lax.rem(lax.axis_index("gx"), 2)


def f32(*shape):
    return jax.ShapeDtypeStruct(shape, jnp.float32)


def split_bf16(x):
    high = x.astype(jnp.bfloat16)
    return high, (x - high.astype(jnp.float32)).astype(jnp.bfloat16)


def faces_kernel(fx_lo, fx_hi, fy_lo, fy_hi, bx_lo, bx_hi, by_lo, by_hi, s_first, s_next, sy_lo, sy_hi):
    even = parity() == 0
    for slot, refs in enumerate(((fx_lo, fx_hi, fy_lo, fy_hi), (bx_lo, bx_hi, by_lo, by_hi))):
        low, high = refs[0][0], refs[1][0]
        s_first[slot] = jnp.where(even, high, low)
        s_next[slot] = jnp.where(even, low, high)
        for x in range(PLANES):
            sy_lo[slot, x : x + 1, :] = refs[2][x, 0:1, :]
            sy_hi[slot, x : x + 1, :] = refs[3][x, 7:8, :]


def faces(field, buoyancy):
    plane_lo = pl.BlockSpec((1, PLANES, DEPTH), lambda i: (0, 0, 0))
    plane_hi = pl.BlockSpec((1, PLANES, DEPTH), lambda i: (PLANES - 1, 0, 0))
    rows_lo = pl.BlockSpec((PLANES, 8, DEPTH), lambda i: (0, 0, 0))
    rows_hi = pl.BlockSpec((PLANES, 8, DEPTH), lambda i: (0, PLANES // 8 - 1, 0))
    out = pl.BlockSpec((2, PLANES, DEPTH), lambda i: (0, 0, 0))
    return pl.pallas_call(
        faces_kernel,
        grid=(1,),
        in_specs=[plane_lo, plane_hi, rows_lo, rows_hi] * 2,
        out_specs=[out] * 4,
        out_shape=[f32(2, PLANES, DEPTH)] * 4,
        compiler_params=ROOM,
        cost_estimate=pl.CostEstimate(flops=0, bytes_accessed=3 << 20, transcendentals=0),
        name="faces",
    )(*([in_hbm(field)] * 4 + [in_hbm(buoyancy)] * 4))


def sources_kernel(cells, data, out):
    base_x = lax.axis_index("gx") * PLANES
    base_y = lax.axis_index("gy") * PLANES
    local_x = cells[0:1, :] - base_x
    local_y = cells[1:2, :] - base_y
    inside = (local_x >= 0) & (local_x < PLANES) & (local_y >= 0) & (local_y < PLANES)
    row = jnp.where(inside, local_x * PLANES + local_y, -1)
    depth_id = lax.broadcasted_iota(jnp.int32, (8, 1024), 0)
    here = depth_id == cells[2:3, :]
    parts = []
    for step in range(2):
        value = jnp.where(here, data[step : step + 1, :], 0.0)
        parts.append(split_bf16(value))
    table = jnp.concatenate([parts[0][0], parts[0][1], parts[1][0], parts[1][1]], axis=0)
    lane = lax.broadcasted_iota(jnp.int32, (128, 128), 1)
    pad = jnp.zeros((96, 1024), jnp.bfloat16)
    table = jnp.concatenate([table, pad], axis=0)
    for start in range(0, ROWS, 128):
        ids = lax.broadcasted_iota(jnp.int32, (128, 1024), 0) + start
        select = jnp.where(ids == row, 1.0, 0.0).astype(jnp.bfloat16)
        product = lax.dot_general(
            select, table, (((1,), (1,)), ((), ())), preferred_element_type=jnp.float32
        )
        for step in range(2):
            high = pltpu.roll(product, (128 - 16 * step) % 128, 1)
            low = pltpu.roll(product, 128 - 16 * step - 8, 1)
            out[step, start : start + 128, :] = jnp.where(lane < 8, high + low, 0.0)


def sources(cells, data):
    return pl.pallas_call(
        sources_kernel,
        in_specs=[VMEM, VMEM],
        out_specs=VMEM,
        out_shape=f32(2, ROWS, 128),
        cost_estimate=pl.CostEstimate(flops=1, bytes_accessed=1, transcendentals=0),
        compiler_params=ROOM,
        name="sources",
    )(cells, data)


def onehot_kernel(ids, out):
    for start in range(0, 512, 128):
        tile = lax.broadcasted_iota(jnp.int32, (128, 1024), 0) + start
        out[start : start + 128, :] = jnp.where(tile == ids[...], 1.0, 0.0).astype(jnp.bfloat16)


def onehots(ids):
    return pl.pallas_call(
        onehot_kernel,
        in_specs=[VMEM],
        out_specs=VMEM,
        out_shape=jax.ShapeDtypeStruct((512, 1024), jnp.bfloat16),
        cost_estimate=pl.CostEstimate(flops=1, bytes_accessed=1, transcendentals=0),
        compiler_params=ROOM,
        name="onehots",
    )(ids)


def in_hbm(x):
    return pltpu.with_memory_space_constraint(x, pltpu.HBM)


def sides():
    gx = lax.axis_index("gx")
    gy = lax.axis_index("gy")
    inside = (gx > 0) & (gx < lax.axis_size("gx") - 1)
    return [
        1.0,
        jnp.where(inside, 1.0, 0.0),
        jnp.where(gy > 0, 1.0, 0.0),
        jnp.where(gy < lax.axis_size("gy") - 1, 1.0, 0.0),
    ]


def edge_terms(own_b, far_b, own_f, far_f, stiff):
    terms = []
    for side, keep in enumerate(sides()):
        coef = 0.5 * (own_b[side][1] + keep * far_b[side][1])
        flux = coef * (keep * far_f[side] - own_f[side])
        terms.append(stiff[side][...] * flux)
    return terms


def make_plane(f_buf, b_buf, s_buf, o_buf, n_buf, src, step):
    row8 = lax.broadcasted_iota(jnp.int32, (8, DEPTH), 0)
    lane128 = lax.broadcasted_iota(jnp.int32, (PLANES, 128), 1)

    def plane(x, flux_before, last=False):
        base = pl.multiple_of(x * PLANES, PLANES)
        at = pl.ds(base, PLANES)
        c = f_buf[at, :]
        b = b_buf[at, :]
        if last:
            flux_x = jnp.zeros_like(c)
        else:
            nearby = pl.ds(base + PLANES, PLANES)
            flux_x = (b + b_buf[nearby, :]) * (f_buf[nearby, :] - c)
        flux_y = (b + pltpu.roll(b, PLANES - 1, 0)) * (pltpu.roll(c, PLANES - 1, 0) - c)
        flux_y = jnp.concatenate(
            [flux_y[0:24], jnp.where(row8 == 7, 0.0, flux_y[24:32])], axis=0
        )
        flux_z = (b + pltpu.roll(b, DEPTH - 1, 1)) * (pltpu.roll(c, DEPTH - 1, 1) - c)
        flux_z = jnp.concatenate(
            [flux_z[:, : DEPTH - 128], jnp.where(lane128 == 127, 0.0, flux_z[:, DEPTH - 128 :])],
            axis=1,
        )
        total = (flux_x - flux_before) + (flux_y - pltpu.roll(flux_y, 1, 0))
        total = total + (flux_z - pltpu.roll(flux_z, 1, 1))
        head = slice(0, 128)
        tail = slice(DEPTH - 128, DEPTH)
        total = jnp.concatenate(
            [
                total[:, head] - jnp.where(lane128 == 0, b[:, head] * c[:, head], 0.0),
                total[:, 128 : DEPTH - 128],
                total[:, tail] - jnp.where(lane128 == 127, b[:, tail] * c[:, tail], 0.0),
            ],
            axis=1,
        )
        value = (2.0 * c - o_buf[at, :]) + (0.5 * s_buf[at, :]) * total
        n_buf[at, 128:DEPTH] = value[:, 128:]
        n_buf[at, head] = value[:, head] + src[step, at, :]
        return flux_x

    return plane


def inner0_kernel(field, older, buoy, stiff, src, out, *rest):
    values, stiff_out = rest[:4], rest[4:8]
    f_buf, b_buf, s_buf, o_buf, n_buf, in_sem, out_sem = rest[8:]
    copies = []
    for chunk in range(CHUNKS):
        part = pl.ds(chunk * SPAN, SPAN)
        pairs = ((field, f_buf), (buoy, b_buf), (stiff, s_buf), (older, o_buf))
        group = [
            pltpu.make_async_copy(hbm.at[part], buf.at[part], in_sem.at[chunk, k])
            for k, (hbm, buf) in enumerate(pairs)
        ]
        for copy in group:
            copy.start()
        copies.append(group)
    inner_plane = make_plane(f_buf, b_buf, s_buf, o_buf, n_buf, src, 0)

    def plane(x, flux, last=False):
        flux = inner_plane(x, flux, last)
        base = pl.multiple_of(x * PLANES, PLANES)
        for side in range(2):
            row = pl.ds(base + 31 * side, 1)
            values[2 + side][pl.ds(x, 1), :] = n_buf[row, :]
            stiff_out[2 + side][pl.ds(x, 1), :] = s_buf[row, :]
        return flux

    out_copies = []
    for copy in copies[0][:2]:
        copy.wait()
    flux = jnp.zeros((PLANES, DEPTH), jnp.float32)
    for chunk in range(CHUNKS):
        for copy in copies[chunk][2:]:
            copy.wait()
        if chunk + 1 < CHUNKS:
            for copy in copies[chunk + 1][:2]:
                copy.wait()
            flux = lax.fori_loop(chunk * PER, chunk * PER + PER, plane, flux, unroll=4)
        else:
            flux = lax.fori_loop(chunk * PER, chunk * PER + PER - 4, plane, flux, unroll=4)
            for x in range(PLANES - 4, PLANES):
                flux = plane(x, flux, x == PLANES - 1)
        part = pl.ds(chunk * SPAN, SPAN)
        copy = pltpu.make_async_copy(n_buf.at[part], out.at[part], out_sem.at[chunk])
        copy.start()
        out_copies.append(copy)
    odd = parity()
    for side in range(2):
        place = (1 - odd if side == 0 else odd) * (ROWS - PLANES)
        at = pl.ds(pl.multiple_of(place, PLANES), PLANES)
        values[side][...] = n_buf[at, :]
        stiff_out[side][...] = s_buf[at, :]
    for copy in out_copies:
        copy.wait()


def inner0(field, older, buoy, stiff, src):
    big = pltpu.VMEM((ROWS, DEPTH), jnp.float32)
    return pl.pallas_call(
        inner0_kernel,
        in_specs=[ANY] * 4 + [VMEM],
        out_specs=[ANY] + [VMEM] * 8,
        out_shape=[pltpu.HBM((ROWS, DEPTH), jnp.float32)] + [f32(PLANES, DEPTH)] * 8,
        scratch_shapes=[big] * 5
        + [pltpu.SemaphoreType.DMA((CHUNKS, 4)), pltpu.SemaphoreType.DMA((CHUNKS,))],
        compiler_params=ROOM,
        cost_estimate=pl.CostEstimate(flops=1 << 40, bytes_accessed=10 << 20, transcendentals=0),
        name="inner0",
    )(in_hbm(field), in_hbm(older), in_hbm(buoy), in_hbm(stiff), src)


def inner1_kernel(given, b_buf, s_buf, o_buf, src, x_first, x_next, y_lo, y_hi, f_buf, n_buf, saved, sem):
    even = parity() == 0
    first, following = x_first[0:PLANES], x_next[0:PLANES]
    f_buf[0:PLANES, :] = jnp.where(even, following, first)
    f_buf[ROWS - PLANES : ROWS, :] = jnp.where(even, first, following)
    for x in range(PLANES):
        f_buf[x * PLANES : x * PLANES + 1, :] = y_lo[x : x + 1, :]
        f_buf[x * PLANES + 31 : x * PLANES + 32, :] = y_hi[x : x + 1, :]
    save = pltpu.make_async_copy(f_buf, saved, sem)
    save.start()
    plane = make_plane(f_buf, b_buf, s_buf, o_buf, n_buf, src, 1)
    flux = jnp.zeros((PLANES, DEPTH), jnp.float32)
    flux = lax.fori_loop(0, PLANES - 4, plane, flux, unroll=4)
    for x in range(PLANES - 4, PLANES):
        flux = plane(x, flux, x == PLANES - 1)
    save.wait()


def inner1(given, buoy, stiff, older, src, fixed):
    big = pltpu.VMEM((ROWS, DEPTH), jnp.float32)
    return pl.pallas_call(
        inner1_kernel,
        in_specs=[VMEM] * 9,
        out_specs=[VMEM, VMEM, ANY],
        out_shape=[big, big, pltpu.HBM((ROWS, DEPTH), jnp.float32)],
        scratch_shapes=[pltpu.SemaphoreType.DMA],
        input_output_aliases={0: 0},
        compiler_params=ROOM,
        cost_estimate=pl.CostEstimate(flops=1 << 40, bytes_accessed=10 << 20, transcendentals=0),
        name="inner1",
    )(given, buoy, stiff, older, src, *fixed)


def fix_kernel(*refs):
    own, far, value, stiff = (refs[4 * k : 4 * k + 4] for k in range(4))
    rim_x, rim_corner = refs[16:18]
    out, terms = refs[18:22], refs[22]
    first = [ref[0] for ref in own]
    second = [ref[0] for ref in far]
    for side, term in enumerate(edge_terms(own, far, first, second, stiff)):
        terms[side] = term
        out[side][0:PLANES] = value[side][...] + term
    odd = parity()
    for side in range(2):
        place = (1 - odd if side == 0 else odd) * (PLANES - 1)
        for end in range(2):
            row = slice(31 * end, 31 * end + 1)
            out[side][row, :] += terms[2 + end, pl.ds(place, 1), :]
            out[2 + end][pl.ds(place, 1), :] += terms[side, row, :]
        out[side][PLANES : PLANES + 16] = rim_x[...]
        out[side][PLANES + 16 : PLANES + 24] = rim_corner[0:8, :]


def fix_faces(own, far, values, stiff, rim_x, rim_corner):
    return pl.pallas_call(
        fix_kernel,
        in_specs=[VMEM] * 18,
        out_specs=[VMEM] * 4,
        out_shape=[f32(PLANES + 24, DEPTH)] * 2 + [f32(PLANES, DEPTH)] * 2,
        scratch_shapes=[pltpu.VMEM((4, PLANES, DEPTH), jnp.float32)],
        compiler_params=ROOM,
        cost_estimate=pl.CostEstimate(flops=1 << 20, bytes_accessed=2 << 20, transcendentals=0),
        name="fix_faces",
    )(*own, *far, *values, *stiff, rim_x, rim_corner)


def interpolation():
    fine = lax.broadcasted_iota(jnp.int32, (COARSE, DEPTH), 1)
    coarse = lax.broadcasted_iota(jnp.int32, (COARSE, DEPTH), 0)
    gap = jnp.abs(fine - 2 * coarse).astype(jnp.float32)
    return jnp.maximum(1.0 - 0.5 * gap, 0.0).astype(jnp.bfloat16)


def dot(a, b):
    return jnp.dot(a, b, preferred_element_type=jnp.float32)


def coarse_kernel(received, onehot, along, rim_x, rim_y, rows):
    high, low = split_bf16(received[...])
    c_high = dot(onehot[...], high)
    c_low = dot(onehot[...], low)
    coarse = c_high + c_low
    for n in range(2):
        for half in range(2):
            lanes = slice(half * 128, half * 128 + 128)
            spot = slice(n * 256 + half * 128, n * 256 + half * 128 + 128)
            rim_x[:, spot] = coarse[n * 256 : n * 256 + 16, lanes]
            if n == 0:
                rows[half] = coarse[:, lanes]
            rim_y[:, spot] = rows[half, pl.ds(n * 256, 16, stride=16), :]
    weights = interpolation()
    along[...] = dot(c_high.astype(jnp.bfloat16), weights) + dot(c_low.astype(jnp.bfloat16), weights)


def coarse_tiles(received, onehot):
    return pl.pallas_call(
        coarse_kernel,
        in_specs=[VMEM, VMEM],
        out_specs=[VMEM] * 3,
        out_shape=[f32(512, DEPTH), f32(16, DEPTH), f32(16, DEPTH)],
        scratch_shapes=[pltpu.VMEM((2, 512, 128), jnp.float32)],
        compiler_params=ROOM,
        cost_estimate=pl.CostEstimate(flops=1 << 30, bytes_accessed=3 << 20, transcendentals=0),
        name="coarse_tiles",
    )(received, onehot)


def upsample_kernel(along, *refs):
    sources_hbm, fine, near, sem = refs[:4], refs[4], refs[5:9], refs[9]
    loads = [pltpu.make_async_copy(a, b, sem.at[k]) for k, (a, b) in enumerate(zip(sources_hbm, near))]
    for copy in loads:
        copy.start()
    for n in range(2):
        for k in range(16):
            rows = along[n * 256 + k * 16 : n * 256 + k * 16 + 16, :]
            middle = 0.5 * (rows + pltpu.roll(rows, 15, 0))
            base = (n * 17 + k) * PLANES
            for part in range(4):
                lanes = slice(part * 128, part * 128 + 128)
                fine[part, pl.ds(base, 16, stride=2), :] = rows[:, lanes]
                fine[part, pl.ds(base + 1, 16, stride=2), :] = middle[:, lanes]
    for copy in loads:
        copy.wait()


def upsampling(along, *arrays):
    big = pltpu.VMEM((ROWS, DEPTH), jnp.float32)
    return pl.pallas_call(
        upsample_kernel,
        in_specs=[VMEM] + [ANY] * 4,
        out_specs=[VMEM] * 5,
        out_shape=[pltpu.VMEM((4, 2 * 17 * PLANES, 128), jnp.float32)] + [big] * 4,
        scratch_shapes=[pltpu.SemaphoreType.DMA((4,))],
        compiler_params=ROOM,
        cost_estimate=pl.CostEstimate(flops=1 << 40, bytes_accessed=8 << 20, transcendentals=0),
        name="upsampling",
    )(along, *[in_hbm(a) for a in arrays])


def image_kernel(source, along, fine_in, rim_y, first, second, *rest):
    own, far, own2, far2, stiff = (rest[4 * k : 4 * k + 4] for k in range(5))
    image, saved, fine, rims, rim_along, out, terms, third, sem = rest[20:]
    even = parity() == 0
    near = [ref[0:PLANES] for ref in own2]
    distant = [ref[0:PLANES] for ref in far2]
    for side, term in enumerate(edge_terms(own, far, near, distant, stiff)):
        terms[side] = term
    gx = lax.axis_index("gx")
    gy = lax.axis_index("gy")
    keep_x = jnp.where(gx < lax.axis_size("gx") - 1, 1.0, 0.0)
    keep_y = jnp.where(gy < lax.axis_size("gy") - 1, 1.0, 0.0)
    for n in range(2):
        lanes = slice(n * 256, n * 256 + 256)
        ahead = jnp.where(even, far2[0][PLANES:, lanes], far2[1][PLANES:, lanes])
        rims[n * 40 : n * 40 + 16] = ahead[0:16] * keep_x
        rims[n * 40 + 16 : n * 40 + 32] = rim_y[:, lanes] * keep_y
        rims[n * 40 + 32 : n * 40 + 40] = ahead[16:24] * (keep_x * keep_y)
    weights = interpolation()
    high, low = split_bf16(rims[...])
    rim_along[...] = dot(high, weights) + dot(low, weights)
    row16 = lax.broadcasted_iota(jnp.int32, (16, DEPTH), 0)
    for n in range(2):
        rows = rim_along[n * 40 : n * 40 + 16, :]
        side = rim_along[n * 40 + 32 : n * 40 + 33, :]
        middle = 0.5 * (rows + jnp.where(row16 == 15, side, pltpu.roll(rows, 15, 0)))
        base = (n * 17 + 16) * PLANES
        for part in range(4):
            lanes = slice(part * 128, part * 128 + 128)
            fine[part, pl.ds(base, 16, stride=2), :] = rows[:, lanes]
            fine[part, pl.ds(base + 1, 16, stride=2), :] = middle[:, lanes]
        for k in range(16):
            last = n * 256 + k * 16 + 15
            pair = n * 40 + 16 + k
            middle = 0.5 * (along[last : last + 1, :] + rim_along[pair : pair + 1, :])
            row = (n * 17 + k) * PLANES + 31
            for part in range(4):
                fine[part, row : row + 1, :] = middle[:, part * 128 : part * 128 + 128]
    scale = -1.0 / (2.0 * MUTE_RADIUS * MUTE_RADIUS)
    y = (lax.broadcasted_iota(jnp.int32, (PLANES, DEPTH), 0) + gy * PLANES - source[0, 1]).astype(jnp.float32)
    z = (lax.broadcasted_iota(jnp.int32, (PLANES, DEPTH), 1) - source[0, 2]).astype(jnp.float32)
    decay_yz = jnp.exp((y * y + z * z) * scale)
    x_base = gx * PLANES - source[0, 0]
    copies = []
    for k in range(16):
        for odd in range(2):
            x = 2 * k + odd
            at = slice(x * PLANES, (x + 1) * PLANES)
            value = second[at, :]
            if x == 0:
                value = value + jnp.where(even, terms[1], terms[0])
            if x == PLANES - 1:
                value = value + jnp.where(even, terms[0], terms[1])
            third[at, :] = value
            third[x * PLANES : x * PLANES + 1, :] += terms[2, x : x + 1, :]
            third[x * PLANES + 31 : x * PLANES + 32, :] += terms[3, x : x + 1, :]
            dx = jnp.full((1, 128), x_base + x, jnp.int32).astype(jnp.float32)
            decay = jnp.exp((dx * dx) * scale)
            for part in range(4):
                lanes = slice(part * 128, part * 128 + 128)
                taper = 1.0 - decay * decay_yz[:, lanes]
                snaps = []
                for n in range(2):
                    start = (n * 17 + k) * PLANES
                    snap = fine[part, start : start + PLANES, :]
                    if odd:
                        snap = 0.5 * (snap + fine[part, start + PLANES : start + 2 * PLANES, :])
                    snaps.append(snap)
                out[at, lanes] = taper * (
                    snaps[0] * first[at, lanes] + snaps[1] * third[at, lanes]
                )
        if k % 2 == 1:
            rows = pl.ds((k - 1) * 2 * PLANES, 4 * PLANES)
            for pos, (here, there) in enumerate(((out, image), (third, saved))):
                slot = 2 * (k // 2) + pos
                copies.append(pltpu.make_async_copy(here.at[rows], there.at[rows], sem.at[slot]))
                copies[-1].start()
    for copy in copies:
        copy.wait()


def imaging(source, along, fine, rim_y, first, second, edges):
    big = pltpu.VMEM((ROWS, DEPTH), jnp.float32)
    return pl.pallas_call(
        image_kernel,
        in_specs=[SMEM] + [VMEM] * 25,
        out_specs=[ANY, ANY, VMEM],
        out_shape=[pltpu.HBM((ROWS, DEPTH), jnp.float32)] * 2
        + [pltpu.VMEM((4, 2 * 17 * PLANES, 128), jnp.float32)],
        input_output_aliases={2: 2},
        scratch_shapes=[
            pltpu.VMEM((80, COARSE), jnp.float32),
            pltpu.VMEM((80, DEPTH), jnp.float32),
            big,
            pltpu.VMEM((4, PLANES, DEPTH), jnp.float32),
            big,
            pltpu.SemaphoreType.DMA((16,)),
        ],
        compiler_params=ROOM,
        cost_estimate=pl.CostEstimate(flops=20 << 20, bytes_accessed=8 << 20, transcendentals=0),
        name="imaging",
    )(source, along, fine, rim_y, first, second, *edges)


def per_device(
    stiffness,
    buoyancy,
    older_field,
    current_field,
    stored_tiles,
    tile_ids,
    tile_counts,
    receiver_cells,
    receiver_data,
    source_cell,
):
    older = older_field[0].reshape(ROWS, DEPTH)
    current = current_field[0].reshape(ROWS, DEPTH)
    stiff = stiffness.reshape(ROWS, DEPTH)
    buoy = buoyancy.reshape(ROWS, DEPTH)

    own = list(faces(current_field[0], buoyancy))
    far = exchange(own)
    tiles, own[0] = lax.optimization_barrier((stored_tiles, own[0]))
    received = lax.all_to_all(
        tiles[0, 0], ("shot", "gx"), split_axis=0, concat_axis=0, tiled=True
    ).reshape(1024, COARSE)
    slot = lax.broadcasted_iota(jnp.int32, (32, 32), 1)
    ids = jnp.where(slot < tile_counts[0, 0][:, None], tile_ids[0, 0], -1).reshape(1, 1024)
    onehot = onehots(ids)
    src = sources(receiver_cells[0], receiver_data[0])
    partial, *rest = inner0(current, older, buoy, stiff, src)
    values, stiff_faces = rest[:4], rest[4:]
    along, rim_x, rim_y = coarse_tiles(received, onehot)
    rim_y_far = rotate(rim_y, "gy", -1)
    fine, partial, buoy_near, stiff_near, first_near = upsampling(along, partial, buoy, stiff, current)
    own2 = fix_faces(own, far, values, stiff_faces, rim_x, rim_y_far)
    far2 = exchange(own2)
    second_near, third, second = inner1(partial, buoy_near, stiff_near, first_near, src, own2)
    edges = [*own, *far, *own2, *far2, *stiff_faces]
    image, last_current, _ = imaging(
        source_cell, along, fine, rim_y_far, second_near, third, edges
    )
    shape = current_field.shape
    return image.reshape(shape), second.reshape(shape), last_current.reshape(shape)


def exchange(own):
    first, following, y_lo, y_hi = own
    return [
        swap(first, "gx", 0),
        swap(following, "gx", 1),
        rotate(y_hi, "gy", 1),
        rotate(y_lo, "gy", -1),
    ]


def solution(mesh):
    in_specs = (
        P("gx", "gy", None),
        P("gx", "gy", None),
        P("shot", "gx", "gy", None),
        P("shot", "gx", "gy", None),
        P(("shot", "gx"), "gy", None, None, None),
        P(("shot", "gx"), "gy", None, None),
        P(("shot", "gx"), "gy", None),
        P("shot", None, None),
        P("shot", None, None),
        P("shot", None),
    )
    out_specs = (
        P("shot", "gx", "gy", None),
        P("shot", "gx", "gy", None),
        P("shot", "gx", "gy", None),
    )
    return jax.shard_map(
        per_device, mesh=mesh, in_specs=in_specs, out_specs=out_specs, check_vma=False
    )
```

```python
import jax
import jax.numpy as jnp
from jax import lax
from jax.experimental import pallas as pl
from jax.experimental.pallas import tpu as pltpu
from jax.sharding import PartitionSpec as P

MUTE_RADIUS = 3.0
PLANES = 32
ROWS = 1024
DEPTH = 512
COARSE = 256
CHUNKS = 4
PER = PLANES // CHUNKS
SPAN = ROWS // CHUNKS
VMEM = pl.BlockSpec(memory_space=pltpu.VMEM)
SMEM = pl.BlockSpec(memory_space=pltpu.SMEM)
ANY = pl.BlockSpec(memory_space=pl.ANY)
ROOM = pltpu.CompilerParams(vmem_limit_bytes=16 << 20)


def rotate(block, axis, step):
    count = lax.axis_size(axis)
    return lax.ppermute(block, axis, [(i, (i + step) % count) for i in range(count)])


def f32(*shape):
    return jax.ShapeDtypeStruct(shape, jnp.float32)


def split_bf16(x):
    high = x.astype(jnp.bfloat16)
    return high, (x - high.astype(jnp.float32)).astype(jnp.bfloat16)


def faces_kernel(fx_lo, fx_hi, fy_lo, fy_hi, bx_lo, bx_hi, by_lo, by_hi, sx_lo, sx_hi, sy_lo, sy_hi):
    for slot, refs in enumerate(((fx_lo, fx_hi, fy_lo, fy_hi), (bx_lo, bx_hi, by_lo, by_hi))):
        sx_lo[slot] = refs[0][0]
        sx_hi[slot] = refs[1][0]
        for x in range(PLANES):
            sy_lo[slot, x : x + 1, :] = refs[2][x, 0:1, :]
            sy_hi[slot, x : x + 1, :] = refs[3][x, 7:8, :]


def faces(field, buoyancy):
    plane_lo = pl.BlockSpec((1, PLANES, DEPTH), lambda i: (0, 0, 0))
    plane_hi = pl.BlockSpec((1, PLANES, DEPTH), lambda i: (PLANES - 1, 0, 0))
    rows_lo = pl.BlockSpec((PLANES, 8, DEPTH), lambda i: (0, 0, 0))
    rows_hi = pl.BlockSpec((PLANES, 8, DEPTH), lambda i: (0, PLANES // 8 - 1, 0))
    out = pl.BlockSpec((2, PLANES, DEPTH), lambda i: (0, 0, 0))
    return pl.pallas_call(
        faces_kernel,
        grid=(1,),
        in_specs=[plane_lo, plane_hi, rows_lo, rows_hi] * 2,
        out_specs=[out] * 4,
        out_shape=[f32(2, PLANES, DEPTH)] * 4,
        compiler_params=ROOM,
        cost_estimate=pl.CostEstimate(flops=0, bytes_accessed=3 << 20, transcendentals=0),
        name="faces",
    )(*([in_hbm(field)] * 4 + [in_hbm(buoyancy)] * 4))


def sources_kernel(cells, data, out):
    base_x = lax.axis_index("gx") * PLANES
    base_y = lax.axis_index("gy") * PLANES
    local_x = cells[0:1, :] - base_x
    local_y = cells[1:2, :] - base_y
    inside = (local_x >= 0) & (local_x < PLANES) & (local_y >= 0) & (local_y < PLANES)
    row = jnp.where(inside, local_x * PLANES + local_y, -1)
    depth_id = lax.broadcasted_iota(jnp.int32, (8, 1024), 0)
    here = depth_id == cells[2:3, :]
    parts = []
    for step in range(2):
        value = jnp.where(here, data[step : step + 1, :], 0.0)
        parts.append(split_bf16(value))
    table = jnp.concatenate([parts[0][0], parts[0][1], parts[1][0], parts[1][1]], axis=0)
    lane = lax.broadcasted_iota(jnp.int32, (128, 128), 1)
    pad = jnp.zeros((96, 1024), jnp.bfloat16)
    table = jnp.concatenate([table, pad], axis=0)
    for start in range(0, ROWS, 128):
        ids = lax.broadcasted_iota(jnp.int32, (128, 1024), 0) + start
        select = jnp.where(ids == row, 1.0, 0.0).astype(jnp.bfloat16)
        product = lax.dot_general(
            select, table, (((1,), (1,)), ((), ())), preferred_element_type=jnp.float32
        )
        for step in range(2):
            high = pltpu.roll(product, (128 - 16 * step) % 128, 1)
            low = pltpu.roll(product, 128 - 16 * step - 8, 1)
            out[step, start : start + 128, :] = jnp.where(lane < 8, high + low, 0.0)


def sources(cells, data):
    return pl.pallas_call(
        sources_kernel,
        in_specs=[VMEM, VMEM],
        out_specs=VMEM,
        out_shape=f32(2, ROWS, 128),
        cost_estimate=pl.CostEstimate(flops=1, bytes_accessed=1, transcendentals=0),
        compiler_params=ROOM,
        name="sources",
    )(cells, data)


def in_hbm(x):
    return pltpu.with_memory_space_constraint(x, pltpu.HBM)


def edge_fluxes(own_b, far_b, own_f, far_f):
    gx = lax.axis_index("gx")
    gy = lax.axis_index("gy")
    keep = [
        jnp.where(gx > 0, 1.0, 0.0),
        jnp.where(gx < lax.axis_size("gx") - 1, 1.0, 0.0),
        jnp.where(gy > 0, 1.0, 0.0),
        jnp.where(gy < lax.axis_size("gy") - 1, 1.0, 0.0),
    ]
    return [
        (own_b[side][1] + keep[side] * far_b[side][1])
        * (keep[side] * far_f[side][0] - own_f[side][0])
        for side in range(4)
    ]


def inner_kernel(field, older, buoy, stiff, src, *rest, step):
    if step == 0:
        own, far, rest = rest[:4], rest[4:8], rest[8:]
        out, faces_out, stiff_out = rest[0], rest[1:5], rest[5:9]
        f_buf, b_buf, s_buf, o_buf, n_buf, edges, in_sem, out_sem = rest[9:]
    else:
        out, f_buf, b_buf, s_buf, o_buf, n_buf, in_sem, out_sem = rest
    copies = []
    for chunk in range(CHUNKS):
        part = pl.ds(chunk * SPAN, SPAN)
        pairs = ((field, f_buf), (buoy, b_buf), (stiff, s_buf), (older, o_buf))
        group = [
            pltpu.make_async_copy(hbm.at[part], buf.at[part], in_sem.at[chunk, k])
            for k, (hbm, buf) in enumerate(pairs)
        ]
        for copy in group:
            copy.start()
        copies.append(group)
    row8 = lax.broadcasted_iota(jnp.int32, (8, DEPTH), 0)
    lane128 = lax.broadcasted_iota(jnp.int32, (PLANES, 128), 1)
    out_copies = []

    if step == 0:
        for side, flux in enumerate(edge_fluxes(own, far, own, far)):
            edges[side] = flux

    def arrive(chunk):
        for copy in copies[chunk][:2]:
            copy.wait()

    def plane(x, flux_before, last=False):
        base = pl.multiple_of(x * PLANES, PLANES)
        at = pl.ds(base, PLANES)
        c = f_buf[at, :]
        b = b_buf[at, :]
        if last:
            flux_x = edges[1] if step == 0 else jnp.zeros_like(c)
        else:
            nearby = pl.ds(base + PLANES, PLANES)
            flux_x = (b + b_buf[nearby, :]) * (f_buf[nearby, :] - c)
        flux_y = (b + pltpu.roll(b, PLANES - 1, 0)) * (pltpu.roll(c, PLANES - 1, 0) - c)
        flux_y = jnp.concatenate(
            [flux_y[0:24], jnp.where(row8 == 7, 0.0, flux_y[24:32])], axis=0
        )
        flux_z = (b + pltpu.roll(b, DEPTH - 1, 1)) * (pltpu.roll(c, DEPTH - 1, 1) - c)
        flux_z = jnp.concatenate(
            [flux_z[:, : DEPTH - 128], jnp.where(lane128 == 127, 0.0, flux_z[:, DEPTH - 128 :])],
            axis=1,
        )
        total = (flux_x - flux_before) + (flux_y - pltpu.roll(flux_y, 1, 0))
        total = total + (flux_z - pltpu.roll(flux_z, 1, 1))
        if step == 0:
            total = jnp.concatenate(
                [
                    total[0:8] + jnp.where(row8 == 0, edges[2, pl.ds(x, 1), :], 0.0),
                    total[8:24],
                    total[24:32] + jnp.where(row8 == 7, edges[3, pl.ds(x, 1), :], 0.0),
                ],
                axis=0,
            )
        head = slice(0, 128)
        tail = slice(DEPTH - 128, DEPTH)
        total = jnp.concatenate(
            [
                total[:, head] - jnp.where(lane128 == 0, b[:, head] * c[:, head], 0.0),
                total[:, 128 : DEPTH - 128],
                total[:, tail] - jnp.where(lane128 == 127, b[:, tail] * c[:, tail], 0.0),
            ],
            axis=1,
        )
        value = (2.0 * c - o_buf[at, :]) + (0.5 * s_buf[at, :]) * total
        n_buf[at, 128:DEPTH] = value[:, 128:]
        n_buf[at, head] = value[:, head] + src[step, at, :]
        if step == 0:
            faces_out[2][0, pl.ds(x, 1), :] = n_buf[pl.ds(base, 1), :]
            faces_out[3][0, pl.ds(x, 1), :] = n_buf[pl.ds(base + PLANES - 1, 1), :]
            stiff_out[2][pl.ds(x, 1), :] = s_buf[pl.ds(base, 1), :]
            stiff_out[3][pl.ds(x, 1), :] = s_buf[pl.ds(base + PLANES - 1, 1), :]
        return flux_x

    arrive(0)
    flux = -edges[0] if step == 0 else jnp.zeros((PLANES, DEPTH), jnp.float32)
    for chunk in range(CHUNKS):
        for copy in copies[chunk][2:]:
            copy.wait()
        if chunk + 1 < CHUNKS:
            arrive(chunk + 1)
            flux = lax.fori_loop(chunk * PER, chunk * PER + PER, plane, flux, unroll=4)
        else:
            flux = lax.fori_loop(chunk * PER, chunk * PER + PER - 4, plane, flux, unroll=4)
            for x in range(PLANES - 4, PLANES):
                flux = plane(x, flux, x == PLANES - 1)
        part = pl.ds(chunk * SPAN, SPAN)
        copy = pltpu.make_async_copy(n_buf.at[part], out.at[part], out_sem.at[chunk])
        copy.start()
        out_copies.append(copy)
    if step == 0:
        faces_out[0][0] = n_buf[0:PLANES, :]
        faces_out[1][0] = n_buf[ROWS - PLANES : ROWS, :]
        stiff_out[0][...] = s_buf[0:PLANES, :]
        stiff_out[1][...] = s_buf[ROWS - PLANES : ROWS, :]
    for copy in out_copies:
        copy.wait()


def inner(field, older, buoy, stiff, src, halos, step):
    big = pltpu.VMEM((ROWS, DEPTH), jnp.float32)
    scratch = [big] * 5
    sems = [pltpu.SemaphoreType.DMA((CHUNKS, 4)), pltpu.SemaphoreType.DMA((CHUNKS,))]
    out_shape = [pltpu.HBM((ROWS, DEPTH), jnp.float32)]
    out_specs = [ANY]
    if step == 0:
        out_shape += [f32(1, PLANES, DEPTH)] * 4 + [f32(PLANES, DEPTH)] * 4
        out_specs += [VMEM] * 8
        scratch = scratch + [pltpu.VMEM((4, PLANES, DEPTH), jnp.float32)]
    return pl.pallas_call(
        lambda *refs: inner_kernel(*refs, step=step),
        in_specs=[ANY] * 4 + [VMEM] * (1 + len(halos)),
        out_specs=out_specs,
        out_shape=out_shape,
        scratch_shapes=scratch + sems,
        compiler_params=ROOM,
        cost_estimate=pl.CostEstimate(bytes_accessed=10 << 20, flops=1<<40, transcendentals=0),
        name="inner%d" % step,
    )(in_hbm(field), in_hbm(older), in_hbm(buoy), in_hbm(stiff), src, *halos)


def interpolation():
    fine = lax.broadcasted_iota(jnp.int32, (COARSE, DEPTH), 1)
    coarse = lax.broadcasted_iota(jnp.int32, (COARSE, DEPTH), 0)
    gap = jnp.abs(fine - 2 * coarse).astype(jnp.float32)
    return jnp.maximum(1.0 - 0.5 * gap, 0.0).astype(jnp.bfloat16)


def dot(a, b):
    return jnp.dot(a, b, preferred_element_type=jnp.float32)


def coarse_kernel(received, ids, along, rim_x, rim_y, corner, tiles, c_high, c_low, rows, sem):
    copies = []
    for part in range(4):
        at = pl.ds(part * 256, 256)
        copies.append(pltpu.make_async_copy(received.at[at], tiles.at[at], sem.at[part]))
        copies[-1].start()
    tile = lax.broadcasted_iota(jnp.int32, (512, 256), 0)
    for part in range(4):
        at = slice(part * 256, part * 256 + 256)
        select = jnp.where(tile == ids[:, at], 1.0, 0.0).astype(jnp.bfloat16)
        copies[part].wait()
        high, low = split_bf16(tiles[at, :])
        if part == 0:
            c_high[...] = dot(select, high)
            c_low[...] = dot(select, low)
        else:
            c_high[...] += dot(select, high)
            c_low[...] += dot(select, low)
    coarse = c_high[...] + c_low[...]
    for n in range(2):
        rim_x[n] = coarse[n * 256 : n * 256 + 16, :]
        corner[n] = coarse[n * 256 : n * 256 + 8, :]
    for half in range(2):
        lanes = slice(half * 128, half * 128 + 128)
        rows[half] = coarse[:, lanes]
        for n in range(2):
            rim_y[n, :, lanes] = rows[half, pl.ds(n * 256, 16, stride=16), :]
    weights = interpolation()
    along[...] = dot(c_high[...].astype(jnp.bfloat16), weights) + dot(
        c_low[...].astype(jnp.bfloat16), weights
    )


def coarse_tiles(received, ids):
    return pl.pallas_call(
        coarse_kernel,
        in_specs=[ANY, VMEM],
        out_specs=[VMEM] * 4,
        out_shape=[f32(512, DEPTH), f32(2, 16, COARSE), f32(2, 16, COARSE), f32(2, 8, COARSE)],
        scratch_shapes=[
            pltpu.VMEM((1024, COARSE), jnp.float32),
            pltpu.VMEM((512, COARSE), jnp.float32),
            pltpu.VMEM((512, COARSE), jnp.float32),
            pltpu.VMEM((2, 512, 128), jnp.float32),
            pltpu.SemaphoreType.DMA((4,)),
        ],
        compiler_params=ROOM,
        cost_estimate=pl.CostEstimate(flops=1 << 30, bytes_accessed=3 << 20, transcendentals=0),
        name="coarse_tiles",
    )(in_hbm(received), ids)


SCALE = -1.0 / (2.0 * MUTE_RADIUS * MUTE_RADIUS)


def picture_kernel(source, along, first_hbm, second_hbm, *rest):
    own, far, own2, far2, stiff = (rest[4 * k : 4 * k + 4] for k in range(5))
    image, saved, strip, plane_strip, last_plane, last_rows = rest[20:26]
    fine, out, first, third, terms, in_sem, sem = rest[26:]
    loads = []
    for k in range(4):
        at = pl.ds(k * SPAN, SPAN)
        pair = [
            pltpu.make_async_copy(first_hbm.at[at], first.at[at], in_sem.at[k, 0]),
            pltpu.make_async_copy(second_hbm.at[at], third.at[at], in_sem.at[k, 1]),
        ]
        for copy in pair:
            copy.start()
        loads.append(pair)
    for side, flux in enumerate(edge_fluxes(own, far, own2, far2)):
        terms[side] = (0.5 * stiff[side][...]) * flux
    row16 = lax.broadcasted_iota(jnp.int32, (16, DEPTH), 0)
    for n in range(2):
        for k in range(16):
            rows = along[n * 256 + k * 16 : n * 256 + k * 16 + 16, :]
            middle = 0.5 * (rows + jnp.where(row16 == 15, 0.0, pltpu.roll(rows, 15, 0)))
            base = (n * 17 + k) * PLANES
            for part in range(4):
                lanes = slice(part * 128, part * 128 + 128)
                fine[part, pl.ds(base, 16, stride=2), :] = rows[:, lanes]
                fine[part, pl.ds(base + 1, 16, stride=2), :] = middle[:, lanes]
        for part in range(4):
            base = (n * 17 + 16) * PLANES
            fine[part, base : base + PLANES, :] = jnp.zeros((PLANES, 128), jnp.float32)
    gx = lax.axis_index("gx")
    gy = lax.axis_index("gy")
    y = (lax.broadcasted_iota(jnp.int32, (PLANES, DEPTH), 0) + gy * PLANES - source[0, 1]).astype(jnp.float32)
    z = (lax.broadcasted_iota(jnp.int32, (PLANES, DEPTH), 1) - source[0, 2]).astype(jnp.float32)
    decay_yz = jnp.exp((y * y + z * z) * SCALE)
    x_base = gx * PLANES - source[0, 0]
    copies = []
    for x in range(PLANES):
        k = x // 2
        if x % PER == 0:
            for copy in loads[x // PER]:
                copy.wait()
        at = slice(x * PLANES, (x + 1) * PLANES)
        if x == 0:
            third[at, :] += terms[0]
        if x == PLANES - 1:
            third[at, :] += terms[1]
        third[x * PLANES : x * PLANES + 1, :] += terms[2, x : x + 1, :]
        third[x * PLANES + 31 : x * PLANES + 32, :] += terms[3, x : x + 1, :]
        last_rows[x : x + 1, :] = third[x * PLANES + 31 : x * PLANES + 32, :]
        dx = jnp.full((1, 128), x_base + x, jnp.int32).astype(jnp.float32)
        decay = jnp.exp((dx * dx) * SCALE)
        for part in range(4):
            lanes = slice(part * 128, part * 128 + 128)
            taper = 1.0 - decay * decay_yz[:, lanes]
            snaps = []
            for n in range(2):
                start = (n * 17 + k) * PLANES
                snap = fine[part, start : start + PLANES, :]
                if x % 2:
                    snap = 0.5 * (snap + fine[part, start + PLANES : start + 2 * PLANES, :])
                snaps.append(snap)
            value = taper * (snaps[0] * first[at, lanes] + snaps[1] * third[at, lanes])
            out[x, :, lanes] = value
            strip[x, :, lanes] = value[24:32]
        if x % 4 == 3:
            group = pl.ds(x - 3, 3 if x == PLANES - 1 else 4)
            rows = pl.ds((x - 3) * PLANES, 4 * PLANES)
            copies.append(
                pltpu.make_async_copy(
                    out.at[group, 0:24], image.at[group, 0:24], sem.at[x // 4, 0]
                )
            )
            copies.append(pltpu.make_async_copy(third.at[rows], saved.at[rows], sem.at[x // 4, 1]))
            for copy in copies[-2:]:
                copy.start()
    plane_strip[...] = out[PLANES - 1, 0:24, :]
    last_plane[...] = third[ROWS - PLANES : ROWS, :]
    for copy in copies:
        copy.wait()


def picture(source, along, first, second, edges):
    big = pltpu.VMEM((ROWS, DEPTH), jnp.float32)
    return pl.pallas_call(
        picture_kernel,
        in_specs=[SMEM, VMEM, ANY, ANY] + [VMEM] * 20,
        out_specs=[ANY, ANY] + [VMEM] * 4,
        out_shape=[
            pltpu.HBM((PLANES, PLANES, DEPTH), jnp.float32),
            pltpu.HBM((ROWS, DEPTH), jnp.float32),
            f32(PLANES, 8, DEPTH),
            f32(24, DEPTH),
            f32(PLANES, DEPTH),
            f32(PLANES, DEPTH),
        ],
        scratch_shapes=[
            pltpu.VMEM((4, 2 * 17 * PLANES, 128), jnp.float32),
            pltpu.VMEM((PLANES, PLANES, DEPTH), jnp.float32),
            big,
            big,
            pltpu.VMEM((4, PLANES, DEPTH), jnp.float32),
            pltpu.SemaphoreType.DMA((4, 2)),
            pltpu.SemaphoreType.DMA((8, 2)),
        ],
        compiler_params=ROOM,
        cost_estimate=pl.CostEstimate(flops=1 << 40, bytes_accessed=8 << 20, transcendentals=0),
        name="picture",
    )(source, along, in_hbm(first), in_hbm(second), *edges)


def rims_kernel(
    source, rim_x, rim_y, corner, strip, plane_strip, q3_plane, q3_rows, q2_plane, q2_rows,
    image_in, image, rims, along, fine, strip_out, plane_out, delta, sem,
):
    gx = lax.axis_index("gx")
    gy = lax.axis_index("gy")
    keep_x = jnp.where(gx < lax.axis_size("gx") - 1, 1.0, 0.0)
    keep_y = jnp.where(gy < lax.axis_size("gy") - 1, 1.0, 0.0)
    for n in range(2):
        rims[n * 40 : n * 40 + 16] = rim_x[n] * (0.5 * keep_x)
        rims[n * 40 + 16 : n * 40 + 32] = rim_y[n] * (0.5 * keep_y)
        rims[n * 40 + 32 : n * 40 + 40] = corner[n] * (0.5 * keep_x * keep_y)
    weights = interpolation()
    high, low = split_bf16(rims[...])
    along[...] = dot(high, weights) + dot(low, weights)
    row16 = lax.broadcasted_iota(jnp.int32, (16, DEPTH), 0)
    for n in range(2):
        for way in range(2):
            rows = along[n * 40 + way * 16 : n * 40 + way * 16 + 16, :]
            end = along[n * 40 + 32 : n * 40 + 33, :] if way == 0 else 0.0
            middle = 0.5 * (rows + jnp.where(row16 == 15, end, pltpu.roll(rows, 15, 0)))
            base = (n * 2 + way) * PLANES
            for part in range(4):
                lanes = slice(part * 128, part * 128 + 128)
                fine[part, pl.ds(base, 16, stride=2), :] = rows[:, lanes]
                fine[part, pl.ds(base + 1, 16, stride=2), :] = middle[:, lanes]
    index = lax.broadcasted_iota(jnp.int32, (PLANES, 128), 0)
    last_x = gx * PLANES + (PLANES - 1) - source[0, 0]
    last_y = gy * PLANES + (PLANES - 1) - source[0, 1]
    for part in range(4):
        lanes = slice(part * 128, part * 128 + 128)
        z = (lax.broadcasted_iota(jnp.int32, (PLANES, 128), 1) + part * 128 - source[0, 2]).astype(jnp.float32)
        for way in range(2):
            if way == 0:
                fixed = last_x
                moving = (index + gy * PLANES - source[0, 1]).astype(jnp.float32)
                pair = (q2_plane[0, :, lanes], q3_plane[:, lanes])
            else:
                fixed = last_y
                moving = (index + gx * PLANES - source[0, 0]).astype(jnp.float32)
                pair = (q2_rows[0, :, lanes], q3_rows[:, lanes])
            fixed = jnp.full((PLANES, 128), fixed, jnp.int32).astype(jnp.float32)
            distance = fixed * fixed + moving * moving + z * z
            taper = 1.0 - jnp.exp(distance * SCALE)
            total = None
            for n in range(2):
                base = (n * 2 + way) * PLANES
                term = fine[part, base : base + PLANES, :] * pair[n]
                total = term if total is None else total + term
            delta[way, :, lanes] = taper * total
    row8 = lax.broadcasted_iota(jnp.int32, (8, DEPTH), 0)
    for x in range(PLANES):
        value = strip[x] + jnp.where(row8 == 7, delta[1, x : x + 1, :], 0.0)
        if x == PLANES - 1:
            value = value + delta[0, 24:32, :]
        strip_out[x] = value
    plane_out[...] = plane_strip[...] + delta[0, 0:24, :]
    copies = [
        pltpu.make_async_copy(strip_out, image.at[:, 24:32], sem.at[0]),
        pltpu.make_async_copy(plane_out, image.at[PLANES - 1, 0:24], sem.at[1]),
    ]
    for copy in copies:
        copy.start()
    for copy in copies:
        copy.wait()


def add_rims(source, rims, strips, faces2, image):
    return pl.pallas_call(
        rims_kernel,
        in_specs=[SMEM] + [VMEM] * 9 + [ANY],
        out_specs=ANY,
        out_shape=pltpu.HBM((PLANES, PLANES, DEPTH), jnp.float32),
        input_output_aliases={10: 0},
        scratch_shapes=[
            pltpu.VMEM((80, COARSE), jnp.float32),
            pltpu.VMEM((80, DEPTH), jnp.float32),
            pltpu.VMEM((4, 4 * PLANES, 128), jnp.float32),
            pltpu.VMEM((PLANES, 8, DEPTH), jnp.float32),
            pltpu.VMEM((24, DEPTH), jnp.float32),
            pltpu.VMEM((2, PLANES, DEPTH), jnp.float32),
            pltpu.SemaphoreType.DMA((2,)),
        ],
        compiler_params=ROOM,
        cost_estimate=pl.CostEstimate(flops=1 << 20, bytes_accessed=2 << 20, transcendentals=0),
        name="add_rims",
    )(source, *rims, *strips, *faces2, in_hbm(image))


def per_device(
    stiffness,
    buoyancy,
    older_field,
    current_field,
    stored_tiles,
    tile_ids,
    tile_counts,
    receiver_cells,
    receiver_data,
    source_cell,
):
    older = older_field[0].reshape(ROWS, DEPTH)
    current = current_field[0].reshape(ROWS, DEPTH)
    stiff = stiffness.reshape(ROWS, DEPTH)
    buoy = buoyancy.reshape(ROWS, DEPTH)

    own = list(faces(current_field[0], buoyancy))
    far = exchange(own)
    tiles, own[0] = lax.optimization_barrier((stored_tiles, own[0]))
    received = lax.all_to_all(
        tiles[0, 0], ("shot", "gx"), split_axis=0, concat_axis=0, tiled=True
    ).reshape(1024, COARSE)
    numbers, counts, far = lax.optimization_barrier((tile_ids, tile_counts, far))
    slot = lax.broadcasted_iota(jnp.int32, (32, 32), 1)
    ids = jnp.where(slot < counts[0, 0][:, None], numbers[0, 0], -1).reshape(1, 1024)
    src = sources(receiver_cells[0], receiver_data[0])
    second, *rest = inner(current, older, buoy, stiff, src, [*own, *far], 0)
    own2, stiff_faces = rest[:4], rest[4:]
    far2 = exchange(own2)
    (third,) = inner(second, current, buoy, stiff, src, [], 1)

    received, third = lax.optimization_barrier((received, third))
    along, rim_x, rim_y, corner = coarse_tiles(received, ids)
    rims = [rotate(rim_x, "gx", -1), rotate(rim_y, "gy", -1), diagonal(corner)]
    edges = [*own, *far, *own2, *far2, *stiff_faces]
    image, last_current, *strips = picture(source_cell, along, second, third, edges)
    image = add_rims(source_cell, rims, strips, [own2[1], own2[3]], image)
    shape = current_field.shape
    return image.reshape(shape), second.reshape(shape), last_current.reshape(shape)


def exchange(own):
    x_lo, x_hi, y_lo, y_hi = own
    return [rotate(x_hi, "gx", 1), rotate(x_lo, "gx", -1), rotate(y_hi, "gy", 1), rotate(y_lo, "gy", -1)]


def diagonal(block):
    nx, ny = lax.axis_size("gx"), lax.axis_size("gy")
    route = [
        (i * ny + j, ((i - 1) % nx) * ny + (j - 1) % ny) for i in range(nx) for j in range(ny)
    ]
    return lax.ppermute(block, ("gx", "gy"), route)


def solution(mesh):
    in_specs = (
        P("gx", "gy", None),
        P("gx", "gy", None),
        P("shot", "gx", "gy", None),
        P("shot", "gx", "gy", None),
        P(("shot", "gx"), "gy", None, None, None),
        P(("shot", "gx"), "gy", None, None),
        P(("shot", "gx"), "gy", None),
        P("shot", None, None),
        P("shot", None, None),
        P("shot", None),
    )
    out_specs = (
        P("shot", "gx", "gy", None),
        P("shot", "gx", "gy", None),
        P("shot", "gx", "gy", None),
    )
    return jax.shard_map(
        per_device, mesh=mesh, in_specs=in_specs, out_specs=out_specs, check_vma=False
    )
```

```python
import jax
import jax.numpy as jnp
from jax import lax
from jax.experimental import pallas as pl
from jax.experimental.pallas import tpu as pltpu
from jax.sharding import PartitionSpec as P

MUTE_RADIUS = 3.0
PLANES = 32
ROWS = 1024
DEPTH = 512
COARSE = 256
CHUNKS = 4
PER = PLANES // CHUNKS
SPAN = ROWS // CHUNKS
VMEM = pl.BlockSpec(memory_space=pltpu.VMEM)
SMEM = pl.BlockSpec(memory_space=pltpu.SMEM)
ANY = pl.BlockSpec(memory_space=pl.ANY)
ROOM = pltpu.CompilerParams(vmem_limit_bytes=16 << 20)


def rotate(block, axis, step):
    count = lax.axis_size(axis)
    return lax.ppermute(block, axis, [(i, (i + step) % count) for i in range(count)])


def f32(*shape):
    return jax.ShapeDtypeStruct(shape, jnp.float32)


def split_bf16(x):
    high = x.astype(jnp.bfloat16)
    return high, (x - high.astype(jnp.float32)).astype(jnp.bfloat16)


def faces_kernel(fx_lo, fx_hi, fy_lo, fy_hi, bx_lo, bx_hi, by_lo, by_hi, sx_lo, sx_hi, sy_lo, sy_hi):
    for slot, refs in enumerate(((fx_lo, fx_hi, fy_lo, fy_hi), (bx_lo, bx_hi, by_lo, by_hi))):
        sx_lo[slot] = refs[0][0]
        sx_hi[slot] = refs[1][0]
        for x in range(PLANES):
            sy_lo[slot, x : x + 1, :] = refs[2][x, 0:1, :]
            sy_hi[slot, x : x + 1, :] = refs[3][x, 7:8, :]


def faces(field, buoyancy):
    plane_lo = pl.BlockSpec((1, PLANES, DEPTH), lambda i: (0, 0, 0))
    plane_hi = pl.BlockSpec((1, PLANES, DEPTH), lambda i: (PLANES - 1, 0, 0))
    rows_lo = pl.BlockSpec((PLANES, 8, DEPTH), lambda i: (0, 0, 0))
    rows_hi = pl.BlockSpec((PLANES, 8, DEPTH), lambda i: (0, PLANES // 8 - 1, 0))
    out = pl.BlockSpec((2, PLANES, DEPTH), lambda i: (0, 0, 0))
    return pl.pallas_call(
        faces_kernel,
        grid=(1,),
        in_specs=[plane_lo, plane_hi, rows_lo, rows_hi] * 2,
        out_specs=[out] * 4,
        out_shape=[f32(2, PLANES, DEPTH)] * 4,
        compiler_params=ROOM,
        cost_estimate=pl.CostEstimate(flops=0, bytes_accessed=3 << 20, transcendentals=0),
        name="faces",
    )(*([in_hbm(field)] * 4 + [in_hbm(buoyancy)] * 4))


def sources_kernel(cells, data, out):
    base_x = lax.axis_index("gx") * PLANES
    base_y = lax.axis_index("gy") * PLANES
    local_x = cells[0:1, :] - base_x
    local_y = cells[1:2, :] - base_y
    inside = (local_x >= 0) & (local_x < PLANES) & (local_y >= 0) & (local_y < PLANES)
    row = jnp.where(inside, local_x * PLANES + local_y, -1)
    depth_id = lax.broadcasted_iota(jnp.int32, (8, 1024), 0)
    here = depth_id == cells[2:3, :]
    parts = []
    for step in range(2):
        value = jnp.where(here, data[step : step + 1, :], 0.0)
        parts.append(split_bf16(value))
    table = jnp.concatenate([parts[0][0], parts[0][1], parts[1][0], parts[1][1]], axis=0)
    lane = lax.broadcasted_iota(jnp.int32, (128, 128), 1)
    pad = jnp.zeros((96, 1024), jnp.bfloat16)
    table = jnp.concatenate([table, pad], axis=0)
    for start in range(0, ROWS, 128):
        ids = lax.broadcasted_iota(jnp.int32, (128, 1024), 0) + start
        select = jnp.where(ids == row, 1.0, 0.0).astype(jnp.bfloat16)
        product = lax.dot_general(
            select, table, (((1,), (1,)), ((), ())), preferred_element_type=jnp.float32
        )
        for step in range(2):
            high = pltpu.roll(product, (128 - 16 * step) % 128, 1)
            low = pltpu.roll(product, 128 - 16 * step - 8, 1)
            out[step, start : start + 128, :] = jnp.where(lane < 8, high + low, 0.0)


def sources(cells, data):
    return pl.pallas_call(
        sources_kernel,
        in_specs=[VMEM, VMEM],
        out_specs=VMEM,
        out_shape=f32(2, ROWS, 128),
        cost_estimate=pl.CostEstimate(flops=1, bytes_accessed=1, transcendentals=0),
        compiler_params=ROOM,
        name="sources",
    )(cells, data)


def in_hbm(x):
    return pltpu.with_memory_space_constraint(x, pltpu.HBM)


def edge_fluxes(own_b, far_b, own_f, far_f):
    gx = lax.axis_index("gx")
    gy = lax.axis_index("gy")
    keep = [
        jnp.where(gx > 0, 1.0, 0.0),
        jnp.where(gx < lax.axis_size("gx") - 1, 1.0, 0.0),
        jnp.where(gy > 0, 1.0, 0.0),
        jnp.where(gy < lax.axis_size("gy") - 1, 1.0, 0.0),
    ]
    return [
        (own_b[side][1] + keep[side] * far_b[side][1])
        * (keep[side] * far_f[side][0] - own_f[side][0])
        for side in range(4)
    ]


def inner_kernel(field, older, buoy, stiff, src, *rest, step):
    if step == 0:
        own, far, rest = rest[:4], rest[4:8], rest[8:]
        out, faces_out, stiff_out = rest[0], rest[1:5], rest[5:9]
        f_buf, b_buf, s_buf, o_buf, n_buf, edges, in_sem, out_sem = rest[9:]
    else:
        out, f_buf, b_buf, s_buf, o_buf, n_buf, in_sem, out_sem = rest
    copies = []
    for chunk in range(CHUNKS):
        part = pl.ds(chunk * SPAN, SPAN)
        pairs = ((field, f_buf), (buoy, b_buf), (stiff, s_buf), (older, o_buf))
        group = [
            pltpu.make_async_copy(hbm.at[part], buf.at[part], in_sem.at[chunk, k])
            for k, (hbm, buf) in enumerate(pairs)
        ]
        for copy in group:
            copy.start()
        copies.append(group)
    row8 = lax.broadcasted_iota(jnp.int32, (8, DEPTH), 0)
    lane128 = lax.broadcasted_iota(jnp.int32, (PLANES, 128), 1)
    out_copies = []

    if step == 0:
        for side, flux in enumerate(edge_fluxes(own, far, own, far)):
            edges[side] = flux

    def arrive(chunk):
        for copy in copies[chunk][:2]:
            copy.wait()

    def plane(x, flux_before, last=False):
        base = pl.multiple_of(x * PLANES, PLANES)
        at = pl.ds(base, PLANES)
        c = f_buf[at, :]
        b = b_buf[at, :]
        if last:
            flux_x = edges[1] if step == 0 else jnp.zeros_like(c)
        else:
            nearby = pl.ds(base + PLANES, PLANES)
            flux_x = (b + b_buf[nearby, :]) * (f_buf[nearby, :] - c)
        flux_y = (b + pltpu.roll(b, PLANES - 1, 0)) * (pltpu.roll(c, PLANES - 1, 0) - c)
        flux_y = jnp.concatenate(
            [flux_y[0:24], jnp.where(row8 == 7, 0.0, flux_y[24:32])], axis=0
        )
        flux_z = (b + pltpu.roll(b, DEPTH - 1, 1)) * (pltpu.roll(c, DEPTH - 1, 1) - c)
        flux_z = jnp.concatenate(
            [flux_z[:, : DEPTH - 128], jnp.where(lane128 == 127, 0.0, flux_z[:, DEPTH - 128 :])],
            axis=1,
        )
        total = (flux_x - flux_before) + (flux_y - pltpu.roll(flux_y, 1, 0))
        total = total + (flux_z - pltpu.roll(flux_z, 1, 1))
        if step == 0:
            total = jnp.concatenate(
                [
                    total[0:8] + jnp.where(row8 == 0, edges[2, pl.ds(x, 1), :], 0.0),
                    total[8:24],
                    total[24:32] + jnp.where(row8 == 7, edges[3, pl.ds(x, 1), :], 0.0),
                ],
                axis=0,
            )
        head = slice(0, 128)
        tail = slice(DEPTH - 128, DEPTH)
        total = jnp.concatenate(
            [
                total[:, head] - jnp.where(lane128 == 0, b[:, head] * c[:, head], 0.0),
                total[:, 128 : DEPTH - 128],
                total[:, tail] - jnp.where(lane128 == 127, b[:, tail] * c[:, tail], 0.0),
            ],
            axis=1,
        )
        value = (2.0 * c - o_buf[at, :]) + (0.5 * s_buf[at, :]) * total
        n_buf[at, 128:DEPTH] = value[:, 128:]
        n_buf[at, head] = value[:, head] + src[step, at, :]
        if step == 0:
            faces_out[2][0, pl.ds(x, 1), :] = n_buf[pl.ds(base, 1), :]
            faces_out[3][0, pl.ds(x, 1), :] = n_buf[pl.ds(base + PLANES - 1, 1), :]
            stiff_out[2][pl.ds(x, 1), :] = s_buf[pl.ds(base, 1), :]
            stiff_out[3][pl.ds(x, 1), :] = s_buf[pl.ds(base + PLANES - 1, 1), :]
        return flux_x

    arrive(0)
    flux = -edges[0] if step == 0 else jnp.zeros((PLANES, DEPTH), jnp.float32)
    for chunk in range(CHUNKS):
        for copy in copies[chunk][2:]:
            copy.wait()
        if chunk + 1 < CHUNKS:
            arrive(chunk + 1)
            flux = lax.fori_loop(chunk * PER, chunk * PER + PER, plane, flux, unroll=4)
        else:
            flux = lax.fori_loop(chunk * PER, chunk * PER + PER - 4, plane, flux, unroll=4)
            for x in range(PLANES - 4, PLANES):
                flux = plane(x, flux, x == PLANES - 1)
        part = pl.ds(chunk * SPAN, SPAN)
        copy = pltpu.make_async_copy(n_buf.at[part], out.at[part], out_sem.at[chunk])
        copy.start()
        out_copies.append(copy)
    if step == 0:
        faces_out[0][0] = n_buf[0:PLANES, :]
        faces_out[1][0] = n_buf[ROWS - PLANES : ROWS, :]
        stiff_out[0][...] = s_buf[0:PLANES, :]
        stiff_out[1][...] = s_buf[ROWS - PLANES : ROWS, :]
    for copy in out_copies:
        copy.wait()


def inner(field, older, buoy, stiff, src, halos, step):
    big = pltpu.VMEM((ROWS, DEPTH), jnp.float32)
    scratch = [big] * 5
    sems = [pltpu.SemaphoreType.DMA((CHUNKS, 4)), pltpu.SemaphoreType.DMA((CHUNKS,))]
    out_shape = [pltpu.HBM((ROWS, DEPTH), jnp.float32)]
    out_specs = [ANY]
    if step == 0:
        out_shape += [f32(1, PLANES, DEPTH)] * 4 + [f32(PLANES, DEPTH)] * 4
        out_specs += [VMEM] * 8
        scratch = scratch + [pltpu.VMEM((4, PLANES, DEPTH), jnp.float32)]
    return pl.pallas_call(
        lambda *refs: inner_kernel(*refs, step=step),
        in_specs=[ANY] * 4 + [VMEM] * (1 + len(halos)),
        out_specs=out_specs,
        out_shape=out_shape,
        scratch_shapes=scratch + sems,
        compiler_params=ROOM,
        cost_estimate=pl.CostEstimate(flops=(1 << 40) >> (6 * step), bytes_accessed=1, transcendentals=0),
        name="inner%d" % step,
    )(in_hbm(field), in_hbm(older), in_hbm(buoy), in_hbm(stiff), src, *halos)


def interpolation():
    fine = lax.broadcasted_iota(jnp.int32, (COARSE, DEPTH), 1)
    coarse = lax.broadcasted_iota(jnp.int32, (COARSE, DEPTH), 0)
    gap = jnp.abs(fine - 2 * coarse).astype(jnp.float32)
    return jnp.maximum(1.0 - 0.5 * gap, 0.0).astype(jnp.bfloat16)


def dot(a, b):
    return jnp.dot(a, b, preferred_element_type=jnp.float32)


def rim_rows_kernel(received, ids, rim_x, rim_y, corner, tiles, sem):
    copies = []
    for part in range(4):
        at = pl.ds(part * 256, 256)
        copies.append(pltpu.make_async_copy(received.at[at], tiles.at[at], sem.at[part]))
        copies[-1].start()
    row = lax.broadcasted_iota(jnp.int32, (16, 1024), 0)
    wanted = jnp.concatenate([row, row * 16, row + 256, row * 16 + 256], axis=0)
    select = jnp.where(wanted == ids[...], 1.0, 0.0).astype(jnp.bfloat16)
    total = jnp.zeros((64, COARSE), jnp.float32)
    for part in range(4):
        at = slice(part * 256, part * 256 + 256)
        copies[part].wait()
        high, low = split_bf16(tiles[at, :])
        total = total + (dot(select[:, at], high) + dot(select[:, at], low))
    for n in range(2):
        rim_x[n] = total[n * 32 : n * 32 + 16]
        rim_y[n] = total[n * 32 + 16 : n * 32 + 32]
        corner[n] = total[n * 32 : n * 32 + 8]


def rim_rows(received, ids):
    return pl.pallas_call(
        rim_rows_kernel,
        in_specs=[ANY, VMEM],
        out_specs=[VMEM] * 3,
        out_shape=[f32(2, 16, COARSE), f32(2, 16, COARSE), f32(2, 8, COARSE)],
        scratch_shapes=[pltpu.VMEM((1024, COARSE), jnp.float32), pltpu.SemaphoreType.DMA((4,))],
        compiler_params=ROOM,
        cost_estimate=pl.CostEstimate(flops=1 << 30, bytes_accessed=3 << 20, transcendentals=0),
        name="rim_rows",
    )(in_hbm(received), ids)


SCALE = -1.0 / (2.0 * MUTE_RADIUS * MUTE_RADIUS)


def picture_kernel(source, received, ids, first_hbm, second_hbm, *rest):
    own, far, own2, far2, stiff = (rest[4 * k : 4 * k + 4] for k in range(5))
    image, saved, strip, plane_strip, factors = rest[20:25]
    fine, out, first, third, terms, tiles, onehot, along, tile_sem, in_sem, sem = rest[25:]
    tile_copies = []
    for part in range(4):
        at = pl.ds(part * 256, 256)
        tile_copies.append(pltpu.make_async_copy(received.at[at], tiles.at[at], tile_sem.at[part]))
        tile_copies[-1].start()
    loads = []
    for k in range(4):
        at = pl.ds(k * SPAN, SPAN)
        pair = [
            pltpu.make_async_copy(first_hbm.at[at], first.at[at], in_sem.at[k, 0]),
            pltpu.make_async_copy(second_hbm.at[at], third.at[at], in_sem.at[k, 1]),
        ]
        for copy in pair:
            copy.start()
        loads.append(pair)
    for side, flux in enumerate(edge_fluxes(own, far, own2, far2)):
        terms[side] = (0.5 * stiff[side][...]) * flux
    for start in range(0, 512, 128):
        tile = lax.broadcasted_iota(jnp.int32, (128, 1024), 0) + start
        onehot[start : start + 128, :] = jnp.where(tile == ids[...], 1.0, 0.0).astype(jnp.bfloat16)
    for copy in tile_copies:
        copy.wait()
    weights = interpolation()
    high, low = split_bf16(tiles[...])
    c_high = dot(onehot[...], high).astype(jnp.bfloat16)
    c_low = dot(onehot[...], low).astype(jnp.bfloat16)
    along[...] = dot(c_high, weights) + dot(c_low, weights)
    row16 = lax.broadcasted_iota(jnp.int32, (16, DEPTH), 0)
    for n in range(2):
        for k in range(16):
            rows = along[n * 256 + k * 16 : n * 256 + k * 16 + 16, :]
            middle = 0.5 * (rows + jnp.where(row16 == 15, 0.0, pltpu.roll(rows, 15, 0)))
            base = (n * 17 + k) * PLANES
            for part in range(4):
                lanes = slice(part * 128, part * 128 + 128)
                fine[part, pl.ds(base, 16, stride=2), :] = rows[:, lanes]
                fine[part, pl.ds(base + 1, 16, stride=2), :] = middle[:, lanes]
        for part in range(4):
            base = (n * 17 + 16) * PLANES
            fine[part, base : base + PLANES, :] = jnp.zeros((PLANES, 128), jnp.float32)
    gx = lax.axis_index("gx")
    gy = lax.axis_index("gy")
    y = (lax.broadcasted_iota(jnp.int32, (PLANES, DEPTH), 0) + gy * PLANES - source[0, 1]).astype(jnp.float32)
    z = (lax.broadcasted_iota(jnp.int32, (PLANES, DEPTH), 1) - source[0, 2]).astype(jnp.float32)
    decay_yz = jnp.exp((y * y + z * z) * SCALE)
    x_base = gx * PLANES - source[0, 0]
    copies = []
    for x in range(PLANES):
        k = x // 2
        if x % PER == 0:
            for copy in loads[x // PER]:
                copy.wait()
        at = slice(x * PLANES, (x + 1) * PLANES)
        if x == 0:
            third[at, :] += terms[0]
        if x == PLANES - 1:
            third[at, :] += terms[1]
        third[x * PLANES : x * PLANES + 1, :] += terms[2, x : x + 1, :]
        third[x * PLANES + 31 : x * PLANES + 32, :] += terms[3, x : x + 1, :]
        factors[1, 1, x : x + 1, :] = third[x * PLANES + 31 : x * PLANES + 32, :]
        dx = jnp.full((1, 128), x_base + x, jnp.int32).astype(jnp.float32)
        decay = jnp.exp((dx * dx) * SCALE)
        for part in range(4):
            lanes = slice(part * 128, part * 128 + 128)
            taper = 1.0 - decay * decay_yz[:, lanes]
            snaps = []
            for n in range(2):
                start = (n * 17 + k) * PLANES
                snap = fine[part, start : start + PLANES, :]
                if x % 2:
                    snap = 0.5 * (snap + fine[part, start + PLANES : start + 2 * PLANES, :])
                snaps.append(snap)
            value = taper * (snaps[0] * first[at, lanes] + snaps[1] * third[at, lanes])
            out[x, :, lanes] = value
            strip[x, :, lanes] = value[24:32]
        if x % 4 == 3:
            group = pl.ds(x - 3, 3 if x == PLANES - 1 else 4)
            rows = pl.ds((x - 3) * PLANES, 4 * PLANES)
            copies.append(
                pltpu.make_async_copy(
                    out.at[group, 0:24], image.at[group, 0:24], sem.at[x // 4, 0]
                )
            )
            copies.append(pltpu.make_async_copy(third.at[rows], saved.at[rows], sem.at[x // 4, 1]))
            for copy in copies[-2:]:
                copy.start()
    plane_strip[...] = out[PLANES - 1, 0:24, :]
    last_x = jnp.full((PLANES, DEPTH), x_base + PLANES - 1, jnp.int32).astype(jnp.float32)
    last_y = jnp.full((PLANES, DEPTH), gy * PLANES + 31 - source[0, 1], jnp.int32).astype(jnp.float32)
    x = (lax.broadcasted_iota(jnp.int32, (PLANES, DEPTH), 0) + x_base).astype(jnp.float32)
    for way, (a, b) in enumerate(((last_x, y), (x, last_y))):
        taper = 1.0 - jnp.exp((a * a + b * b + z * z) * SCALE)
        newest = third[ROWS - PLANES : ROWS, :] if way == 0 else factors[1, 1]
        factors[way, 1] = taper * newest
        factors[way, 0] = taper * own2[1 + 2 * way][0]
    for copy in copies:
        copy.wait()


def picture(source, received, ids, first, second, edges):
    big = pltpu.VMEM((ROWS, DEPTH), jnp.float32)
    return pl.pallas_call(
        picture_kernel,
        in_specs=[SMEM, ANY, VMEM, ANY, ANY] + [VMEM] * 20,
        out_specs=[ANY, ANY] + [VMEM] * 3,
        out_shape=[
            pltpu.HBM((PLANES, PLANES, DEPTH), jnp.float32),
            pltpu.HBM((ROWS, DEPTH), jnp.float32),
            f32(PLANES, 8, DEPTH),
            f32(24, DEPTH),
            f32(2, 2, PLANES, DEPTH),
        ],
        scratch_shapes=[
            pltpu.VMEM((4, 2 * 17 * PLANES, 128), jnp.float32),
            pltpu.VMEM((PLANES, PLANES, DEPTH), jnp.float32),
            big,
            big,
            pltpu.VMEM((4, PLANES, DEPTH), jnp.float32),
            pltpu.VMEM((1024, COARSE), jnp.float32),
            pltpu.VMEM((512, 1024), jnp.bfloat16),
            pltpu.VMEM((512, DEPTH), jnp.float32),
            pltpu.SemaphoreType.DMA((4,)),
            pltpu.SemaphoreType.DMA((4, 2)),
            pltpu.SemaphoreType.DMA((8, 2)),
        ],
        compiler_params=ROOM,
        cost_estimate=pl.CostEstimate(flops=1 << 40, bytes_accessed=8 << 20, transcendentals=0),
        name="picture",
    )(source, in_hbm(received), ids, in_hbm(first), in_hbm(second), *edges)


def rims_kernel(
    rim_x_hbm, rim_y_hbm, corner_hbm, strip, plane_strip, factors,
    image_in, image, rim_x, rim_y, corner, rims, along, fine, strip_out, plane_out, delta, sem,
):
    pairs = ((rim_x_hbm, rim_x), (rim_y_hbm, rim_y), (corner_hbm, corner))
    loads = [pltpu.make_async_copy(a, b, sem.at[2 + k]) for k, (a, b) in enumerate(pairs)]
    for copy in loads:
        copy.start()
    weights = interpolation()
    gx = lax.axis_index("gx")
    gy = lax.axis_index("gy")
    keep_x = jnp.where(gx < lax.axis_size("gx") - 1, 1.0, 0.0)
    keep_y = jnp.where(gy < lax.axis_size("gy") - 1, 1.0, 0.0)
    for copy in loads:
        copy.wait()
    for n in range(2):
        rims[n * 40 : n * 40 + 16] = rim_x[n] * (0.5 * keep_x)
        rims[n * 40 + 16 : n * 40 + 32] = rim_y[n] * (0.5 * keep_y)
        rims[n * 40 + 32 : n * 40 + 40] = corner[n] * (0.5 * keep_x * keep_y)
    high, low = split_bf16(rims[...])
    along[...] = dot(high, weights) + dot(low, weights)
    row16 = lax.broadcasted_iota(jnp.int32, (16, DEPTH), 0)
    for n in range(2):
        for way in range(2):
            rows = along[n * 40 + way * 16 : n * 40 + way * 16 + 16, :]
            end = along[n * 40 + 32 : n * 40 + 33, :] if way == 0 else 0.0
            middle = 0.5 * (rows + jnp.where(row16 == 15, end, pltpu.roll(rows, 15, 0)))
            base = (n * 2 + way) * PLANES
            for part in range(4):
                lanes = slice(part * 128, part * 128 + 128)
                fine[part, pl.ds(base, 16, stride=2), :] = rows[:, lanes]
                fine[part, pl.ds(base + 1, 16, stride=2), :] = middle[:, lanes]
    for part in range(4):
        lanes = slice(part * 128, part * 128 + 128)
        for way in range(2):
            delta[way, :, lanes] = (
                fine[part, way * PLANES : (way + 1) * PLANES, :] * factors[way, 0, :, lanes]
                + fine[part, (2 + way) * PLANES : (3 + way) * PLANES, :] * factors[way, 1, :, lanes]
            )
    row8 = lax.broadcasted_iota(jnp.int32, (8, DEPTH), 0)
    for x in range(PLANES):
        value = strip[x] + jnp.where(row8 == 7, delta[1, x : x + 1, :], 0.0)
        if x == PLANES - 1:
            value = value + delta[0, 24:32, :]
        strip_out[x] = value
    plane_out[...] = plane_strip[...] + delta[0, 0:24, :]
    copies = [
        pltpu.make_async_copy(strip_out, image.at[:, 24:32], sem.at[0]),
        pltpu.make_async_copy(plane_out, image.at[PLANES - 1, 0:24], sem.at[1]),
    ]
    for copy in copies:
        copy.start()
    for copy in copies:
        copy.wait()


def add_rims(rims, strips, image):
    return pl.pallas_call(
        rims_kernel,
        in_specs=[ANY] * 3 + [VMEM] * 3 + [ANY],
        out_specs=ANY,
        out_shape=pltpu.HBM((PLANES, PLANES, DEPTH), jnp.float32),
        input_output_aliases={6: 0},
        scratch_shapes=[
            pltpu.VMEM((2, 16, COARSE), jnp.float32),
            pltpu.VMEM((2, 16, COARSE), jnp.float32),
            pltpu.VMEM((2, 8, COARSE), jnp.float32),
            pltpu.VMEM((80, COARSE), jnp.float32),
            pltpu.VMEM((80, DEPTH), jnp.float32),
            pltpu.VMEM((4, 4 * PLANES, 128), jnp.float32),
            pltpu.VMEM((PLANES, 8, DEPTH), jnp.float32),
            pltpu.VMEM((24, DEPTH), jnp.float32),
            pltpu.VMEM((2, PLANES, DEPTH), jnp.float32),
            pltpu.SemaphoreType.DMA((5,)),
        ],
        compiler_params=ROOM,
        cost_estimate=pl.CostEstimate(flops=1 << 20, bytes_accessed=2 << 20, transcendentals=0),
        name="add_rims",
    )(*rims, *strips, in_hbm(image))


def per_device(
    stiffness,
    buoyancy,
    older_field,
    current_field,
    stored_tiles,
    tile_ids,
    tile_counts,
    receiver_cells,
    receiver_data,
    source_cell,
):
    older = older_field[0].reshape(ROWS, DEPTH)
    current = current_field[0].reshape(ROWS, DEPTH)
    stiff = stiffness.reshape(ROWS, DEPTH)
    buoy = buoyancy.reshape(ROWS, DEPTH)

    own = list(faces(current_field[0], buoyancy))
    far = exchange(own)
    tiles, own[0] = lax.optimization_barrier((stored_tiles, own[0]))
    received = lax.all_to_all(
        tiles[0, 0], ("shot", "gx"), split_axis=0, concat_axis=0, tiled=True
    ).reshape(1024, COARSE)
    numbers, counts, far[0], far[1] = lax.optimization_barrier((tile_ids, tile_counts, far[0], far[1]))
    slot = lax.broadcasted_iota(jnp.int32, (32, 32), 1)
    ids = jnp.where(slot < counts[0, 0][:, None], numbers[0, 0], -1).reshape(1, 1024)
    src = sources(receiver_cells[0], receiver_data[0])
    second, *rest = inner(current, older, buoy, stiff, src, [*own, *far], 0)
    own2, stiff_faces = rest[:4], rest[4:]
    far2 = exchange(own2)
    (third,) = inner(second, current, buoy, stiff, src, [], 1)

    received, third = lax.optimization_barrier((received, third))
    rim_x, rim_y, corner = rim_rows(received, ids)
    rims = [rotate(rim_x, "gx", -1), rotate(rim_y, "gy", -1), diagonal(corner)]
    edges = [*own, *far, *own2, *far2, *stiff_faces]
    image, last_current, *strips = picture(source_cell, received, ids, second, third, edges)
    image = add_rims(rims, strips, image)
    shape = current_field.shape
    return image.reshape(shape), second.reshape(shape), last_current.reshape(shape)


def exchange(own):
    x_lo, x_hi, y_lo, y_hi = own
    return [rotate(x_hi, "gx", 1), rotate(x_lo, "gx", -1), rotate(y_hi, "gy", 1), rotate(y_lo, "gy", -1)]


def diagonal(block):
    nx, ny = lax.axis_size("gx"), lax.axis_size("gy")
    route = [
        (i * ny + j, ((i - 1) % nx) * ny + (j - 1) % ny) for i in range(nx) for j in range(ny)
    ]
    return lax.ppermute(block, ("gx", "gy"), route)


def solution(mesh):
    in_specs = (
        P("gx", "gy", None),
        P("gx", "gy", None),
        P("shot", "gx", "gy", None),
        P("shot", "gx", "gy", None),
        P(("shot", "gx"), "gy", None, None, None),
        P(("shot", "gx"), "gy", None, None),
        P(("shot", "gx"), "gy", None),
        P("shot", None, None),
        P("shot", None, None),
        P("shot", None),
    )
    out_specs = (
        P("shot", "gx", "gy", None),
        P("shot", "gx", "gy", None),
        P("shot", "gx", "gy", None),
    )
    return jax.shard_map(
        per_device, mesh=mesh, in_specs=in_specs, out_specs=out_specs, check_vma=False
    )
```

```python
import jax
import jax.numpy as jnp
from jax import lax
from jax.experimental import pallas as pl
from jax.experimental.pallas import tpu as pltpu
from jax.sharding import PartitionSpec as P

MUTE_RADIUS = 3.0
PLANES = 32
ROWS = 1024
DEPTH = 512
COARSE = 256
CHUNKS = 4
PER = PLANES // CHUNKS
SPAN = ROWS // CHUNKS
VMEM = pl.BlockSpec(memory_space=pltpu.VMEM)
SMEM = pl.BlockSpec(memory_space=pltpu.SMEM)
ANY = pl.BlockSpec(memory_space=pl.ANY)
ROOM = pltpu.CompilerParams(vmem_limit_bytes=16 << 20)


def swap(block, axis, start):
    count = lax.axis_size(axis)
    route = []
    for low in range(start, count - 1, 2):
        route += [(low, low + 1), (low + 1, low)]
    return lax.ppermute(block, axis, route)


def parity(axis):
    return lax.rem(lax.axis_index(axis), 2)


def by_side(messages):
    values = []
    for axis, pair in (("gx", messages[:2]), ("gy", messages[2:])):
        odd = parity(axis) == 1
        values += [jnp.where(odd, pair[0], pair[1]), jnp.where(odd, pair[1], pair[0])]
    return values


def f32(*shape):
    return jax.ShapeDtypeStruct(shape, jnp.float32)


def split_bf16(x):
    high = x.astype(jnp.bfloat16)
    return high, (x - high.astype(jnp.float32)).astype(jnp.bfloat16)


def faces_kernel(fx_lo, fx_hi, fy_lo, fy_hi, bx_lo, bx_hi, by_lo, by_hi, x_first, x_next, y_first, y_next):
    odd_x = parity("gx") == 1
    odd_y = parity("gy") == 1
    for slot, refs in enumerate(((fx_lo, fx_hi, fy_lo, fy_hi), (bx_lo, bx_hi, by_lo, by_hi))):
        low, high = refs[0][0], refs[1][0]
        x_first[slot] = jnp.where(odd_x, low, high)
        x_next[slot] = jnp.where(odd_x, high, low)
        for x in range(PLANES):
            low, high = refs[2][x, 0:1, :], refs[3][x, 7:8, :]
            y_first[slot, x : x + 1, :] = jnp.where(odd_y, low, high)
            y_next[slot, x : x + 1, :] = jnp.where(odd_y, high, low)


def faces(field, buoyancy):
    plane_lo = pl.BlockSpec((1, PLANES, DEPTH), lambda i: (0, 0, 0))
    plane_hi = pl.BlockSpec((1, PLANES, DEPTH), lambda i: (PLANES - 1, 0, 0))
    rows_lo = pl.BlockSpec((PLANES, 8, DEPTH), lambda i: (0, 0, 0))
    rows_hi = pl.BlockSpec((PLANES, 8, DEPTH), lambda i: (0, PLANES // 8 - 1, 0))
    out = pl.BlockSpec((2, PLANES, DEPTH), lambda i: (0, 0, 0))
    return pl.pallas_call(
        faces_kernel,
        grid=(1,),
        in_specs=[plane_lo, plane_hi, rows_lo, rows_hi] * 2,
        out_specs=[out] * 4,
        out_shape=[f32(2, PLANES, DEPTH)] * 4,
        compiler_params=ROOM,
        cost_estimate=pl.CostEstimate(flops=0, bytes_accessed=3 << 20, transcendentals=0),
        name="faces",
    )(*([in_hbm(field)] * 4 + [in_hbm(buoyancy)] * 4))


def sources_kernel(cells, data, out):
    base_x = lax.axis_index("gx") * PLANES
    base_y = lax.axis_index("gy") * PLANES
    local_x = cells[0:1, :] - base_x
    local_y = cells[1:2, :] - base_y
    inside = (local_x >= 0) & (local_x < PLANES) & (local_y >= 0) & (local_y < PLANES)
    row = jnp.where(inside, local_x * PLANES + local_y, -1)
    depth_id = lax.broadcasted_iota(jnp.int32, (8, 1024), 0)
    here = depth_id == cells[2:3, :]
    parts = []
    for step in range(2):
        value = jnp.where(here, data[step : step + 1, :], 0.0)
        parts.append(split_bf16(value))
    table = jnp.concatenate([parts[0][0], parts[0][1], parts[1][0], parts[1][1]], axis=0)
    lane = lax.broadcasted_iota(jnp.int32, (128, 128), 1)
    pad = jnp.zeros((96, 1024), jnp.bfloat16)
    table = jnp.concatenate([table, pad], axis=0)
    for start in range(0, ROWS, 128):
        ids = lax.broadcasted_iota(jnp.int32, (128, 1024), 0) + start
        select = jnp.where(ids == row, 1.0, 0.0).astype(jnp.bfloat16)
        product = lax.dot_general(
            select, table, (((1,), (1,)), ((), ())), preferred_element_type=jnp.float32
        )
        for step in range(2):
            high = pltpu.roll(product, (128 - 16 * step) % 128, 1)
            low = pltpu.roll(product, 128 - 16 * step - 8, 1)
            out[step, start : start + 128, :] = jnp.where(lane < 8, high + low, 0.0)


def sources(cells, data):
    return pl.pallas_call(
        sources_kernel,
        in_specs=[VMEM, VMEM],
        out_specs=VMEM,
        out_shape=f32(2, ROWS, 128),
        cost_estimate=pl.CostEstimate(flops=1, bytes_accessed=1, transcendentals=0),
        compiler_params=ROOM,
        name="sources",
    )(cells, data)


def in_hbm(x):
    return pltpu.with_memory_space_constraint(x, pltpu.HBM)


def edge_fluxes(own_b, far_b, own_f, far_f):
    gx = lax.axis_index("gx")
    gy = lax.axis_index("gy")
    keep = [
        jnp.where(gx > 0, 1.0, 0.0),
        jnp.where(gx < lax.axis_size("gx") - 1, 1.0, 0.0),
        jnp.where(gy > 0, 1.0, 0.0),
        jnp.where(gy < lax.axis_size("gy") - 1, 1.0, 0.0),
    ]
    return [
        (own_b[side] + keep[side] * far_b[side])
        * (keep[side] * far_f[side] - own_f[side])
        for side in range(4)
    ]


def inner_kernel(field, older, buoy, stiff, src, *rest, step):
    if step == 0:
        own, far, rest = rest[:4], rest[4:8], rest[8:]
        out, faces_out, stiff_out = rest[0], rest[1:5], rest[5:9]
        f_buf, b_buf, s_buf, o_buf, n_buf, edges, in_sem, out_sem = rest[9:]
    else:
        out, f_buf, b_buf, s_buf, o_buf, n_buf, in_sem, out_sem = rest
    copies = []
    for chunk in range(CHUNKS):
        part = pl.ds(chunk * SPAN, SPAN)
        pairs = ((field, f_buf), (buoy, b_buf), (stiff, s_buf), (older, o_buf))
        group = [
            pltpu.make_async_copy(hbm.at[part], buf.at[part], in_sem.at[chunk, k])
            for k, (hbm, buf) in enumerate(pairs)
        ]
        for copy in group:
            copy.start()
        copies.append(group)
    row8 = lax.broadcasted_iota(jnp.int32, (8, DEPTH), 0)
    lane128 = lax.broadcasted_iota(jnp.int32, (PLANES, 128), 1)
    out_copies = []

    if step == 0:
        near_b, away_b = by_side([m[1] for m in own]), by_side([m[1] for m in far])
        near_f, away_f = by_side([m[0] for m in own]), by_side([m[0] for m in far])
        for side, flux in enumerate(edge_fluxes(near_b, away_b, near_f, away_f)):
            edges[side] = flux

    def arrive(chunk):
        for copy in copies[chunk][:2]:
            copy.wait()

    def plane(x, flux_before, last=False):
        base = pl.multiple_of(x * PLANES, PLANES)
        at = pl.ds(base, PLANES)
        c = f_buf[at, :]
        b = b_buf[at, :]
        if last:
            flux_x = edges[1] if step == 0 else jnp.zeros_like(c)
        else:
            nearby = pl.ds(base + PLANES, PLANES)
            flux_x = (b + b_buf[nearby, :]) * (f_buf[nearby, :] - c)
        flux_y = (b + pltpu.roll(b, PLANES - 1, 0)) * (pltpu.roll(c, PLANES - 1, 0) - c)
        flux_y = jnp.concatenate(
            [flux_y[0:24], jnp.where(row8 == 7, 0.0, flux_y[24:32])], axis=0
        )
        flux_z = (b + pltpu.roll(b, DEPTH - 1, 1)) * (pltpu.roll(c, DEPTH - 1, 1) - c)
        flux_z = jnp.concatenate(
            [flux_z[:, : DEPTH - 128], jnp.where(lane128 == 127, 0.0, flux_z[:, DEPTH - 128 :])],
            axis=1,
        )
        total = (flux_x - flux_before) + (flux_y - pltpu.roll(flux_y, 1, 0))
        total = total + (flux_z - pltpu.roll(flux_z, 1, 1))
        if step == 0:
            total = jnp.concatenate(
                [
                    total[0:8] + jnp.where(row8 == 0, edges[2, pl.ds(x, 1), :], 0.0),
                    total[8:24],
                    total[24:32] + jnp.where(row8 == 7, edges[3, pl.ds(x, 1), :], 0.0),
                ],
                axis=0,
            )
        head = slice(0, 128)
        tail = slice(DEPTH - 128, DEPTH)
        total = jnp.concatenate(
            [
                total[:, head] - jnp.where(lane128 == 0, b[:, head] * c[:, head], 0.0),
                total[:, 128 : DEPTH - 128],
                total[:, tail] - jnp.where(lane128 == 127, b[:, tail] * c[:, tail], 0.0),
            ],
            axis=1,
        )
        value = (2.0 * c - o_buf[at, :]) + (0.5 * s_buf[at, :]) * total
        n_buf[at, 128:DEPTH] = value[:, 128:]
        n_buf[at, head] = value[:, head] + src[step, at, :]
        if step == 0:
            odd = parity("gy")
            faces_out[2][0, pl.ds(x, 1), :] = n_buf[pl.ds(base + 31 * (1 - odd), 1), :]
            faces_out[3][0, pl.ds(x, 1), :] = n_buf[pl.ds(base + 31 * odd, 1), :]
            stiff_out[2][pl.ds(x, 1), :] = s_buf[pl.ds(base, 1), :]
            stiff_out[3][pl.ds(x, 1), :] = s_buf[pl.ds(base + PLANES - 1, 1), :]
        return flux_x

    arrive(0)
    flux = -edges[0] if step == 0 else jnp.zeros((PLANES, DEPTH), jnp.float32)
    for chunk in range(CHUNKS):
        for copy in copies[chunk][2:]:
            copy.wait()
        if chunk + 1 < CHUNKS:
            arrive(chunk + 1)
            flux = lax.fori_loop(chunk * PER, chunk * PER + PER, plane, flux, unroll=4)
        else:
            flux = lax.fori_loop(chunk * PER, chunk * PER + PER - 4, plane, flux, unroll=4)
            for x in range(PLANES - 4, PLANES):
                flux = plane(x, flux, x == PLANES - 1)
        part = pl.ds(chunk * SPAN, SPAN)
        copy = pltpu.make_async_copy(n_buf.at[part], out.at[part], out_sem.at[chunk])
        copy.start()
        out_copies.append(copy)
    if step == 0:
        low, high = n_buf[0:PLANES, :], n_buf[ROWS - PLANES : ROWS, :]
        odd = parity("gx") == 1
        faces_out[0][0] = jnp.where(odd, low, high)
        faces_out[1][0] = jnp.where(odd, high, low)
        stiff_out[0][...] = s_buf[0:PLANES, :]
        stiff_out[1][...] = s_buf[ROWS - PLANES : ROWS, :]
    for copy in out_copies:
        copy.wait()


def inner(field, older, buoy, stiff, src, halos, step):
    big = pltpu.VMEM((ROWS, DEPTH), jnp.float32)
    scratch = [big] * 5
    sems = [pltpu.SemaphoreType.DMA((CHUNKS, 4)), pltpu.SemaphoreType.DMA((CHUNKS,))]
    out_shape = [pltpu.HBM((ROWS, DEPTH), jnp.float32)]
    out_specs = [ANY]
    if step == 0:
        out_shape += [f32(1, PLANES, DEPTH)] * 4 + [f32(PLANES, DEPTH)] * 4
        out_specs += [VMEM] * 8
        scratch = scratch + [pltpu.VMEM((4, PLANES, DEPTH), jnp.float32)]
    return pl.pallas_call(
        lambda *refs: inner_kernel(*refs, step=step),
        in_specs=[ANY] * 4 + [VMEM] * (1 + len(halos)),
        out_specs=out_specs,
        out_shape=out_shape,
        scratch_shapes=scratch + sems,
        compiler_params=ROOM,
        cost_estimate=pl.CostEstimate(flops=(1 << 40) >> (6 * step), bytes_accessed=1, transcendentals=0),
        name="inner%d" % step,
    )(in_hbm(field), in_hbm(older), in_hbm(buoy), in_hbm(stiff), src, *halos)


def interpolation():
    fine = lax.broadcasted_iota(jnp.int32, (COARSE, DEPTH), 1)
    coarse = lax.broadcasted_iota(jnp.int32, (COARSE, DEPTH), 0)
    gap = jnp.abs(fine - 2 * coarse).astype(jnp.float32)
    return jnp.maximum(1.0 - 0.5 * gap, 0.0).astype(jnp.bfloat16)


def dot(a, b):
    return jnp.dot(a, b, preferred_element_type=jnp.float32)


def rim_rows_kernel(received, ids, rim_x, rim_y, corner, tiles, sem):
    copies = []
    for part in range(4):
        at = pl.ds(part * 256, 256)
        copies.append(pltpu.make_async_copy(received.at[at], tiles.at[at], sem.at[part]))
        copies[-1].start()
    row = lax.broadcasted_iota(jnp.int32, (16, 1024), 0)
    wanted = jnp.concatenate([row, row * 16, row + 256, row * 16 + 256], axis=0)
    select = jnp.where(wanted == ids[...], 1.0, 0.0).astype(jnp.bfloat16)
    total = jnp.zeros((64, COARSE), jnp.float32)
    for part in range(4):
        at = slice(part * 256, part * 256 + 256)
        copies[part].wait()
        high, low = split_bf16(tiles[at, :])
        total = total + (dot(select[:, at], high) + dot(select[:, at], low))
    for n in range(2):
        rim_x[n] = total[n * 32 : n * 32 + 16]
        rim_y[n] = total[n * 32 + 16 : n * 32 + 32]
        corner[n] = total[n * 32 : n * 32 + 8]


def rim_rows(received, ids):
    return pl.pallas_call(
        rim_rows_kernel,
        in_specs=[ANY, VMEM],
        out_specs=[VMEM] * 3,
        out_shape=[f32(2, 16, COARSE), f32(2, 16, COARSE), f32(2, 8, COARSE)],
        scratch_shapes=[pltpu.VMEM((1024, COARSE), jnp.float32), pltpu.SemaphoreType.DMA((4,))],
        compiler_params=ROOM,
        cost_estimate=pl.CostEstimate(flops=1 << 30, bytes_accessed=3 << 20, transcendentals=0),
        name="rim_rows",
    )(in_hbm(received), ids)


SCALE = -1.0 / (2.0 * MUTE_RADIUS * MUTE_RADIUS)


def picture_kernel(source, received, ids, first_hbm, second_hbm, *rest):
    own, far, own2, far2, stiff = (rest[4 * k : 4 * k + 4] for k in range(5))
    image, saved, strip, plane_strip, factors = rest[20:25]
    fine, out, first, third, terms, tiles, onehot, along, tile_sem, in_sem, sem = rest[25:]
    tile_copies = []
    for part in range(4):
        at = pl.ds(part * 256, 256)
        tile_copies.append(pltpu.make_async_copy(received.at[at], tiles.at[at], tile_sem.at[part]))
        tile_copies[-1].start()
    loads = []
    for k in range(4):
        at = pl.ds(k * SPAN, SPAN)
        pair = [
            pltpu.make_async_copy(first_hbm.at[at], first.at[at], in_sem.at[k, 0]),
            pltpu.make_async_copy(second_hbm.at[at], third.at[at], in_sem.at[k, 1]),
        ]
        for copy in pair:
            copy.start()
        loads.append(pair)
    near_b, away_b = by_side([m[1] for m in own]), by_side([m[1] for m in far])
    near_f, away_f = by_side([m[0] for m in own2]), by_side([m[0] for m in far2])
    for side, flux in enumerate(edge_fluxes(near_b, away_b, near_f, away_f)):
        terms[side] = (0.5 * stiff[side][...]) * flux
    factors[0, 0] = near_f[1]
    factors[1, 0] = near_f[3]
    for start in range(0, 512, 128):
        tile = lax.broadcasted_iota(jnp.int32, (128, 1024), 0) + start
        onehot[start : start + 128, :] = jnp.where(tile == ids[...], 1.0, 0.0).astype(jnp.bfloat16)
    for copy in tile_copies:
        copy.wait()
    weights = interpolation()
    high, low = split_bf16(tiles[...])
    c_high = dot(onehot[...], high).astype(jnp.bfloat16)
    c_low = dot(onehot[...], low).astype(jnp.bfloat16)
    along[...] = dot(c_high, weights) + dot(c_low, weights)
    row16 = lax.broadcasted_iota(jnp.int32, (16, DEPTH), 0)
    for n in range(2):
        for k in range(16):
            rows = along[n * 256 + k * 16 : n * 256 + k * 16 + 16, :]
            middle = 0.5 * (rows + jnp.where(row16 == 15, 0.0, pltpu.roll(rows, 15, 0)))
            base = (n * 17 + k) * PLANES
            for part in range(4):
                lanes = slice(part * 128, part * 128 + 128)
                fine[part, pl.ds(base, 16, stride=2), :] = rows[:, lanes]
                fine[part, pl.ds(base + 1, 16, stride=2), :] = middle[:, lanes]
        for part in range(4):
            base = (n * 17 + 16) * PLANES
            fine[part, base : base + PLANES, :] = jnp.zeros((PLANES, 128), jnp.float32)
    gx = lax.axis_index("gx")
    gy = lax.axis_index("gy")
    y = (lax.broadcasted_iota(jnp.int32, (PLANES, DEPTH), 0) + gy * PLANES - source[0, 1]).astype(jnp.float32)
    z = (lax.broadcasted_iota(jnp.int32, (PLANES, DEPTH), 1) - source[0, 2]).astype(jnp.float32)
    decay_yz = jnp.exp((y * y + z * z) * SCALE)
    x_base = gx * PLANES - source[0, 0]
    copies = []
    for x in range(PLANES):
        k = x // 2
        if x % PER == 0:
            for copy in loads[x // PER]:
                copy.wait()
        at = slice(x * PLANES, (x + 1) * PLANES)
        if x == 0:
            third[at, :] += terms[0]
        if x == PLANES - 1:
            third[at, :] += terms[1]
        third[x * PLANES : x * PLANES + 1, :] += terms[2, x : x + 1, :]
        third[x * PLANES + 31 : x * PLANES + 32, :] += terms[3, x : x + 1, :]
        factors[1, 1, x : x + 1, :] = third[x * PLANES + 31 : x * PLANES + 32, :]
        dx = jnp.full((1, 128), x_base + x, jnp.int32).astype(jnp.float32)
        decay = jnp.exp((dx * dx) * SCALE)
        for part in range(4):
            lanes = slice(part * 128, part * 128 + 128)
            taper = 1.0 - decay * decay_yz[:, lanes]
            snaps = []
            for n in range(2):
                start = (n * 17 + k) * PLANES
                snap = fine[part, start : start + PLANES, :]
                if x % 2:
                    snap = 0.5 * (snap + fine[part, start + PLANES : start + 2 * PLANES, :])
                snaps.append(snap)
            value = taper * (snaps[0] * first[at, lanes] + snaps[1] * third[at, lanes])
            out[x, :, lanes] = value
            strip[x, :, lanes] = value[24:32]
        if x % 4 == 3:
            group = pl.ds(x - 3, 3 if x == PLANES - 1 else 4)
            rows = pl.ds((x - 3) * PLANES, 4 * PLANES)
            copies.append(
                pltpu.make_async_copy(
                    out.at[group, 0:24], image.at[group, 0:24], sem.at[x // 4, 0]
                )
            )
            copies.append(pltpu.make_async_copy(third.at[rows], saved.at[rows], sem.at[x // 4, 1]))
            for copy in copies[-2:]:
                copy.start()
    plane_strip[...] = out[PLANES - 1, 0:24, :]
    last_x = jnp.full((PLANES, DEPTH), x_base + PLANES - 1, jnp.int32).astype(jnp.float32)
    last_y = jnp.full((PLANES, DEPTH), gy * PLANES + 31 - source[0, 1], jnp.int32).astype(jnp.float32)
    x = (lax.broadcasted_iota(jnp.int32, (PLANES, DEPTH), 0) + x_base).astype(jnp.float32)
    for way, (a, b) in enumerate(((last_x, y), (x, last_y))):
        taper = 1.0 - jnp.exp((a * a + b * b + z * z) * SCALE)
        newest = third[ROWS - PLANES : ROWS, :] if way == 0 else factors[1, 1]
        factors[way, 1] = taper * newest
        factors[way, 0] = taper * factors[way, 0]
    for copy in copies:
        copy.wait()


def picture(source, received, ids, first, second, edges):
    big = pltpu.VMEM((ROWS, DEPTH), jnp.float32)
    return pl.pallas_call(
        picture_kernel,
        in_specs=[SMEM, ANY, VMEM, ANY, ANY] + [VMEM] * 20,
        out_specs=[ANY, ANY] + [VMEM] * 3,
        out_shape=[
            pltpu.HBM((PLANES, PLANES, DEPTH), jnp.float32),
            pltpu.HBM((ROWS, DEPTH), jnp.float32),
            f32(PLANES, 8, DEPTH),
            f32(24, DEPTH),
            f32(2, 2, PLANES, DEPTH),
        ],
        scratch_shapes=[
            pltpu.VMEM((4, 2 * 17 * PLANES, 128), jnp.float32),
            pltpu.VMEM((PLANES, PLANES, DEPTH), jnp.float32),
            big,
            big,
            pltpu.VMEM((4, PLANES, DEPTH), jnp.float32),
            pltpu.VMEM((1024, COARSE), jnp.float32),
            pltpu.VMEM((512, 1024), jnp.bfloat16),
            pltpu.VMEM((512, DEPTH), jnp.float32),
            pltpu.SemaphoreType.DMA((4,)),
            pltpu.SemaphoreType.DMA((4, 2)),
            pltpu.SemaphoreType.DMA((8, 2)),
        ],
        compiler_params=ROOM,
        cost_estimate=pl.CostEstimate(flops=1 << 40, bytes_accessed=8 << 20, transcendentals=0),
        name="picture",
    )(source, in_hbm(received), ids, in_hbm(first), in_hbm(second), *edges)


def rims_kernel(
    rim_x_hbm, rim_y_hbm, corner_hbm, strip, plane_strip, factors,
    image_in, image, rim_x, rim_y, corner, rims, along, fine, strip_out, plane_out, delta, sem,
):
    pairs = ((rim_x_hbm, rim_x), (rim_y_hbm, rim_y), (corner_hbm, corner))
    loads = [pltpu.make_async_copy(a, b, sem.at[2 + k]) for k, (a, b) in enumerate(pairs)]
    for copy in loads:
        copy.start()
    weights = interpolation()
    gx = lax.axis_index("gx")
    gy = lax.axis_index("gy")
    keep_x = jnp.where(gx < lax.axis_size("gx") - 1, 1.0, 0.0)
    keep_y = jnp.where(gy < lax.axis_size("gy") - 1, 1.0, 0.0)
    for copy in loads:
        copy.wait()
    for n in range(2):
        rims[n * 40 : n * 40 + 16] = rim_x[n] * (0.5 * keep_x)
        rims[n * 40 + 16 : n * 40 + 32] = rim_y[n] * (0.5 * keep_y)
        rims[n * 40 + 32 : n * 40 + 40] = corner[n] * (0.5 * keep_x * keep_y)
    high, low = split_bf16(rims[...])
    along[...] = dot(high, weights) + dot(low, weights)
    row16 = lax.broadcasted_iota(jnp.int32, (16, DEPTH), 0)
    for n in range(2):
        for way in range(2):
            rows = along[n * 40 + way * 16 : n * 40 + way * 16 + 16, :]
            end = along[n * 40 + 32 : n * 40 + 33, :] if way == 0 else 0.0
            middle = 0.5 * (rows + jnp.where(row16 == 15, end, pltpu.roll(rows, 15, 0)))
            base = (n * 2 + way) * PLANES
            for part in range(4):
                lanes = slice(part * 128, part * 128 + 128)
                fine[part, pl.ds(base, 16, stride=2), :] = rows[:, lanes]
                fine[part, pl.ds(base + 1, 16, stride=2), :] = middle[:, lanes]
    for part in range(4):
        lanes = slice(part * 128, part * 128 + 128)
        for way in range(2):
            delta[way, :, lanes] = (
                fine[part, way * PLANES : (way + 1) * PLANES, :] * factors[way, 0, :, lanes]
                + fine[part, (2 + way) * PLANES : (3 + way) * PLANES, :] * factors[way, 1, :, lanes]
            )
    row8 = lax.broadcasted_iota(jnp.int32, (8, DEPTH), 0)
    for x in range(PLANES):
        value = strip[x] + jnp.where(row8 == 7, delta[1, x : x + 1, :], 0.0)
        if x == PLANES - 1:
            value = value + delta[0, 24:32, :]
        strip_out[x] = value
    plane_out[...] = plane_strip[...] + delta[0, 0:24, :]
    copies = [
        pltpu.make_async_copy(strip_out, image.at[:, 24:32], sem.at[0]),
        pltpu.make_async_copy(plane_out, image.at[PLANES - 1, 0:24], sem.at[1]),
    ]
    for copy in copies:
        copy.start()
    for copy in copies:
        copy.wait()


def add_rims(rims, strips, image):
    return pl.pallas_call(
        rims_kernel,
        in_specs=[ANY] * 3 + [VMEM] * 3 + [ANY],
        out_specs=ANY,
        out_shape=pltpu.HBM((PLANES, PLANES, DEPTH), jnp.float32),
        input_output_aliases={6: 0},
        scratch_shapes=[
            pltpu.VMEM((2, 16, COARSE), jnp.float32),
            pltpu.VMEM((2, 16, COARSE), jnp.float32),
            pltpu.VMEM((2, 8, COARSE), jnp.float32),
            pltpu.VMEM((80, COARSE), jnp.float32),
            pltpu.VMEM((80, DEPTH), jnp.float32),
            pltpu.VMEM((4, 4 * PLANES, 128), jnp.float32),
            pltpu.VMEM((PLANES, 8, DEPTH), jnp.float32),
            pltpu.VMEM((24, DEPTH), jnp.float32),
            pltpu.VMEM((2, PLANES, DEPTH), jnp.float32),
            pltpu.SemaphoreType.DMA((5,)),
        ],
        compiler_params=ROOM,
        cost_estimate=pl.CostEstimate(flops=1 << 20, bytes_accessed=2 << 20, transcendentals=0),
        name="add_rims",
    )(*rims, *strips, in_hbm(image))


def per_device(
    stiffness,
    buoyancy,
    older_field,
    current_field,
    stored_tiles,
    tile_ids,
    tile_counts,
    receiver_cells,
    receiver_data,
    source_cell,
):
    older = older_field[0].reshape(ROWS, DEPTH)
    current = current_field[0].reshape(ROWS, DEPTH)
    stiff = stiffness.reshape(ROWS, DEPTH)
    buoy = buoyancy.reshape(ROWS, DEPTH)

    own = list(faces(current_field[0], buoyancy))
    far = exchange(own)
    tiles, own[0] = lax.optimization_barrier((stored_tiles, own[0]))
    received = lax.all_to_all(
        tiles[0, 0], ("shot", "gx"), split_axis=0, concat_axis=0, tiled=True
    ).reshape(1024, COARSE)
    numbers, counts, far[0], far[1] = lax.optimization_barrier((tile_ids, tile_counts, far[0], far[1]))
    slot = lax.broadcasted_iota(jnp.int32, (32, 32), 1)
    ids = jnp.where(slot < counts[0, 0][:, None], numbers[0, 0], -1).reshape(1, 1024)
    src = sources(receiver_cells[0], receiver_data[0])
    second, *rest = inner(current, older, buoy, stiff, src, [*own, *far], 0)
    own2, stiff_faces = rest[:4], rest[4:]
    far2 = exchange(own2)
    (third,) = inner(second, current, buoy, stiff, src, [], 1)

    received, third = lax.optimization_barrier((received, third))
    rim_x, rim_y, corner = rim_rows(received, ids)
    rims = [down(rim_x, "gx"), down(rim_y, "gy"), diagonal(corner)]
    edges = [*own, *far, *own2, *far2, *stiff_faces]
    image, last_current, *strips = picture(source_cell, received, ids, second, third, edges)
    image = add_rims(rims, strips, image)
    shape = current_field.shape
    return image.reshape(shape), second.reshape(shape), last_current.reshape(shape)


def exchange(own):
    return [
        swap(own[0], "gx", 0),
        swap(own[1], "gx", 1),
        swap(own[2], "gy", 0),
        swap(own[3], "gy", 1),
    ]


def down(block, axis):
    return lax.ppermute(block, axis, [(i, i - 1) for i in range(1, lax.axis_size(axis))])


def diagonal(block):
    nx, ny = lax.axis_size("gx"), lax.axis_size("gy")
    route = [(i * ny + j, (i - 1) * ny + j - 1) for i in range(1, nx) for j in range(1, ny)]
    return lax.ppermute(block, ("gx", "gy"), route)


def solution(mesh):
    in_specs = (
        P("gx", "gy", None),
        P("gx", "gy", None),
        P("shot", "gx", "gy", None),
        P("shot", "gx", "gy", None),
        P(("shot", "gx"), "gy", None, None, None),
        P(("shot", "gx"), "gy", None, None),
        P(("shot", "gx"), "gy", None),
        P("shot", None, None),
        P("shot", None, None),
        P("shot", None),
    )
    out_specs = (
        P("shot", "gx", "gy", None),
        P("shot", "gx", "gy", None),
        P("shot", "gx", "gy", None),
    )
    return jax.shard_map(
        per_device, mesh=mesh, in_specs=in_specs, out_specs=out_specs, check_vma=False
    )
```

```python
import jax
import jax.numpy as jnp
from jax import lax
from jax.experimental import pallas as pl
from jax.experimental.pallas import tpu as pltpu
from jax.sharding import PartitionSpec as P

MUTE_RADIUS = 3.0
PLANES = 32
ROWS = 1024
DEPTH = 512
COARSE = 256
CHUNKS = 4
PER = PLANES // CHUNKS
SPAN = ROWS // CHUNKS
VMEM = pl.BlockSpec(memory_space=pltpu.VMEM)
SMEM = pl.BlockSpec(memory_space=pltpu.SMEM)
ANY = pl.BlockSpec(memory_space=pl.ANY)
ROOM = pltpu.CompilerParams(vmem_limit_bytes=16 << 20)


def swap(block, axis, start):
    count = lax.axis_size(axis)
    route = []
    for low in range(start, count - 1, 2):
        route += [(low, low + 1), (low + 1, low)]
    return lax.ppermute(block, axis, route)


def parity(axis):
    return lax.rem(lax.axis_index(axis), 2)


def by_side(messages):
    values = []
    for axis, pair in (("gx", messages[:2]), ("gy", messages[2:])):
        odd = parity(axis) == 1
        values += [jnp.where(odd, pair[0], pair[1]), jnp.where(odd, pair[1], pair[0])]
    return values


def f32(*shape):
    return jax.ShapeDtypeStruct(shape, jnp.float32)


def split_bf16(x):
    high = x.astype(jnp.bfloat16)
    return high, (x - high.astype(jnp.float32)).astype(jnp.bfloat16)


def faces_kernel(fx_lo, fx_hi, fy_lo, fy_hi, bx_lo, bx_hi, by_lo, by_hi, x_first, x_next, y_first, y_next):
    odd_x = parity("gx") == 1
    odd_y = parity("gy") == 1
    for slot, refs in enumerate(((fx_lo, fx_hi, fy_lo, fy_hi), (bx_lo, bx_hi, by_lo, by_hi))):
        low, high = refs[0][0], refs[1][0]
        x_first[slot] = jnp.where(odd_x, low, high)
        x_next[slot] = jnp.where(odd_x, high, low)
        for x in range(PLANES):
            low, high = refs[2][x, 0:1, :], refs[3][x, 7:8, :]
            y_first[slot, x : x + 1, :] = jnp.where(odd_y, low, high)
            y_next[slot, x : x + 1, :] = jnp.where(odd_y, high, low)


def faces(field, buoyancy):
    plane_lo = pl.BlockSpec((1, PLANES, DEPTH), lambda i: (0, 0, 0))
    plane_hi = pl.BlockSpec((1, PLANES, DEPTH), lambda i: (PLANES - 1, 0, 0))
    rows_lo = pl.BlockSpec((PLANES, 8, DEPTH), lambda i: (0, 0, 0))
    rows_hi = pl.BlockSpec((PLANES, 8, DEPTH), lambda i: (0, PLANES // 8 - 1, 0))
    out = pl.BlockSpec((2, PLANES, DEPTH), lambda i: (0, 0, 0))
    return pl.pallas_call(
        faces_kernel,
        grid=(1,),
        in_specs=[plane_lo, plane_hi, rows_lo, rows_hi] * 2,
        out_specs=[out] * 4,
        out_shape=[f32(2, PLANES, DEPTH)] * 4,
        compiler_params=ROOM,
        cost_estimate=pl.CostEstimate(flops=0, bytes_accessed=3 << 20, transcendentals=0),
        name="faces",
    )(*([in_hbm(field)] * 4 + [in_hbm(buoyancy)] * 4))


def sources_kernel(cells, data, out):
    base_x = lax.axis_index("gx") * PLANES
    base_y = lax.axis_index("gy") * PLANES
    local_x = cells[0:1, :] - base_x
    local_y = cells[1:2, :] - base_y
    inside = (local_x >= 0) & (local_x < PLANES) & (local_y >= 0) & (local_y < PLANES)
    row = jnp.where(inside, local_x * PLANES + local_y, -1)
    depth_id = lax.broadcasted_iota(jnp.int32, (8, 1024), 0)
    here = depth_id == cells[2:3, :]
    parts = []
    for step in range(2):
        value = jnp.where(here, data[step : step + 1, :], 0.0)
        parts.append(split_bf16(value))
    table = jnp.concatenate([parts[0][0], parts[0][1], parts[1][0], parts[1][1]], axis=0)
    lane = lax.broadcasted_iota(jnp.int32, (128, 128), 1)
    pad = jnp.zeros((96, 1024), jnp.bfloat16)
    table = jnp.concatenate([table, pad], axis=0)
    for start in range(0, ROWS, 128):
        ids = lax.broadcasted_iota(jnp.int32, (128, 1024), 0) + start
        select = jnp.where(ids == row, 1.0, 0.0).astype(jnp.bfloat16)
        product = lax.dot_general(
            select, table, (((1,), (1,)), ((), ())), preferred_element_type=jnp.float32
        )
        for step in range(2):
            high = pltpu.roll(product, (128 - 16 * step) % 128, 1)
            low = pltpu.roll(product, 128 - 16 * step - 8, 1)
            out[step, start : start + 128, :] = jnp.where(lane < 8, high + low, 0.0)


def sources(cells, data):
    return pl.pallas_call(
        sources_kernel,
        in_specs=[VMEM, VMEM],
        out_specs=VMEM,
        out_shape=f32(2, ROWS, 128),
        cost_estimate=pl.CostEstimate(flops=1, bytes_accessed=1, transcendentals=0),
        compiler_params=ROOM,
        name="sources",
    )(cells, data)


def in_hbm(x):
    return pltpu.with_memory_space_constraint(x, pltpu.HBM)


def edge_fluxes(own_b, far_b, own_f, far_f):
    gx = lax.axis_index("gx")
    gy = lax.axis_index("gy")
    keep = [
        jnp.where(gx > 0, 1.0, 0.0),
        jnp.where(gx < lax.axis_size("gx") - 1, 1.0, 0.0),
        jnp.where(gy > 0, 1.0, 0.0),
        jnp.where(gy < lax.axis_size("gy") - 1, 1.0, 0.0),
    ]
    return [
        (own_b[side] + keep[side] * far_b[side])
        * (keep[side] * far_f[side] - own_f[side])
        for side in range(4)
    ]


def inner_kernel(field, older, buoy, stiff, src, *rest, step):
    if step == 0:
        own, far, rest = rest[:4], rest[4:8], rest[8:]
        out, faces_out, stiff_out = rest[0], rest[1:5], rest[5:9]
        f_buf, b_buf, s_buf, o_buf, n_buf, edges, in_sem, out_sem = rest[9:]
    else:
        out, f_buf, b_buf, s_buf, o_buf, n_buf, in_sem, out_sem = rest
    copies = []
    for chunk in range(CHUNKS):
        part = pl.ds(chunk * SPAN, SPAN)
        pairs = ((field, f_buf), (buoy, b_buf), (stiff, s_buf), (older, o_buf))
        group = [
            pltpu.make_async_copy(hbm.at[part], buf.at[part], in_sem.at[chunk, k])
            for k, (hbm, buf) in enumerate(pairs)
        ]
        for copy in group:
            copy.start()
        copies.append(group)
    row8 = lax.broadcasted_iota(jnp.int32, (8, DEPTH), 0)
    lane128 = lax.broadcasted_iota(jnp.int32, (PLANES, 128), 1)
    out_copies = []

    if step == 0:
        near_b, away_b = by_side([m[1] for m in own]), by_side([m[1] for m in far])
        near_f, away_f = by_side([m[0] for m in own]), by_side([m[0] for m in far])
        for side, flux in enumerate(edge_fluxes(near_b, away_b, near_f, away_f)):
            edges[side] = flux

    def arrive(chunk):
        for copy in copies[chunk][:2]:
            copy.wait()

    def plane(x, flux_before, last=False):
        base = pl.multiple_of(x * PLANES, PLANES)
        at = pl.ds(base, PLANES)
        c = f_buf[at, :]
        b = b_buf[at, :]
        if last:
            flux_x = edges[1] if step == 0 else jnp.zeros_like(c)
        else:
            nearby = pl.ds(base + PLANES, PLANES)
            flux_x = (b + b_buf[nearby, :]) * (f_buf[nearby, :] - c)
        flux_y = (b + pltpu.roll(b, PLANES - 1, 0)) * (pltpu.roll(c, PLANES - 1, 0) - c)
        flux_y = jnp.concatenate(
            [flux_y[0:24], jnp.where(row8 == 7, 0.0, flux_y[24:32])], axis=0
        )
        flux_z = (b + pltpu.roll(b, DEPTH - 1, 1)) * (pltpu.roll(c, DEPTH - 1, 1) - c)
        flux_z = jnp.concatenate(
            [flux_z[:, : DEPTH - 128], jnp.where(lane128 == 127, 0.0, flux_z[:, DEPTH - 128 :])],
            axis=1,
        )
        total = (flux_x - flux_before) + (flux_y - pltpu.roll(flux_y, 1, 0))
        total = total + (flux_z - pltpu.roll(flux_z, 1, 1))
        if step == 0:
            total = jnp.concatenate(
                [
                    total[0:8] + jnp.where(row8 == 0, edges[2, pl.ds(x, 1), :], 0.0),
                    total[8:24],
                    total[24:32] + jnp.where(row8 == 7, edges[3, pl.ds(x, 1), :], 0.0),
                ],
                axis=0,
            )
        head = slice(0, 128)
        tail = slice(DEPTH - 128, DEPTH)
        total = jnp.concatenate(
            [
                total[:, head] - jnp.where(lane128 == 0, b[:, head] * c[:, head], 0.0),
                total[:, 128 : DEPTH - 128],
                total[:, tail] - jnp.where(lane128 == 127, b[:, tail] * c[:, tail], 0.0),
            ],
            axis=1,
        )
        value = (2.0 * c - o_buf[at, :]) + (0.5 * s_buf[at, :]) * total
        n_buf[at, 128:DEPTH] = value[:, 128:]
        n_buf[at, head] = value[:, head] + src[step, at, :]
        if step == 0:
            odd = parity("gy")
            faces_out[2][0, pl.ds(x, 1), :] = n_buf[pl.ds(base + 31 * (1 - odd), 1), :]
            faces_out[3][0, pl.ds(x, 1), :] = n_buf[pl.ds(base + 31 * odd, 1), :]
            stiff_out[2][pl.ds(x, 1), :] = s_buf[pl.ds(base, 1), :]
            stiff_out[3][pl.ds(x, 1), :] = s_buf[pl.ds(base + PLANES - 1, 1), :]
        return flux_x

    arrive(0)
    flux = -edges[0] if step == 0 else jnp.zeros((PLANES, DEPTH), jnp.float32)
    for chunk in range(CHUNKS):
        for copy in copies[chunk][2:]:
            copy.wait()
        if chunk + 1 < CHUNKS:
            arrive(chunk + 1)
            flux = lax.fori_loop(chunk * PER, chunk * PER + PER, plane, flux, unroll=4)
        else:
            flux = lax.fori_loop(chunk * PER, chunk * PER + PER - 4, plane, flux, unroll=4)
            for x in range(PLANES - 4, PLANES):
                flux = plane(x, flux, x == PLANES - 1)
        part = pl.ds(chunk * SPAN, SPAN)
        copy = pltpu.make_async_copy(n_buf.at[part], out.at[part], out_sem.at[chunk])
        copy.start()
        out_copies.append(copy)
    if step == 0:
        low, high = n_buf[0:PLANES, :], n_buf[ROWS - PLANES : ROWS, :]
        odd = parity("gx") == 1
        faces_out[0][0] = jnp.where(odd, low, high)
        faces_out[1][0] = jnp.where(odd, high, low)
        stiff_out[0][...] = s_buf[0:PLANES, :]
        stiff_out[1][...] = s_buf[ROWS - PLANES : ROWS, :]
    for copy in out_copies:
        copy.wait()


def inner(field, older, buoy, stiff, src, halos, step):
    big = pltpu.VMEM((ROWS, DEPTH), jnp.float32)
    scratch = [big] * 5
    sems = [pltpu.SemaphoreType.DMA((CHUNKS, 4)), pltpu.SemaphoreType.DMA((CHUNKS,))]
    out_shape = [pltpu.HBM((ROWS, DEPTH), jnp.float32)]
    out_specs = [ANY]
    if step == 0:
        out_shape += [f32(1, PLANES, DEPTH)] * 4 + [f32(PLANES, DEPTH)] * 4
        out_specs += [VMEM] * 8
        scratch = scratch + [pltpu.VMEM((4, PLANES, DEPTH), jnp.float32)]
    return pl.pallas_call(
        lambda *refs: inner_kernel(*refs, step=step),
        in_specs=[ANY] * 4 + [VMEM] * (1 + len(halos)),
        out_specs=out_specs,
        out_shape=out_shape,
        scratch_shapes=scratch + sems,
        compiler_params=ROOM,
        cost_estimate=pl.CostEstimate(flops=(1 << 40) >> (6 * step), bytes_accessed=1, transcendentals=0),
        name="inner%d" % step,
    )(in_hbm(field), in_hbm(older), in_hbm(buoy), in_hbm(stiff), src, *halos)


def interpolation():
    fine = lax.broadcasted_iota(jnp.int32, (COARSE, DEPTH), 1)
    coarse = lax.broadcasted_iota(jnp.int32, (COARSE, DEPTH), 0)
    gap = jnp.abs(fine - 2 * coarse).astype(jnp.float32)
    return jnp.maximum(1.0 - 0.5 * gap, 0.0).astype(jnp.bfloat16)


def dot(a, b):
    return jnp.dot(a, b, preferred_element_type=jnp.float32)


def rim_rows_kernel(received, ids, rim_x, rim_y, corner, tiles, sem):
    copies = []
    for part in range(4):
        at = pl.ds(part * 256, 256)
        copies.append(pltpu.make_async_copy(received.at[at], tiles.at[at], sem.at[part]))
        copies[-1].start()
    row = lax.broadcasted_iota(jnp.int32, (16, 1024), 0)
    wanted = jnp.concatenate([row, row * 16, row + 256, row * 16 + 256], axis=0)
    select = jnp.where(wanted == ids[...], 1.0, 0.0).astype(jnp.bfloat16)
    total = jnp.zeros((64, COARSE), jnp.float32)
    for part in range(4):
        at = slice(part * 256, part * 256 + 256)
        copies[part].wait()
        high, low = split_bf16(tiles[at, :])
        total = total + (dot(select[:, at], high) + dot(select[:, at], low))
    for n in range(2):
        rim_x[n] = total[n * 32 : n * 32 + 16]
        rim_y[n] = total[n * 32 + 16 : n * 32 + 32]
        corner[n] = total[n * 32 : n * 32 + 8]


def rim_rows(received, ids):
    return pl.pallas_call(
        rim_rows_kernel,
        in_specs=[ANY, VMEM],
        out_specs=[VMEM] * 3,
        out_shape=[f32(2, 16, COARSE), f32(2, 16, COARSE), f32(2, 8, COARSE)],
        scratch_shapes=[pltpu.VMEM((1024, COARSE), jnp.float32), pltpu.SemaphoreType.DMA((4,))],
        compiler_params=ROOM,
        cost_estimate=pl.CostEstimate(flops=1 << 30, bytes_accessed=3 << 20, transcendentals=0),
        name="rim_rows",
    )(in_hbm(received), ids)


SCALE = -1.0 / (2.0 * MUTE_RADIUS * MUTE_RADIUS)


def picture_kernel(source, received, ids, first_hbm, second_hbm, *rest):
    own, far, own2, far2, stiff = (rest[4 * k : 4 * k + 4] for k in range(5))
    image, saved, strip, plane_strip, factors = rest[20:25]
    fine, out, first, third, terms, tiles, onehot, along, tile_sem, in_sem, sem = rest[25:]
    tile_copies = []
    for part in range(4):
        at = pl.ds(part * 256, 256)
        tile_copies.append(pltpu.make_async_copy(received.at[at], tiles.at[at], tile_sem.at[part]))
        tile_copies[-1].start()
    loads = []
    for k in range(4):
        at = pl.ds(k * SPAN, SPAN)
        pair = [
            pltpu.make_async_copy(first_hbm.at[at], first.at[at], in_sem.at[k, 0]),
            pltpu.make_async_copy(second_hbm.at[at], third.at[at], in_sem.at[k, 1]),
        ]
        for copy in pair:
            copy.start()
        loads.append(pair)
    near_b, away_b = by_side([m[1] for m in own]), by_side([m[1] for m in far])
    near_f, away_f = by_side([m[0] for m in own2]), by_side([m[0] for m in far2])
    for side, flux in enumerate(edge_fluxes(near_b, away_b, near_f, away_f)):
        terms[side] = (0.5 * stiff[side][...]) * flux
    factors[0, 0] = near_f[1]
    factors[1, 0] = near_f[3]
    for start in range(0, 512, 128):
        tile = lax.broadcasted_iota(jnp.int32, (128, 1024), 0) + start
        onehot[start : start + 128, :] = jnp.where(tile == ids[...], 1.0, 0.0).astype(jnp.bfloat16)
    for copy in tile_copies:
        copy.wait()
    weights = interpolation()
    high, low = split_bf16(tiles[...])
    c_high = dot(onehot[...], high).astype(jnp.bfloat16)
    c_low = dot(onehot[...], low).astype(jnp.bfloat16)
    along[...] = dot(c_high, weights) + dot(c_low, weights)
    row16 = lax.broadcasted_iota(jnp.int32, (16, DEPTH), 0)
    for n in range(2):
        for k in range(16):
            rows = along[n * 256 + k * 16 : n * 256 + k * 16 + 16, :]
            middle = 0.5 * (rows + jnp.where(row16 == 15, 0.0, pltpu.roll(rows, 15, 0)))
            base = (n * 17 + k) * PLANES
            for part in range(4):
                lanes = slice(part * 128, part * 128 + 128)
                fine[part, pl.ds(base, 16, stride=2), :] = rows[:, lanes]
                fine[part, pl.ds(base + 1, 16, stride=2), :] = middle[:, lanes]
        for part in range(4):
            base = (n * 17 + 16) * PLANES
            fine[part, base : base + PLANES, :] = jnp.zeros((PLANES, 128), jnp.float32)
    gx = lax.axis_index("gx")
    gy = lax.axis_index("gy")
    y = (lax.broadcasted_iota(jnp.int32, (PLANES, DEPTH), 0) + gy * PLANES - source[0, 1]).astype(jnp.float32)
    z = (lax.broadcasted_iota(jnp.int32, (PLANES, DEPTH), 1) - source[0, 2]).astype(jnp.float32)
    decay_yz = jnp.exp((y * y + z * z) * SCALE)
    x_base = gx * PLANES - source[0, 0]
    copies = []
    for x in range(PLANES):
        k = x // 2
        if x % PER == 0:
            for copy in loads[x // PER]:
                copy.wait()
        at = slice(x * PLANES, (x + 1) * PLANES)
        if x == 0:
            third[at, :] += terms[0]
        if x == PLANES - 1:
            third[at, :] += terms[1]
        third[x * PLANES : x * PLANES + 1, :] += terms[2, x : x + 1, :]
        third[x * PLANES + 31 : x * PLANES + 32, :] += terms[3, x : x + 1, :]
        factors[1, 1, x : x + 1, :] = third[x * PLANES + 31 : x * PLANES + 32, :]
        dx = jnp.full((1, 128), x_base + x, jnp.int32).astype(jnp.float32)
        decay = jnp.exp((dx * dx) * SCALE)
        for part in range(4):
            lanes = slice(part * 128, part * 128 + 128)
            taper = 1.0 - decay * decay_yz[:, lanes]
            snaps = []
            for n in range(2):
                start = (n * 17 + k) * PLANES
                snap = fine[part, start : start + PLANES, :]
                if x % 2:
                    snap = 0.5 * (snap + fine[part, start + PLANES : start + 2 * PLANES, :])
                snaps.append(snap)
            value = taper * (snaps[0] * first[at, lanes] + snaps[1] * third[at, lanes])
            out[x, :, lanes] = value
            strip[x, :, lanes] = value[24:32]
        if x % 4 == 3:
            group = pl.ds(x - 3, 3 if x == PLANES - 1 else 4)
            rows = pl.ds((x - 3) * PLANES, 4 * PLANES)
            copies.append(
                pltpu.make_async_copy(
                    out.at[group, 0:24], image.at[group, 0:24], sem.at[x // 4, 0]
                )
            )
            copies.append(pltpu.make_async_copy(third.at[rows], saved.at[rows], sem.at[x // 4, 1]))
            for copy in copies[-2:]:
                copy.start()
    plane_strip[...] = out[PLANES - 1, 0:24, :]
    last_x = jnp.full((PLANES, DEPTH), x_base + PLANES - 1, jnp.int32).astype(jnp.float32)
    last_y = jnp.full((PLANES, DEPTH), gy * PLANES + 31 - source[0, 1], jnp.int32).astype(jnp.float32)
    x = (lax.broadcasted_iota(jnp.int32, (PLANES, DEPTH), 0) + x_base).astype(jnp.float32)
    for way, (a, b) in enumerate(((last_x, y), (x, last_y))):
        taper = 1.0 - jnp.exp((a * a + b * b + z * z) * SCALE)
        newest = third[ROWS - PLANES : ROWS, :] if way == 0 else factors[1, 1]
        factors[way, 1] = taper * newest
        factors[way, 0] = taper * factors[way, 0]
    for copy in copies:
        copy.wait()


def picture(source, received, ids, first, second, edges):
    big = pltpu.VMEM((ROWS, DEPTH), jnp.float32)
    return pl.pallas_call(
        picture_kernel,
        in_specs=[SMEM, ANY, VMEM, ANY, ANY] + [VMEM] * 20,
        out_specs=[ANY, ANY] + [VMEM] * 3,
        out_shape=[
            pltpu.HBM((PLANES, PLANES, DEPTH), jnp.float32),
            pltpu.HBM((ROWS, DEPTH), jnp.float32),
            f32(PLANES, 8, DEPTH),
            f32(24, DEPTH),
            f32(2, 2, PLANES, DEPTH),
        ],
        scratch_shapes=[
            pltpu.VMEM((4, 2 * 17 * PLANES, 128), jnp.float32),
            pltpu.VMEM((PLANES, PLANES, DEPTH), jnp.float32),
            big,
            big,
            pltpu.VMEM((4, PLANES, DEPTH), jnp.float32),
            pltpu.VMEM((1024, COARSE), jnp.float32),
            pltpu.VMEM((512, 1024), jnp.bfloat16),
            pltpu.VMEM((512, DEPTH), jnp.float32),
            pltpu.SemaphoreType.DMA((4,)),
            pltpu.SemaphoreType.DMA((4, 2)),
            pltpu.SemaphoreType.DMA((8, 2)),
        ],
        compiler_params=ROOM,
        cost_estimate=pl.CostEstimate(flops=1 << 40, bytes_accessed=8 << 20, transcendentals=0),
        name="picture",
    )(source, in_hbm(received), ids, in_hbm(first), in_hbm(second), *edges)


def rims_kernel(
    rim_x_hbm, rim_y_hbm, corner_hbm, strip, plane_strip, factors,
    image_in, image, rim_x, rim_y, corner, rims, along, fine, strip_out, plane_out, delta, sem,
):
    pairs = ((rim_x_hbm, rim_x), (rim_y_hbm, rim_y), (corner_hbm, corner))
    loads = [pltpu.make_async_copy(a, b, sem.at[2 + k]) for k, (a, b) in enumerate(pairs)]
    for copy in loads:
        copy.start()
    weights = interpolation()
    gx = lax.axis_index("gx")
    gy = lax.axis_index("gy")
    keep_x = jnp.where(gx < lax.axis_size("gx") - 1, 1.0, 0.0)
    keep_y = jnp.where(gy < lax.axis_size("gy") - 1, 1.0, 0.0)
    for copy in loads:
        copy.wait()
    for n in range(2):
        rims[n * 40 : n * 40 + 16] = rim_x[n] * (0.5 * keep_x)
        rims[n * 40 + 16 : n * 40 + 32] = rim_y[n] * (0.5 * keep_y)
        rims[n * 40 + 32 : n * 40 + 40] = corner[n] * (0.5 * keep_x * keep_y)
    high, low = split_bf16(rims[...])
    along[...] = dot(high, weights) + dot(low, weights)
    row16 = lax.broadcasted_iota(jnp.int32, (16, DEPTH), 0)
    for n in range(2):
        for way in range(2):
            rows = along[n * 40 + way * 16 : n * 40 + way * 16 + 16, :]
            end = along[n * 40 + 32 : n * 40 + 33, :] if way == 0 else 0.0
            middle = 0.5 * (rows + jnp.where(row16 == 15, end, pltpu.roll(rows, 15, 0)))
            base = (n * 2 + way) * PLANES
            for part in range(4):
                lanes = slice(part * 128, part * 128 + 128)
                fine[part, pl.ds(base, 16, stride=2), :] = rows[:, lanes]
                fine[part, pl.ds(base + 1, 16, stride=2), :] = middle[:, lanes]
    for part in range(4):
        lanes = slice(part * 128, part * 128 + 128)
        for way in range(2):
            delta[way, :, lanes] = (
                fine[part, way * PLANES : (way + 1) * PLANES, :] * factors[way, 0, :, lanes]
                + fine[part, (2 + way) * PLANES : (3 + way) * PLANES, :] * factors[way, 1, :, lanes]
            )
    row8 = lax.broadcasted_iota(jnp.int32, (8, DEPTH), 0)
    for x in range(PLANES):
        value = strip[x] + jnp.where(row8 == 7, delta[1, x : x + 1, :], 0.0)
        if x == PLANES - 1:
            value = value + delta[0, 24:32, :]
        strip_out[x] = value
    plane_out[...] = plane_strip[...] + delta[0, 0:24, :]
    copies = [
        pltpu.make_async_copy(strip_out, image.at[:, 24:32], sem.at[0]),
        pltpu.make_async_copy(plane_out, image.at[PLANES - 1, 0:24], sem.at[1]),
    ]
    for copy in copies:
        copy.start()
    for copy in copies:
        copy.wait()


def add_rims(rims, strips, image):
    return pl.pallas_call(
        rims_kernel,
        in_specs=[ANY] * 3 + [VMEM] * 3 + [ANY],
        out_specs=ANY,
        out_shape=pltpu.HBM((PLANES, PLANES, DEPTH), jnp.float32),
        input_output_aliases={6: 0},
        scratch_shapes=[
            pltpu.VMEM((2, 16, COARSE), jnp.float32),
            pltpu.VMEM((2, 16, COARSE), jnp.float32),
            pltpu.VMEM((2, 8, COARSE), jnp.float32),
            pltpu.VMEM((80, COARSE), jnp.float32),
            pltpu.VMEM((80, DEPTH), jnp.float32),
            pltpu.VMEM((4, 4 * PLANES, 128), jnp.float32),
            pltpu.VMEM((PLANES, 8, DEPTH), jnp.float32),
            pltpu.VMEM((24, DEPTH), jnp.float32),
            pltpu.VMEM((2, PLANES, DEPTH), jnp.float32),
            pltpu.SemaphoreType.DMA((5,)),
        ],
        compiler_params=ROOM,
        cost_estimate=pl.CostEstimate(flops=1 << 20, bytes_accessed=2 << 20, transcendentals=0),
        name="add_rims",
    )(*rims, *strips, in_hbm(image))


def per_device(
    stiffness,
    buoyancy,
    older_field,
    current_field,
    stored_tiles,
    tile_ids,
    tile_counts,
    receiver_cells,
    receiver_data,
    source_cell,
):
    older = older_field[0].reshape(ROWS, DEPTH)
    current = current_field[0].reshape(ROWS, DEPTH)
    stiff = stiffness.reshape(ROWS, DEPTH)
    buoy = buoyancy.reshape(ROWS, DEPTH)

    own = list(faces(current_field[0], buoyancy))
    far = exchange(own)
    tiles, own[0] = lax.optimization_barrier((stored_tiles, own[0]))
    received = lax.all_to_all(
        tiles[0, 0], ("shot", "gx"), split_axis=0, concat_axis=0, tiled=True
    ).reshape(1024, COARSE)
    numbers, counts, far[0], far[1] = lax.optimization_barrier((tile_ids, tile_counts, far[0], far[1]))
    slot = lax.broadcasted_iota(jnp.int32, (32, 32), 1)
    ids = jnp.where(slot < counts[0, 0][:, None], numbers[0, 0], -1).reshape(1, 1024)
    src = sources(receiver_cells[0], receiver_data[0])
    second, *rest = inner(current, older, buoy, stiff, src, [*own, *far], 0)
    own2, stiff_faces = rest[:4], rest[4:]
    far2 = exchange(own2)
    (third,) = inner(second, current, buoy, stiff, src, [], 1)

    received, third = lax.optimization_barrier((received, third))
    rim_x, rim_y, corner = rim_rows(received, ids)
    rims = [down(rim_x, "gx"), down(rim_y, "gy"), diagonal(corner)]
    edges = [*own, *far, *own2, *far2, *stiff_faces]
    image, last_current, *strips = picture(source_cell, received, ids, second, third, edges)
    image = add_rims(rims, strips, image)
    shape = current_field.shape
    return image.reshape(shape), second.reshape(shape), last_current.reshape(shape)


def exchange(own):
    return [
        swap(own[0], "gx", 0),
        swap(own[1], "gx", 1),
        swap(own[2], "gy", 0),
        swap(own[3], "gy", 1),
    ]


def down(block, axis):
    count = lax.axis_size(axis)
    return lax.ppermute(block, axis, [(i, (i - 1) % count) for i in range(count)])


def diagonal(block):
    nx, ny = lax.axis_size("gx"), lax.axis_size("gy")
    route = [
        (i * ny + j, ((i - 1) % nx) * ny + (j - 1) % ny) for i in range(nx) for j in range(ny)
    ]
    return lax.ppermute(block, ("gx", "gy"), route)


def solution(mesh):
    in_specs = (
        P("gx", "gy", None),
        P("gx", "gy", None),
        P("shot", "gx", "gy", None),
        P("shot", "gx", "gy", None),
        P(("shot", "gx"), "gy", None, None, None),
        P(("shot", "gx"), "gy", None, None),
        P(("shot", "gx"), "gy", None),
        P("shot", None, None),
        P("shot", None, None),
        P("shot", None),
    )
    out_specs = (
        P("shot", "gx", "gy", None),
        P("shot", "gx", "gy", None),
        P("shot", "gx", "gy", None),
    )
    return jax.shard_map(
        per_device, mesh=mesh, in_specs=in_specs, out_specs=out_specs, check_vma=False
    )
```
